512 devices in a mesh: dp: 64 (over x, y, z_lo), tensor: 8 (over z_hi, core).
Axes of the slice: x: 4, y: 8, z: 8 (z_hi: 4, z_lo: 2; z = z_hi * 2 + z_lo), core: 2. Of those that a mesh axis runs over, the one named last changes fastest.
Arguments:
- tokens: bfloat16 [8192, 2048], P('dp'), may hold values from -6 to 6
- cotangent: bfloat16 [8192, 2048], P('dp'), may hold values from -6 to 6
- expert_ids: int32 [8192, 4], P('dp'), may hold values from 0 to 63, all different within a row; in each aligned block of 128 rows (0 to 127, 128 to 255, ...) at most 10 rows name the same one
- route_weight: float32 [8192, 4], P('dp'), may hold values from 0.05 to 1
- forget_mask: int32 [8192], P('dp'), may hold values from 0 to 1, as said below
- lengths: int32 [2], replicated, may hold values from 1024 to 4096, as said below
- gate_weight: bfloat16 [64, 1024, 2048], P('dp', 'tensor'), may hold values from -0.125 to 0.125
- up_weight: bfloat16 [64, 1024, 2048], P('dp', 'tensor'), may hold values from -0.125 to 0.125
- down_weight: bfloat16 [64, 1024, 2048], P('dp', 'tensor'), may hold values from -0.1875 to 0.1875
Outputs:
- mixed_out: bfloat16 [8192, 2048], P('dp', 'tensor')
- grad_gate: bfloat16 [64, 1024, 2048], P('dp', 'tensor')
- grad_up: bfloat16 [64, 1024, 2048], P('dp', 'tensor')
- grad_down: bfloat16 [64, 1024, 2048], P('dp', 'tensor')
The draws below stay inside these ranges and needn't reach their ends.
Inputs may be any that keep to these rules, and one draw needn't show every extreme that they name: `expert_ids`: among the rows of one index of dp (aligned blocks of 128 tokens), no expert is named more than 10 times. `forget_mask`: the first token slot of every sequence is 0 and the second is 1. `lengths`: at least one sequence uses all 4096 slots.
All inputs are finite; a program needn't handle non-finite values.
Results may differ from the reference program's by a relative error of at most 0.019.
Values may be sent and summed in bfloat16 or wider, within the bound.
A program may use at most 128 MiB of HBM per device.

```python
import math
import jax
import jax.numpy as jnp
import numpy as np
from jax import lax

D = 2048
FFE = 1024
TOPK = 4
SEQS = 2
TOK_DEV = 128
EXPERTS = 64
SLICE = 128
CAP = 10
TOKENS = 8192
SEQ_LEN = 4096
N_DP = 64
N_TENSOR = 8


def draw_forget_mask(key, part):
    place = jnp.arange(TOKENS, dtype=jnp.int32)
    level = 150 + 450 * place // TOKENS
    rolled = jax.random.randint(key, (TOKENS,), 0, 1000)
    masked = (rolled < level).astype(jnp.int32)
    seq_pos = place % SEQ_LEN
    masked = jnp.where(seq_pos == 0, 0, jnp.where(seq_pos == 1, 1, masked))
    return masked.astype(jnp.int32)


def draw_lengths(key, part):
    first_key, second_key = jax.random.split(key)
    values = jax.random.randint(first_key, (SEQS,), SEQ_LEN // 4, SEQ_LEN + 1)
    chosen = jax.random.randint(second_key, (), 0, SEQS)
    return jnp.where(jnp.arange(SEQS) == chosen, SEQ_LEN, values).astype(jnp.int32)


def shard_levels(stream_key, dims, cuts, low, high):
    def one(position, parts):
        steps = jax.random.uniform(jax.random.fold_in(jax.random.fold_in(stream_key, 6), position), (parts,), jnp.float32, low / len(cuts), high / len(cuts))
        return jnp.repeat(jnp.exp(steps), dims[position] // parts).reshape((-1,) + (1,) * (len(dims) - position - 1))

    gain = one(*cuts[0])
    for cut in cuts[1:]:
        gain = gain * one(*cut)
    return gain


def routed_block(own_key, own, number, rows, number_of, top, reach, lean):
    order = jax.random.permutation(own_key, number_of)
    packed, usual = load_shares(number_of, rows * top, reach, lean, True), load_shares(number_of, rows * top, reach, lean, False)
    places = jnp.arange(number_of)

    def named(tallies, offset_by):
        used = int((tallies > 0).sum())
        fixed = max(1, used // 4)
        passed = fixed + (places - fixed + offset_by * (used - fixed)) % max(1, number_of - fixed)
        return jnp.zeros((number_of,), jnp.int32).at[order[jnp.where(places < fixed, places, passed)]].set(jnp.asarray(tallies, jnp.int32))

    tallies = jnp.where(number % 4 == 0, named(packed, number // 4), named(usual, number - number // 4 - 1))
    mixed = jax.random.permutation(jax.random.fold_in(own, 3), number_of)
    source_of, sink = mixed[0:number_of // 2 * 2:2], mixed[1:number_of // 2 * 2:2]
    margin = jnp.minimum(tallies[source_of] - 1, reach - tallies[sink]) // 2
    margin = jnp.where((source_of == order[0]) | (sink == order[0]) | (tallies[sink] == 0), 0, jnp.maximum(margin, 0))
    passed = jax.random.randint(jax.random.fold_in(own, 4), (number_of // 2,), 0, 1 << 20) % (margin + 1)
    tallies = tallies.at[source_of].add(-passed).at[sink].add(passed)
    items = jnp.searchsorted(jnp.cumsum(tallies), jnp.arange(rows * top), side="right").astype(jnp.int32)
    table = items.reshape(top, rows).T
    table = table[jax.random.permutation(jax.random.fold_in(own, 1), rows)]
    offset_by = jax.random.randint(jax.random.fold_in(own, 2), (rows, 1), 0, top)
    return jnp.take_along_axis(table, (jnp.arange(top)[None, :] + offset_by) % top, axis=1)


def load_shares(count, total, bound, slope, full):
    loads = [(1 << 20) // math.isqrt(grade ** slope) + 1 for grade in range(1, count + 1)]
    largest = bound if full else min(bound, max(-(-total // count), total * loads[0] // sum(loads)))
    least = 1 if total - largest >= count - 1 else 0
    given, rest = [largest] + [least] * (count - 1), total - largest - least * (count - 1)
    while rest > 0:
        candidates = [i for i in range(1, count) if given[i] < largest] or [i for i in range(1, count) if given[i] < bound]
        whole, left = sum([loads[i] for i in candidates]), rest
        for i in candidates:
            extra = min(bound - given[i], max(1, left * loads[i] // whole), rest)
            given[i] = given[i] + extra
            rest = rest - extra
    return np.array(given)


def centred(stream_key, shape, deviation, bound, cuts=(), kind=jnp.bfloat16):
    values = deviation * jax.random.normal(stream_key, shape, jnp.float32)
    if cuts:
        values = values * shard_levels(stream_key, shape, cuts, -0.22, 0.18)
    return jnp.clip(values, -bound, bound).astype(kind)


def setup_inputs(seed: int = 0) -> dict:
    splits = jax.random.split(jax.random.key(seed), 10)
    tokens = centred(splits[0], (TOKENS, D), 1.0, 6.0, ((0, 64),))
    cotangent = centred(splits[1], (TOKENS, D), 1.0, 6.0, ((0, 64),))
    expert_ids_keys = jax.random.split(jax.random.fold_in(splits[2], 1), TOKENS // TOK_DEV)
    expert_ids_turns = jax.random.permutation(jax.random.fold_in(splits[2], 3), TOKENS // TOK_DEV)
    expert_ids = jax.vmap(lambda own, number: routed_block(jax.random.fold_in(splits[2], 2), own, number, TOK_DEV, EXPERTS, TOPK, CAP, 2))(expert_ids_keys, expert_ids_turns).reshape((TOKENS, TOPK))
    route_weight = jnp.clip(jnp.exp(math.log(1.0) - 2.9957323 * jax.random.uniform(splits[3], (TOKENS, TOPK), jnp.float32) ** shard_levels(splits[3], (TOKENS, TOPK), ((0, 64),), -0.2, 0.2)), 0.05, 1.0)
    forget_mask = draw_forget_mask(jax.random.fold_in(splits[9], 71), 0)
    lengths = draw_lengths(jax.random.fold_in(splits[9], 71), 0)
    gate_weight = centred(splits[6], (EXPERTS, FFE, D), D ** -0.5, 0.125, ((0, 64), (1, 8)))
    up_weight = centred(splits[7], (EXPERTS, FFE, D), D ** -0.5, 0.125, ((0, 64), (1, 8)))
    down_weight = centred(splits[8], (EXPERTS, FFE, D), FFE ** -0.5, 0.1875, ((0, 64), (1, 8)))
    return dict(tokens=tokens, cotangent=cotangent, expert_ids=expert_ids, route_weight=route_weight, forget_mask=forget_mask, lengths=lengths, gate_weight=gate_weight, up_weight=up_weight, down_weight=down_weight)


def reference(tokens, cotangent, expert_ids, route_weight, forget_mask, lengths, gate_weight, up_weight, down_weight):
    total_rows = tokens.shape[0]
    token_index = jnp.arange(total_rows, dtype=jnp.int32)
    seq_id = token_index // SEQ_LEN
    seq_pos = token_index - seq_id * SEQ_LEN
    is_valid = (seq_pos < lengths[seq_id]).astype(jnp.int32)
    forget = is_valid * forget_mask
    retain = is_valid - forget
    n_forget = jnp.sum(forget).astype(jnp.float32)
    n_retain = jnp.sum(retain).astype(jnp.float32)
    coefficient = float(TOPK * TOK_DEV) * (retain.astype(jnp.float32) / n_retain - forget.astype(jnp.float32) / n_forget)
    shares = route_weight / jnp.sum(route_weight, axis=1, keepdims=True)
    share_flat = shares.reshape(-1)
    flat_ids = expert_ids.reshape(-1)
    sorted_ids = jnp.argsort(flat_ids, stable=True).astype(jnp.int32)
    counts = jnp.sum((flat_ids[:, None] == jnp.arange(EXPERTS, dtype=jnp.int32)[None, :]).astype(jnp.int32), axis=0)
    starts = (jnp.cumsum(counts) - counts).astype(jnp.int32)
    row_count = N_DP * CAP
    padded_ids = jnp.concatenate([sorted_ids, jnp.zeros((row_count,), jnp.int32)])

    def expert_step(mixed_sum, expert):
        slot_ids = lax.dynamic_slice_in_dim(padded_ids, starts[expert], row_count)
        is_live = jnp.arange(row_count, dtype=jnp.int32) < counts[expert]
        tok_ids = slot_ids // TOPK
        rows_in = jnp.where(is_live[:, None], tokens[tok_ids], jnp.zeros((), tokens.dtype))
        weight = jnp.where(is_live, share_flat[slot_ids], jnp.zeros((), share_flat.dtype))
        routed = ((coefficient[tok_ids] * weight)[:, None] * cotangent[tok_ids].astype(jnp.float32)).astype(jnp.bfloat16)
        gate_pre = jnp.dot(rows_in, gate_weight[expert].T, preferred_element_type=jnp.float32)
        up_pre = jnp.dot(rows_in, up_weight[expert].T, preferred_element_type=jnp.float32)
        sigmoid_gate = jax.nn.sigmoid(gate_pre)
        hidden = (gate_pre * sigmoid_gate * up_pre).astype(jnp.bfloat16)
        pieces = jnp.einsum("rns,nsd->rnd", hidden.reshape(row_count, N_TENSOR, SLICE).astype(jnp.float32),
                            down_weight[expert].reshape(N_TENSOR, SLICE, -1).astype(jnp.float32))
        rounded = lax.optimization_barrier(pieces.astype(jnp.bfloat16))
        expert_out = jnp.sum(rounded.astype(jnp.float32), axis=1)
        mixed_sum = mixed_sum.at[tok_ids].add(weight[:, None] * expert_out)
        grad_down = jnp.dot(hidden.T, routed, preferred_element_type=jnp.float32)
        dhidden = jnp.dot(routed, down_weight[expert].T, preferred_element_type=jnp.float32)
        dgate = (dhidden * up_pre * sigmoid_gate * (1.0 + gate_pre * (1.0 - sigmoid_gate))).astype(jnp.bfloat16)
        dup = (dhidden * gate_pre * sigmoid_gate).astype(jnp.bfloat16)
        grad_gate = jnp.dot(dgate.T, rows_in, preferred_element_type=jnp.float32)
        grad_up = jnp.dot(dup.T, rows_in, preferred_element_type=jnp.float32)
        return mixed_sum, (grad_gate.astype(jnp.bfloat16), grad_up.astype(jnp.bfloat16), grad_down.astype(jnp.bfloat16))

    mixed_sum, grad_all = lax.scan(expert_step, jnp.zeros((total_rows, D), jnp.float32), jnp.arange(EXPERTS, dtype=jnp.int32))
    return (mixed_sum.astype(jnp.bfloat16), grad_all[0], grad_all[1], grad_all[2])
```

```python
import jax
import jax.numpy as jnp
import numpy as np
from jax import lax
from jax.sharding import Mesh
from jax.sharding import PartitionSpec as P


def _swap_pair(x):
    return lax.ppermute(x, "core", [(0, 1), (1, 0)])


def body(
    tokens,
    cotangent,
    expert_ids,
    route_weight,
    forget_mask,
    lengths,
    gate_weight,
    up_weight,
    down_weight,
):
    tok_rows = tokens.shape[0]
    features = tokens.shape[1]
    half = features // 2
    top_count = expert_ids.shape[1]
    owners = lax.axis_size("dp")
    groups = lax.axis_size("zh")
    block = features // (2 * groups)
    capacity = 5 * tok_rows * top_count // (4 * owners)
    core = lax.axis_index("core")
    is_first = core == 0

    seq_count = lengths.shape[0]
    seq_len = tok_rows * owners // seq_count
    token_index = lax.axis_index("dp") * tok_rows + jnp.arange(tok_rows, dtype=jnp.int32)
    seq_id = token_index // seq_len
    seq_pos = token_index - seq_id * seq_len
    in_seq = seq_id[:, None] == jnp.arange(seq_count, dtype=jnp.int32)[None, :]
    limits = jnp.sum(jnp.where(in_seq, lengths[None, :], 0), axis=1)
    is_valid = (seq_pos < limits).astype(jnp.int32)
    forget = is_valid * forget_mask
    retain = is_valid - forget

    shares = route_weight / jnp.sum(route_weight, axis=1, keepdims=True)
    share_flat = shares.reshape(-1)
    assigned = tok_rows * top_count
    flat_ids = expert_ids.reshape(-1)
    one_hot = (flat_ids[:, None] == jnp.arange(owners, dtype=jnp.int32)[None, :]).astype(jnp.int32)
    before = jnp.cumsum(one_hot, axis=0) - one_hot
    slot_id = jnp.sum(before * one_hot, axis=1)
    target = flat_ids * capacity + slot_id
    slots_all = owners * capacity
    source = (
        jnp.full((slots_all,), assigned, jnp.int32)
        .at[target]
        .set(jnp.arange(assigned, dtype=jnp.int32))
    )
    is_live = source < assigned
    source_row = jnp.minimum(source, assigned - 1)
    source_tok = source_row // top_count

    my_tokens = lax.dynamic_slice_in_dim(tokens, core * half, half, axis=1)
    send_rows = jnp.where(
        is_live[:, None], my_tokens[source_tok], jnp.zeros((), tokens.dtype)
    ).reshape(owners, capacity, half)
    recv_rows = lax.all_to_all(send_rows, "dp", split_axis=0, concat_axis=0, tiled=True)
    recv_rows = recv_rows.reshape(slots_all, half)
    other_rows = _swap_pair(recv_rows)
    rows_in = jnp.concatenate(
        [jnp.where(is_first, recv_rows, other_rows), jnp.where(is_first, other_rows, recv_rows)],
        axis=1,
    )

    n_forget, n_retain = lax.psum((jnp.sum(forget), jnp.sum(retain)), "dp")
    coefficient = float(top_count * tok_rows) * (
        retain.astype(jnp.float32) / n_retain.astype(jnp.float32)
        - forget.astype(jnp.float32) / n_forget.astype(jnp.float32)
    )
    slot_weight = jnp.where(is_live, coefficient[source_tok] * share_flat[source_row], 0.0)
    my_cotan = lax.dynamic_slice_in_dim(cotangent, core * half, half, axis=1)
    send_cotan = (
        (slot_weight[:, None] * my_cotan[source_tok].astype(jnp.float32))
        .astype(jnp.bfloat16)
        .reshape(owners, capacity, half)
    )
    recv_cotan = lax.all_to_all(send_cotan, "dp", split_axis=0, concat_axis=0, tiled=True)
    recv_cotan = recv_cotan.reshape(slots_all, half)
    other_cotan = _swap_pair(recv_cotan)
    routed = jnp.concatenate(
        [jnp.where(is_first, recv_cotan, other_cotan), jnp.where(is_first, other_cotan, recv_cotan)],
        axis=1,
    )

    contract_last = (((1,), (1,)), ((), ()))
    contract_first = (((0,), (0,)), ((), ()))
    gate_pre = lax.dot_general(
        gate_weight[0], rows_in, contract_last, preferred_element_type=jnp.float32
    )
    up_pre = lax.dot_general(
        up_weight[0], rows_in, contract_last, preferred_element_type=jnp.float32
    )
    sigmoid_gate = jax.nn.sigmoid(gate_pre)
    hidden = (gate_pre * sigmoid_gate * up_pre).astype(jnp.bfloat16)
    partial_out = lax.dot_general(
        hidden, down_weight[0], contract_first, preferred_element_type=jnp.float32
    ).astype(jnp.bfloat16)
    pieces = partial_out.reshape(slots_all, groups, 2, block)
    keep = jnp.where(is_first, pieces[:, :, 0, :], pieces[:, :, 1, :])
    give = jnp.where(is_first, pieces[:, :, 1, :], pieces[:, :, 0, :])
    pair_sum = (keep.astype(jnp.float32) + _swap_pair(give).astype(jnp.float32)).astype(jnp.bfloat16)
    returned = lax.all_to_all(
        pair_sum.reshape(owners, capacity, groups * block),
        "dp",
        split_axis=0,
        concat_axis=0,
        tiled=True,
    )
    picked = returned.reshape(slots_all, groups * block)[target].astype(jnp.float32) * share_flat[:, None]
    token_terms = jnp.sum(picked.reshape(tok_rows, top_count, groups, block), axis=1)
    mixed_out = lax.psum_scatter(token_terms, "zh", scatter_dimension=1, tiled=True)
    mixed_out = mixed_out.reshape(tok_rows, block).astype(jnp.bfloat16)

    grad_down = jnp.dot(hidden, routed, preferred_element_type=jnp.float32)
    dhidden = lax.dot_general(
        down_weight[0], routed, contract_last, preferred_element_type=jnp.float32
    )
    dgate = (dhidden * up_pre * sigmoid_gate * (1.0 + gate_pre * (1.0 - sigmoid_gate))).astype(
        jnp.bfloat16
    )
    dup = (dhidden * gate_pre * sigmoid_gate).astype(jnp.bfloat16)
    grad_gate = jnp.dot(dgate, rows_in, preferred_element_type=jnp.float32)
    grad_up = jnp.dot(dup, rows_in, preferred_element_type=jnp.float32)
    return (
        mixed_out,
        grad_gate.astype(jnp.bfloat16)[None],
        grad_up.astype(jnp.bfloat16)[None],
        grad_down.astype(jnp.bfloat16)[None],
    )


def solution(mesh):
    n_dp = mesh.shape["dp"]
    n_tensor = mesh.shape["tensor"]
    fine = Mesh(
        np.asarray(mesh.devices).reshape(n_dp, n_tensor // 2, 2), ("dp", "zh", "core")
    )
    tp = ("zh", "core")
    in_specs = (
        P("dp", None),
        P("dp", None),
        P("dp", None),
        P("dp", None),
        P("dp"),
        P(),
        P("dp", tp, None),
        P("dp", tp, None),
        P("dp", tp, None),
    )
    out_specs = (
        P("dp", tp),
        P("dp", tp, None),
        P("dp", tp, None),
        P("dp", tp, None),
    )
    return jax.shard_map(body, mesh=fine, in_specs=in_specs, out_specs=out_specs, check_vma=False)
```

```python
import jax
import jax.numpy as jnp
import numpy as np
from jax import lax
from jax.sharding import Mesh
from jax.sharding import PartitionSpec as P


def _swap_pair(x):
    return lax.ppermute(x, "core", [(0, 1), (1, 0)])


def body(
    tokens,
    cotangent,
    expert_ids,
    route_weight,
    forget_mask,
    lengths,
    gate_weight,
    up_weight,
    down_weight,
):
    tok_rows = tokens.shape[0]
    features = tokens.shape[1]
    half = features // 2
    top_count = expert_ids.shape[1]
    owners = lax.axis_size("dp")
    groups = lax.axis_size("zh")
    block = features // (2 * groups)
    capacity = 5 * tok_rows * top_count // (4 * owners)
    core = lax.axis_index("core")
    is_first = core == 0

    seq_count = lengths.shape[0]
    seq_len = tok_rows * owners // seq_count
    token_index = lax.axis_index("dp") * tok_rows + jnp.arange(tok_rows, dtype=jnp.int32)
    seq_id = token_index // seq_len
    seq_pos = token_index - seq_id * seq_len
    in_seq = seq_id[:, None] == jnp.arange(seq_count, dtype=jnp.int32)[None, :]
    limits = jnp.sum(jnp.where(in_seq, lengths[None, :], 0), axis=1)
    is_valid = (seq_pos < limits).astype(jnp.int32)
    forget = is_valid * forget_mask
    retain = is_valid - forget

    shares = route_weight / jnp.sum(route_weight, axis=1, keepdims=True)
    share_flat = shares.reshape(-1)
    assigned = tok_rows * top_count
    flat_ids = expert_ids.reshape(-1)
    one_hot = (flat_ids[:, None] == jnp.arange(owners, dtype=jnp.int32)[None, :]).astype(jnp.int32)
    before = jnp.cumsum(one_hot, axis=0) - one_hot
    slot_id = jnp.sum(before * one_hot, axis=1)
    target = flat_ids * capacity + slot_id
    slots_all = owners * capacity
    source = (
        jnp.full((slots_all,), assigned, jnp.int32)
        .at[target]
        .set(jnp.arange(assigned, dtype=jnp.int32))
    )
    is_live = source < assigned
    source_row = jnp.minimum(source, assigned - 1)
    source_tok = source_row // top_count

    live_f = is_live.astype(jnp.float32)
    slot_share = jnp.where(is_live, share_flat[source_row], 0.0)
    share_hi = lax.reduce_precision(slot_share, exponent_bits=8, mantissa_bits=7)
    rest = slot_share - share_hi
    share_mid = lax.reduce_precision(rest, exponent_bits=8, mantissa_bits=7)
    share_lo = rest - share_mid
    slot_forget = live_f * forget[source_tok].astype(jnp.float32)
    slot_retain = live_f * retain[source_tok].astype(jnp.float32)
    per_slot = jnp.stack([share_hi, share_mid, share_lo, slot_forget, slot_retain], axis=1)
    per_slot = per_slot.reshape(owners, capacity * 5)
    local_counts = jnp.stack([jnp.sum(forget), jnp.sum(retain)]).astype(jnp.float32)
    meta = jnp.concatenate(
        [
            per_slot,
            jnp.broadcast_to(local_counts[None, :], (owners, 2)),
            jnp.zeros((owners, features - capacity * 5 - 2), jnp.float32),
        ],
        axis=1,
    ).astype(jnp.bfloat16)
    my_tokens = lax.dynamic_slice_in_dim(tokens, core * half, half, axis=1)
    my_cotan = lax.dynamic_slice_in_dim(cotangent, core * half, half, axis=1)
    both = jnp.concatenate([my_tokens, my_cotan], axis=1)
    send = jnp.where(is_live[:, None], both[source_tok], jnp.zeros((), tokens.dtype))
    send = jnp.concatenate([send.reshape(owners, capacity, features), meta[:, None, :]], axis=1)
    recv = lax.all_to_all(send, "dp", split_axis=0, concat_axis=0, tiled=True)
    got = recv[:, :capacity, :].reshape(slots_all, features)
    got_meta = recv[:, capacity, :].astype(jnp.float32)
    other = _swap_pair(got)
    lower = jnp.where(is_first, got, other)
    upper = jnp.where(is_first, other, got)
    rows_in = jnp.concatenate([lower[:, :half], upper[:, :half]], axis=1)
    cot_in = jnp.concatenate([lower[:, half:], upper[:, half:]], axis=1)

    n_forget = jnp.sum(got_meta[:, capacity * 5])
    n_retain = jnp.sum(got_meta[:, capacity * 5 + 1])
    slot_meta = got_meta[:, : capacity * 5].reshape(slots_all, 5)
    got_share = (slot_meta[:, 0] + slot_meta[:, 1]) + slot_meta[:, 2]
    coefficient = float(top_count * tok_rows) * (
        slot_meta[:, 4] / n_retain - slot_meta[:, 3] / n_forget
    )
    routed = ((coefficient * got_share)[:, None] * cot_in.astype(jnp.float32)).astype(jnp.bfloat16)

    contract_last = (((1,), (1,)), ((), ()))
    contract_first = (((0,), (0,)), ((), ()))
    gate_pre = lax.dot_general(
        gate_weight[0], rows_in, contract_last, preferred_element_type=jnp.float32
    )
    up_pre = lax.dot_general(
        up_weight[0], rows_in, contract_last, preferred_element_type=jnp.float32
    )
    sigmoid_gate = jax.nn.sigmoid(gate_pre)
    hidden = (gate_pre * sigmoid_gate * up_pre).astype(jnp.bfloat16)
    partial_out = lax.dot_general(
        hidden, down_weight[0], contract_first, preferred_element_type=jnp.float32
    ).astype(jnp.bfloat16)
    pieces = partial_out.reshape(slots_all, groups, 2, block)
    keep = jnp.where(is_first, pieces[:, :, 0, :], pieces[:, :, 1, :])
    give = jnp.where(is_first, pieces[:, :, 1, :], pieces[:, :, 0, :])
    pair_sum = (keep.astype(jnp.float32) + _swap_pair(give).astype(jnp.float32)).astype(jnp.bfloat16)
    returned = lax.all_to_all(
        pair_sum.reshape(owners, capacity, groups * block),
        "dp",
        split_axis=0,
        concat_axis=0,
        tiled=True,
    )
    picked = returned.reshape(slots_all, groups * block)[target].astype(jnp.float32) * share_flat[:, None]
    token_terms = jnp.sum(picked.reshape(tok_rows, top_count, groups, block), axis=1)
    spread = lax.all_to_all(
        jnp.transpose(token_terms, (1, 0, 2)), "zh", split_axis=0, concat_axis=0, tiled=True
    )
    mixed_out = jnp.sum(spread, axis=0).astype(jnp.bfloat16)

    grad_down = jnp.dot(hidden, routed, preferred_element_type=jnp.float32)
    dhidden = lax.dot_general(
        down_weight[0], routed, contract_last, preferred_element_type=jnp.float32
    )
    dgate = (dhidden * up_pre * sigmoid_gate * (1.0 + gate_pre * (1.0 - sigmoid_gate))).astype(
        jnp.bfloat16
    )
    dup = (dhidden * gate_pre * sigmoid_gate).astype(jnp.bfloat16)
    grad_gate = jnp.dot(dgate, rows_in, preferred_element_type=jnp.float32)
    grad_up = jnp.dot(dup, rows_in, preferred_element_type=jnp.float32)
    return (
        mixed_out,
        grad_gate.astype(jnp.bfloat16)[None],
        grad_up.astype(jnp.bfloat16)[None],
        grad_down.astype(jnp.bfloat16)[None],
    )


def solution(mesh):
    n_dp = mesh.shape["dp"]
    n_tensor = mesh.shape["tensor"]
    fine = Mesh(
        np.asarray(mesh.devices).reshape(n_dp, n_tensor // 2, 2), ("dp", "zh", "core")
    )
    tp = ("zh", "core")
    in_specs = (
        P("dp", None),
        P("dp", None),
        P("dp", None),
        P("dp", None),
        P("dp"),
        P(),
        P("dp", tp, None),
        P("dp", tp, None),
        P("dp", tp, None),
    )
    out_specs = (
        P("dp", tp),
        P("dp", tp, None),
        P("dp", tp, None),
        P("dp", tp, None),
    )
    return jax.shard_map(body, mesh=fine, in_specs=in_specs, out_specs=out_specs, check_vma=False)
```

```python
import functools

import jax
import jax.numpy as jnp
import numpy as np
from jax import lax
from jax.experimental import pallas as pl
from jax.experimental.pallas import tpu as pltpu
from jax.sharding import Mesh
from jax.sharding import PartitionSpec as P


MESH = pl.DeviceIdType.MESH


def _exchange_kernel(n, x_ref, y_ref, send_sem, recv_sem, own_sem):
    me = lax.axis_index("dp")

    def copy_to(peer):
        return pltpu.make_async_remote_copy(
            src_ref=x_ref.at[peer],
            dst_ref=y_ref.at[me],
            send_sem=send_sem.at[peer],
            recv_sem=recv_sem.at[me],
            device_id={"dp": peer},
            device_id_type=MESH,
        )

    def copy_from(source):
        return pltpu.make_async_remote_copy(
            src_ref=x_ref.at[source],
            dst_ref=y_ref.at[source],
            send_sem=send_sem.at[source],
            recv_sem=recv_sem.at[source],
            device_id={"dp": source},
            device_id_type=MESH,
        )

    barrier = pltpu.get_barrier_semaphore()

    def greet(i, carry):
        pl.semaphore_signal(barrier, inc=1, device_id={"dp": lax.rem(me + i, n)}, device_id_type=MESH)
        return carry

    lax.fori_loop(1, n, greet, 0)
    pl.semaphore_wait(barrier, n - 1)
    own = pltpu.make_async_copy(x_ref.at[me], y_ref.at[me], own_sem)
    own.start()

    def send(i, carry):
        copy_to(lax.rem(me + i, n)).start()
        return carry

    lax.fori_loop(1, n, send, 0)

    def finish(i, carry):
        copy_to(lax.rem(me + i, n)).wait_send()
        copy_from(lax.rem(me + n - i, n)).wait_recv()
        return carry

    lax.fori_loop(1, n, finish, 0)
    own.wait()


def _exchange(x, collective_id):
    n = x.shape[0]
    return pl.pallas_call(
        functools.partial(_exchange_kernel, n),
        out_shape=jax.ShapeDtypeStruct(x.shape, x.dtype),
        in_specs=[pl.BlockSpec(memory_space=pl.ANY)],
        out_specs=pl.BlockSpec(memory_space=pl.ANY),
        scratch_shapes=[
            pltpu.SemaphoreType.DMA((n,)),
            pltpu.SemaphoreType.DMA((n,)),
            pltpu.SemaphoreType.DMA(()),
        ],
        compiler_params=pltpu.CompilerParams(collective_id=collective_id, has_side_effects=True),
    )(x)


def _swap_pair(x):
    return lax.ppermute(x, "core", [(0, 1), (1, 0)])


def body(
    tokens,
    cotangent,
    expert_ids,
    route_weight,
    forget_mask,
    lengths,
    gate_weight,
    up_weight,
    down_weight,
):
    tok_rows = tokens.shape[0]
    features = tokens.shape[1]
    half = features // 2
    top_count = expert_ids.shape[1]
    owners = lax.axis_size("dp")
    groups = lax.axis_size("zh")
    block = features // (2 * groups)
    capacity = 5 * tok_rows * top_count // (4 * owners)
    core = lax.axis_index("core")
    is_first = core == 0

    seq_count = lengths.shape[0]
    seq_len = tok_rows * owners // seq_count
    token_index = lax.axis_index("dp") * tok_rows + jnp.arange(tok_rows, dtype=jnp.int32)
    seq_id = token_index // seq_len
    seq_pos = token_index - seq_id * seq_len
    in_seq = seq_id[:, None] == jnp.arange(seq_count, dtype=jnp.int32)[None, :]
    limits = jnp.sum(jnp.where(in_seq, lengths[None, :], 0), axis=1)
    is_valid = (seq_pos < limits).astype(jnp.int32)
    forget = is_valid * forget_mask
    retain = is_valid - forget

    shares = route_weight / jnp.sum(route_weight, axis=1, keepdims=True)
    share_flat = shares.reshape(-1)
    assigned = tok_rows * top_count
    flat_ids = expert_ids.reshape(-1)
    one_hot = (flat_ids[:, None] == jnp.arange(owners, dtype=jnp.int32)[None, :]).astype(jnp.int32)
    before = jnp.cumsum(one_hot, axis=0) - one_hot
    slot_id = jnp.sum(before * one_hot, axis=1)
    target = flat_ids * capacity + slot_id
    slots_all = owners * capacity
    source = (
        jnp.full((slots_all,), assigned, jnp.int32)
        .at[target]
        .set(jnp.arange(assigned, dtype=jnp.int32))
    )
    is_live = source < assigned
    source_row = jnp.minimum(source, assigned - 1)
    source_tok = source_row // top_count

    live_f = is_live.astype(jnp.float32)
    slot_share = jnp.where(is_live, share_flat[source_row], 0.0)
    share_hi = lax.reduce_precision(slot_share, exponent_bits=8, mantissa_bits=7)
    rest = slot_share - share_hi
    share_mid = lax.reduce_precision(rest, exponent_bits=8, mantissa_bits=7)
    share_lo = rest - share_mid
    slot_forget = live_f * forget[source_tok].astype(jnp.float32)
    slot_retain = live_f * retain[source_tok].astype(jnp.float32)
    per_slot = jnp.stack([share_hi, share_mid, share_lo, slot_forget, slot_retain], axis=1)
    per_slot = per_slot.reshape(owners, capacity * 5)
    local_counts = jnp.stack([jnp.sum(forget), jnp.sum(retain)]).astype(jnp.float32)
    meta = jnp.concatenate(
        [
            per_slot,
            jnp.broadcast_to(local_counts[None, :], (owners, 2)),
            jnp.zeros((owners, features - capacity * 5 - 2), jnp.float32),
        ],
        axis=1,
    ).astype(jnp.bfloat16)
    my_tokens = lax.dynamic_slice_in_dim(tokens, core * half, half, axis=1)
    my_cotan = lax.dynamic_slice_in_dim(cotangent, core * half, half, axis=1)
    both = jnp.concatenate([my_tokens, my_cotan], axis=1)
    send = jnp.where(is_live[:, None], both[source_tok], jnp.zeros((), tokens.dtype))
    lanes = 128
    send = jnp.concatenate(
        [send.reshape(owners, capacity * features // lanes, lanes), meta.reshape(owners, features // lanes, lanes)],
        axis=1,
    )
    recv = _exchange(send, 0)
    got = recv[:, : capacity * features // lanes, :].reshape(slots_all, features)
    got_meta = recv[:, capacity * features // lanes :, :].reshape(owners, features).astype(jnp.float32)
    other = _swap_pair(got)
    lower = jnp.where(is_first, got, other)
    upper = jnp.where(is_first, other, got)
    rows_in = jnp.concatenate([lower[:, :half], upper[:, :half]], axis=1)
    cot_in = jnp.concatenate([lower[:, half:], upper[:, half:]], axis=1)

    n_forget = jnp.sum(got_meta[:, capacity * 5])
    n_retain = jnp.sum(got_meta[:, capacity * 5 + 1])
    slot_meta = got_meta[:, : capacity * 5].reshape(slots_all, 5)
    got_share = (slot_meta[:, 0] + slot_meta[:, 1]) + slot_meta[:, 2]
    coefficient = float(top_count * tok_rows) * (
        slot_meta[:, 4] / n_retain - slot_meta[:, 3] / n_forget
    )
    routed = ((coefficient * got_share)[:, None] * cot_in.astype(jnp.float32)).astype(jnp.bfloat16)

    contract_last = (((1,), (1,)), ((), ()))
    contract_first = (((0,), (0,)), ((), ()))
    gate_pre = lax.dot_general(
        gate_weight[0], rows_in, contract_last, preferred_element_type=jnp.float32
    )
    up_pre = lax.dot_general(
        up_weight[0], rows_in, contract_last, preferred_element_type=jnp.float32
    )
    sigmoid_gate = jax.nn.sigmoid(gate_pre)
    hidden = (gate_pre * sigmoid_gate * up_pre).astype(jnp.bfloat16)
    partial_out = lax.dot_general(
        hidden, down_weight[0], contract_first, preferred_element_type=jnp.float32
    ).astype(jnp.bfloat16)
    pieces = partial_out.reshape(slots_all, groups, 2, block)
    keep = jnp.where(is_first, pieces[:, :, 0, :], pieces[:, :, 1, :])
    give = jnp.where(is_first, pieces[:, :, 1, :], pieces[:, :, 0, :])
    pair_sum = (keep.astype(jnp.float32) + _swap_pair(give).astype(jnp.float32)).astype(jnp.bfloat16)
    returned = _exchange(pair_sum.reshape(owners, capacity * groups * block // lanes, lanes), 1)
    picked = returned.reshape(slots_all, groups * block)[target].astype(jnp.float32) * share_flat[:, None]
    token_terms = jnp.sum(picked.reshape(tok_rows, top_count, groups, block), axis=1)
    spread = lax.all_to_all(
        jnp.transpose(token_terms, (1, 0, 2)), "zh", split_axis=0, concat_axis=0, tiled=True
    )
    mixed_out = jnp.sum(spread, axis=0).astype(jnp.bfloat16)

    grad_down = jnp.dot(hidden, routed, preferred_element_type=jnp.float32)
    dhidden = lax.dot_general(
        down_weight[0], routed, contract_last, preferred_element_type=jnp.float32
    )
    dgate = (dhidden * up_pre * sigmoid_gate * (1.0 + gate_pre * (1.0 - sigmoid_gate))).astype(
        jnp.bfloat16
    )
    dup = (dhidden * gate_pre * sigmoid_gate).astype(jnp.bfloat16)
    grad_gate = jnp.dot(dgate, rows_in, preferred_element_type=jnp.float32)
    grad_up = jnp.dot(dup, rows_in, preferred_element_type=jnp.float32)
    return (
        mixed_out,
        grad_gate.astype(jnp.bfloat16)[None],
        grad_up.astype(jnp.bfloat16)[None],
        grad_down.astype(jnp.bfloat16)[None],
    )


def solution(mesh):
    n_dp = mesh.shape["dp"]
    n_tensor = mesh.shape["tensor"]
    fine = Mesh(
        np.asarray(mesh.devices).reshape(n_dp, n_tensor // 2, 2), ("dp", "zh", "core")
    )
    tp = ("zh", "core")
    in_specs = (
        P("dp", None),
        P("dp", None),
        P("dp", None),
        P("dp", None),
        P("dp"),
        P(),
        P("dp", tp, None),
        P("dp", tp, None),
        P("dp", tp, None),
    )
    out_specs = (
        P("dp", tp),
        P("dp", tp, None),
        P("dp", tp, None),
        P("dp", tp, None),
    )
    return jax.shard_map(body, mesh=fine, in_specs=in_specs, out_specs=out_specs, check_vma=False)
```

```python
import functools

import jax
import jax.numpy as jnp
import numpy as np
from jax import lax
from jax.experimental import pallas as pl
from jax.experimental.pallas import tpu as pltpu
from jax.sharding import Mesh
from jax.sharding import PartitionSpec as P


MESH = pl.DeviceIdType.MESH


def _exchange_kernel(n, x_ref, y_ref, send_sem, recv_sem, own_sem):
    me = lax.axis_index("dp")

    def copy_to(peer):
        return pltpu.make_async_remote_copy(
            src_ref=x_ref.at[peer],
            dst_ref=y_ref.at[me],
            send_sem=send_sem.at[peer],
            recv_sem=recv_sem.at[me],
            device_id={"dp": peer},
            device_id_type=MESH,
        )

    def copy_from(source):
        return pltpu.make_async_remote_copy(
            src_ref=x_ref.at[source],
            dst_ref=y_ref.at[source],
            send_sem=send_sem.at[source],
            recv_sem=recv_sem.at[source],
            device_id={"dp": source},
            device_id_type=MESH,
        )

    barrier = pltpu.get_barrier_semaphore()

    def greet(i, carry):
        pl.semaphore_signal(barrier, inc=1, device_id={"dp": lax.rem(me + i, n)}, device_id_type=MESH)
        return carry

    lax.fori_loop(1, n, greet, 0)
    pl.semaphore_wait(barrier, n - 1)
    own = pltpu.make_async_copy(x_ref.at[me], y_ref.at[me], own_sem)
    own.start()

    def send(i, carry):
        copy_to(lax.rem(me + i, n)).start()
        return carry

    lax.fori_loop(1, n, send, 0)

    def finish(i, carry):
        copy_to(lax.rem(me + i, n)).wait_send()
        copy_from(lax.rem(me + n - i, n)).wait_recv()
        return carry

    lax.fori_loop(1, n, finish, 0)
    own.wait()


def _exchange(x, collective_id):
    n = x.shape[0]
    return pl.pallas_call(
        functools.partial(_exchange_kernel, n),
        out_shape=jax.ShapeDtypeStruct(x.shape, x.dtype),
        in_specs=[pl.BlockSpec(memory_space=pl.ANY)],
        out_specs=pl.BlockSpec(memory_space=pl.ANY),
        scratch_shapes=[
            pltpu.SemaphoreType.DMA((n,)),
            pltpu.SemaphoreType.DMA((n,)),
            pltpu.SemaphoreType.DMA(()),
        ],
        compiler_params=pltpu.CompilerParams(collective_id=collective_id, has_side_effects=True),
    )(x)


def _swap_pair(x):
    return lax.ppermute(x, "core", [(0, 1), (1, 0)])


def body(
    tokens,
    cotangent,
    expert_ids,
    route_weight,
    forget_mask,
    lengths,
    gate_weight,
    up_weight,
    down_weight,
):
    tok_rows = tokens.shape[0]
    features = tokens.shape[1]
    half = features // 2
    top_count = expert_ids.shape[1]
    owners = lax.axis_size("dp")
    groups = lax.axis_size("zh")
    block = features // (2 * groups)
    capacity = 5 * tok_rows * top_count // (4 * owners)
    core = lax.axis_index("core")
    is_first = core == 0

    seq_count = lengths.shape[0]
    seq_len = tok_rows * owners // seq_count
    token_index = lax.axis_index("dp") * tok_rows + jnp.arange(tok_rows, dtype=jnp.int32)
    seq_id = token_index // seq_len
    seq_pos = token_index - seq_id * seq_len
    in_seq = seq_id[:, None] == jnp.arange(seq_count, dtype=jnp.int32)[None, :]
    limits = jnp.sum(jnp.where(in_seq, lengths[None, :], 0), axis=1)
    is_valid = (seq_pos < limits).astype(jnp.int32)
    forget = is_valid * forget_mask
    retain = is_valid - forget

    shares = route_weight / jnp.sum(route_weight, axis=1, keepdims=True)
    share_flat = shares.reshape(-1)
    assigned = tok_rows * top_count
    flat_ids = expert_ids.reshape(-1)
    one_hot = (flat_ids[:, None] == jnp.arange(owners, dtype=jnp.int32)[None, :]).astype(jnp.int32)
    before = jnp.cumsum(one_hot, axis=0) - one_hot
    slot_id = jnp.sum(before * one_hot, axis=1)
    target = flat_ids * capacity + slot_id
    slots_all = owners * capacity
    hit = target[None, :] == jnp.arange(slots_all, dtype=jnp.int32)[:, None]
    hit_tok = jnp.any(hit.reshape(slots_all, tok_rows, top_count), axis=2)

    slot_share = jnp.sum(jnp.where(hit, share_flat[None, :], 0.0), axis=1)
    share_hi = lax.reduce_precision(slot_share, exponent_bits=8, mantissa_bits=7)
    rest = slot_share - share_hi
    share_mid = lax.reduce_precision(rest, exponent_bits=8, mantissa_bits=7)
    share_lo = rest - share_mid
    slot_forget = jnp.sum(jnp.where(hit_tok, forget[None, :], 0), axis=1).astype(jnp.float32)
    slot_retain = jnp.sum(jnp.where(hit_tok, retain[None, :], 0), axis=1).astype(jnp.float32)
    per_slot = jnp.stack([share_hi, share_mid, share_lo, slot_forget, slot_retain], axis=1)
    per_slot = per_slot.reshape(owners, capacity * 5)
    local_counts = jnp.stack([jnp.sum(forget), jnp.sum(retain)]).astype(jnp.float32)
    meta = jnp.concatenate(
        [
            per_slot,
            jnp.broadcast_to(local_counts[None, :], (owners, 2)),
            jnp.zeros((owners, features - capacity * 5 - 2), jnp.float32),
        ],
        axis=1,
    ).astype(jnp.bfloat16)
    my_tokens = lax.dynamic_slice_in_dim(tokens, core * half, half, axis=1)
    my_cotan = lax.dynamic_slice_in_dim(cotangent, core * half, half, axis=1)
    both = jnp.concatenate([my_tokens, my_cotan], axis=1)
    send = jnp.dot(hit_tok.astype(both.dtype), both, preferred_element_type=jnp.float32).astype(both.dtype)
    lanes = 128
    send = jnp.concatenate(
        [send.reshape(owners, capacity * features // lanes, lanes), meta.reshape(owners, features // lanes, lanes)],
        axis=1,
    )
    recv = _exchange(send, 0)
    got = recv[:, : capacity * features // lanes, :].reshape(slots_all, features)
    got_meta = recv[:, capacity * features // lanes :, :].reshape(owners, features).astype(jnp.float32)
    other = _swap_pair(got)
    lower = jnp.where(is_first, got, other)
    upper = jnp.where(is_first, other, got)
    rows_in = jnp.concatenate([lower[:, :half], upper[:, :half]], axis=1)
    cot_in = jnp.concatenate([lower[:, half:], upper[:, half:]], axis=1)

    n_forget = jnp.sum(got_meta[:, capacity * 5])
    n_retain = jnp.sum(got_meta[:, capacity * 5 + 1])
    slot_meta = got_meta[:, : capacity * 5].reshape(slots_all, 5)
    got_share = (slot_meta[:, 0] + slot_meta[:, 1]) + slot_meta[:, 2]
    coefficient = float(top_count * tok_rows) * (
        slot_meta[:, 4] / n_retain - slot_meta[:, 3] / n_forget
    )
    routed = ((coefficient * got_share)[:, None] * cot_in.astype(jnp.float32)).astype(jnp.bfloat16)

    contract_last = (((1,), (1,)), ((), ()))
    contract_first = (((0,), (0,)), ((), ()))
    gate_pre = lax.dot_general(
        gate_weight[0], rows_in, contract_last, preferred_element_type=jnp.float32
    )
    up_pre = lax.dot_general(
        up_weight[0], rows_in, contract_last, preferred_element_type=jnp.float32
    )
    sigmoid_gate = jax.nn.sigmoid(gate_pre)
    hidden = (gate_pre * sigmoid_gate * up_pre).astype(jnp.bfloat16)
    partial_out = lax.dot_general(
        hidden, down_weight[0], contract_first, preferred_element_type=jnp.float32
    ).astype(jnp.bfloat16)
    pieces = partial_out.reshape(slots_all, groups, 2, block)
    keep = jnp.where(is_first, pieces[:, :, 0, :], pieces[:, :, 1, :])
    give = jnp.where(is_first, pieces[:, :, 1, :], pieces[:, :, 0, :])
    pair_sum = (keep.astype(jnp.float32) + _swap_pair(give).astype(jnp.float32)).astype(jnp.bfloat16)
    returned = _exchange(pair_sum.reshape(owners, capacity * groups * block // lanes, lanes), 1)
    picked = jnp.dot(
        hit.T.astype(returned.dtype),
        returned.reshape(slots_all, groups * block),
        preferred_element_type=jnp.float32,
    ) * share_flat[:, None]
    token_terms = jnp.sum(picked.reshape(tok_rows, top_count, groups, block), axis=1)
    spread = lax.all_to_all(
        jnp.transpose(token_terms, (1, 0, 2)), "zh", split_axis=0, concat_axis=0, tiled=True
    )
    mixed_out = jnp.sum(spread, axis=0).astype(jnp.bfloat16)

    grad_down = jnp.dot(hidden, routed, preferred_element_type=jnp.float32)
    dhidden = lax.dot_general(
        down_weight[0], routed, contract_last, preferred_element_type=jnp.float32
    )
    dgate = (dhidden * up_pre * sigmoid_gate * (1.0 + gate_pre * (1.0 - sigmoid_gate))).astype(
        jnp.bfloat16
    )
    dup = (dhidden * gate_pre * sigmoid_gate).astype(jnp.bfloat16)
    grad_gate = jnp.dot(dgate, rows_in, preferred_element_type=jnp.float32)
    grad_up = jnp.dot(dup, rows_in, preferred_element_type=jnp.float32)
    return (
        mixed_out,
        grad_gate.astype(jnp.bfloat16)[None],
        grad_up.astype(jnp.bfloat16)[None],
        grad_down.astype(jnp.bfloat16)[None],
    )


def solution(mesh):
    n_dp = mesh.shape["dp"]
    n_tensor = mesh.shape["tensor"]
    fine = Mesh(
        np.asarray(mesh.devices).reshape(n_dp, n_tensor // 2, 2), ("dp", "zh", "core")
    )
    tp = ("zh", "core")
    in_specs = (
        P("dp", None),
        P("dp", None),
        P("dp", None),
        P("dp", None),
        P("dp"),
        P(),
        P("dp", tp, None),
        P("dp", tp, None),
        P("dp", tp, None),
    )
    out_specs = (
        P("dp", tp),
        P("dp", tp, None),
        P("dp", tp, None),
        P("dp", tp, None),
    )
    return jax.shard_map(body, mesh=fine, in_specs=in_specs, out_specs=out_specs, check_vma=False)
```

```python
import functools

import jax
import jax.numpy as jnp
import numpy as np
from jax import lax
from jax.experimental import pallas as pl
from jax.experimental.pallas import tpu as pltpu
from jax.sharding import Mesh
from jax.sharding import PartitionSpec as P


MESH = pl.DeviceIdType.MESH


def _exchange_kernel(n, axis, x_ref, y_ref, send_sem, recv_sem, own_sem):
    me = lax.axis_index(axis)

    def copy_to(peer):
        return pltpu.make_async_remote_copy(
            src_ref=x_ref.at[peer],
            dst_ref=y_ref.at[me],
            send_sem=send_sem.at[peer],
            recv_sem=recv_sem.at[me],
            device_id={axis: peer},
            device_id_type=MESH,
        )

    def copy_from(source):
        return pltpu.make_async_remote_copy(
            src_ref=x_ref.at[source],
            dst_ref=y_ref.at[source],
            send_sem=send_sem.at[source],
            recv_sem=recv_sem.at[source],
            device_id={axis: source},
            device_id_type=MESH,
        )

    barrier = pltpu.get_barrier_semaphore()

    def greet(i, carry):
        pl.semaphore_signal(barrier, inc=1, device_id={axis: lax.rem(me + i, n)}, device_id_type=MESH)
        return carry

    lax.fori_loop(1, n, greet, 0)
    pl.semaphore_wait(barrier, n - 1)
    own = pltpu.make_async_copy(x_ref.at[me], y_ref.at[me], own_sem)
    own.start()

    def send(i, carry):
        copy_to(lax.rem(me + i, n)).start()
        return carry

    lax.fori_loop(1, n, send, 0)

    def finish(i, carry):
        copy_to(lax.rem(me + i, n)).wait_send()
        copy_from(lax.rem(me + n - i, n)).wait_recv()
        return carry

    lax.fori_loop(1, n, finish, 0)
    own.wait()


def _exchange(x, collective_id, axis="dp"):
    n = x.shape[0]
    return pl.pallas_call(
        functools.partial(_exchange_kernel, n, axis),
        out_shape=jax.ShapeDtypeStruct(x.shape, x.dtype),
        in_specs=[pl.BlockSpec(memory_space=pl.ANY)],
        out_specs=pl.BlockSpec(memory_space=pl.ANY),
        scratch_shapes=[
            pltpu.SemaphoreType.DMA((n,)),
            pltpu.SemaphoreType.DMA((n,)),
            pltpu.SemaphoreType.DMA(()),
        ],
        compiler_params=pltpu.CompilerParams(collective_id=collective_id, has_side_effects=True),
    )(x)


def _swap_pair(x):
    return lax.ppermute(x, "core", [(0, 1), (1, 0)])


def body(
    tokens,
    cotangent,
    expert_ids,
    route_weight,
    forget_mask,
    lengths,
    gate_weight,
    up_weight,
    down_weight,
):
    tok_rows = tokens.shape[0]
    features = tokens.shape[1]
    half = features // 2
    top_count = expert_ids.shape[1]
    owners = lax.axis_size("dp")
    groups = lax.axis_size("zh")
    block = features // (2 * groups)
    capacity = 5 * tok_rows * top_count // (4 * owners)
    core = lax.axis_index("core")
    is_first = core == 0

    seq_count = lengths.shape[0]
    seq_len = tok_rows * owners // seq_count
    token_index = lax.axis_index("dp") * tok_rows + jnp.arange(tok_rows, dtype=jnp.int32)
    seq_id = token_index // seq_len
    seq_pos = token_index - seq_id * seq_len
    in_seq = seq_id[:, None] == jnp.arange(seq_count, dtype=jnp.int32)[None, :]
    limits = jnp.sum(jnp.where(in_seq, lengths[None, :], 0), axis=1)
    is_valid = (seq_pos < limits).astype(jnp.int32)
    forget = is_valid * forget_mask
    retain = is_valid - forget

    shares = route_weight / jnp.sum(route_weight, axis=1, keepdims=True)
    share_flat = shares.reshape(-1)
    assigned = tok_rows * top_count
    flat_ids = expert_ids.reshape(-1)
    one_hot = (flat_ids[:, None] == jnp.arange(owners, dtype=jnp.int32)[None, :]).astype(jnp.int32)
    before = jnp.cumsum(one_hot, axis=0) - one_hot
    slot_id = jnp.sum(before * one_hot, axis=1)
    target = flat_ids * capacity + slot_id
    slots_all = owners * capacity
    hit = target[None, :] == jnp.arange(slots_all, dtype=jnp.int32)[:, None]
    hit_tok = jnp.any(hit.reshape(slots_all, tok_rows, top_count), axis=2)

    slot_share = jnp.sum(jnp.where(hit, share_flat[None, :], 0.0), axis=1)
    share_hi = lax.reduce_precision(slot_share, exponent_bits=8, mantissa_bits=7)
    rest = slot_share - share_hi
    share_mid = lax.reduce_precision(rest, exponent_bits=8, mantissa_bits=7)
    share_lo = rest - share_mid
    slot_forget = jnp.sum(jnp.where(hit_tok, forget[None, :], 0), axis=1).astype(jnp.float32)
    slot_retain = jnp.sum(jnp.where(hit_tok, retain[None, :], 0), axis=1).astype(jnp.float32)
    per_slot = jnp.stack([share_hi, share_mid, share_lo, slot_forget, slot_retain], axis=1)
    per_slot = per_slot.reshape(owners, capacity * 5)
    local_counts = jnp.stack([jnp.sum(forget), jnp.sum(retain)]).astype(jnp.float32)
    meta = jnp.concatenate(
        [
            per_slot,
            jnp.broadcast_to(local_counts[None, :], (owners, 2)),
            jnp.zeros((owners, features - capacity * 5 - 2), jnp.float32),
        ],
        axis=1,
    ).astype(jnp.bfloat16)
    my_tokens = lax.dynamic_slice_in_dim(tokens, core * half, half, axis=1)
    my_cotan = lax.dynamic_slice_in_dim(cotangent, core * half, half, axis=1)
    both = jnp.concatenate([my_tokens, my_cotan], axis=1)
    send = jnp.dot(hit_tok.astype(both.dtype), both, preferred_element_type=jnp.float32).astype(both.dtype)
    lanes = 128
    send = jnp.concatenate(
        [send.reshape(owners, capacity * features // lanes, lanes), meta.reshape(owners, features // lanes, lanes)],
        axis=1,
    )
    recv = _exchange(send, 0)
    got = recv[:, : capacity * features // lanes, :].reshape(slots_all, features)
    got_meta = recv[:, capacity * features // lanes :, :].reshape(owners, features).astype(jnp.float32)
    other = _swap_pair(got)
    lower = jnp.where(is_first, got, other)
    upper = jnp.where(is_first, other, got)
    rows_in = jnp.concatenate([lower[:, :half], upper[:, :half]], axis=1)
    cot_in = jnp.concatenate([lower[:, half:], upper[:, half:]], axis=1)

    n_forget = jnp.sum(got_meta[:, capacity * 5])
    n_retain = jnp.sum(got_meta[:, capacity * 5 + 1])
    slot_meta = got_meta[:, : capacity * 5].reshape(slots_all, 5)
    got_share = (slot_meta[:, 0] + slot_meta[:, 1]) + slot_meta[:, 2]
    coefficient = float(top_count * tok_rows) * (
        slot_meta[:, 4] / n_retain - slot_meta[:, 3] / n_forget
    )
    routed = ((coefficient * got_share)[:, None] * cot_in.astype(jnp.float32)).astype(jnp.bfloat16)

    contract_last = (((1,), (1,)), ((), ()))
    contract_first = (((0,), (0,)), ((), ()))
    gate_pre = lax.dot_general(
        gate_weight[0], rows_in, contract_last, preferred_element_type=jnp.float32
    )
    up_pre = lax.dot_general(
        up_weight[0], rows_in, contract_last, preferred_element_type=jnp.float32
    )
    sigmoid_gate = jax.nn.sigmoid(gate_pre)
    hidden = (gate_pre * sigmoid_gate * up_pre).astype(jnp.bfloat16)
    partial_out = lax.dot_general(
        hidden, down_weight[0], contract_first, preferred_element_type=jnp.float32
    ).astype(jnp.bfloat16)
    pieces = partial_out.reshape(slots_all, groups, 2, block)
    keep = jnp.where(is_first, pieces[:, :, 0, :], pieces[:, :, 1, :])
    give = jnp.where(is_first, pieces[:, :, 1, :], pieces[:, :, 0, :])
    pair_sum = (keep.astype(jnp.float32) + _swap_pair(give).astype(jnp.float32)).astype(jnp.bfloat16)
    by_group = _exchange(jnp.transpose(pair_sum, (1, 0, 2)), 2, axis="zh")
    slice_sum = jnp.sum(by_group.astype(jnp.float32), axis=0).astype(jnp.bfloat16)
    returned = _exchange(slice_sum.reshape(owners, capacity * block // lanes, lanes), 1)
    picked = jnp.dot(
        hit.T.astype(returned.dtype),
        returned.reshape(slots_all, block),
        preferred_element_type=jnp.float32,
    ) * share_flat[:, None]
    mixed_out = jnp.sum(picked.reshape(tok_rows, top_count, block), axis=1).astype(jnp.bfloat16)

    grad_down = jnp.dot(hidden, routed, preferred_element_type=jnp.float32)
    dhidden = lax.dot_general(
        down_weight[0], routed, contract_last, preferred_element_type=jnp.float32
    )
    dgate = (dhidden * up_pre * sigmoid_gate * (1.0 + gate_pre * (1.0 - sigmoid_gate))).astype(
        jnp.bfloat16
    )
    dup = (dhidden * gate_pre * sigmoid_gate).astype(jnp.bfloat16)
    grad_gate = jnp.dot(dgate, rows_in, preferred_element_type=jnp.float32)
    grad_up = jnp.dot(dup, rows_in, preferred_element_type=jnp.float32)
    return (
        mixed_out,
        grad_gate.astype(jnp.bfloat16)[None],
        grad_up.astype(jnp.bfloat16)[None],
        grad_down.astype(jnp.bfloat16)[None],
    )


def solution(mesh):
    n_dp = mesh.shape["dp"]
    n_tensor = mesh.shape["tensor"]
    fine = Mesh(
        np.asarray(mesh.devices).reshape(n_dp, n_tensor // 2, 2), ("dp", "zh", "core")
    )
    tp = ("zh", "core")
    in_specs = (
        P("dp", None),
        P("dp", None),
        P("dp", None),
        P("dp", None),
        P("dp"),
        P(),
        P("dp", tp, None),
        P("dp", tp, None),
        P("dp", tp, None),
    )
    out_specs = (
        P("dp", tp),
        P("dp", tp, None),
        P("dp", tp, None),
        P("dp", tp, None),
    )
    return jax.shard_map(body, mesh=fine, in_specs=in_specs, out_specs=out_specs, check_vma=False)
```

```python
import functools

import jax
import jax.numpy as jnp
import numpy as np
from jax import lax
from jax.experimental import pallas as pl
from jax.experimental.pallas import tpu as pltpu
from jax.sharding import Mesh
from jax.sharding import PartitionSpec as P


MESH = pl.DeviceIdType.MESH


def _exchange_kernel(n, axis, x_ref, y_ref, send_sem, recv_sem, own_sem):
    me = lax.axis_index(axis)

    def copy_to(peer):
        return pltpu.make_async_remote_copy(
            src_ref=x_ref.at[peer],
            dst_ref=y_ref.at[me],
            send_sem=send_sem.at[peer],
            recv_sem=recv_sem.at[me],
            device_id={axis: peer},
            device_id_type=MESH,
        )

    def copy_from(source):
        return pltpu.make_async_remote_copy(
            src_ref=x_ref.at[source],
            dst_ref=y_ref.at[source],
            send_sem=send_sem.at[source],
            recv_sem=recv_sem.at[source],
            device_id={axis: source},
            device_id_type=MESH,
        )

    barrier = pltpu.get_barrier_semaphore()

    def greet(i, carry):
        pl.semaphore_signal(barrier, inc=1, device_id={axis: lax.rem(me + i, n)}, device_id_type=MESH)
        return carry

    lax.fori_loop(1, n, greet, 0)
    pl.semaphore_wait(barrier, n - 1)
    own = pltpu.make_async_copy(x_ref.at[me], y_ref.at[me], own_sem)
    own.start()

    def send(i, carry):
        copy_to(lax.rem(me + i, n)).start()
        return carry

    lax.fori_loop(1, n, send, 0)

    def finish(i, carry):
        copy_to(lax.rem(me + i, n)).wait_send()
        copy_from(lax.rem(me + n - i, n)).wait_recv()
        return carry

    lax.fori_loop(1, n, finish, 0)
    own.wait()


def _exchange(x, collective_id, axis="dp"):
    n = x.shape[0]
    return pl.pallas_call(
        functools.partial(_exchange_kernel, n, axis),
        out_shape=jax.ShapeDtypeStruct(x.shape, x.dtype),
        in_specs=[pl.BlockSpec(memory_space=pl.ANY)],
        out_specs=pl.BlockSpec(memory_space=pl.ANY),
        scratch_shapes=[
            pltpu.SemaphoreType.DMA((n,)),
            pltpu.SemaphoreType.DMA((n,)),
            pltpu.SemaphoreType.DMA(()),
        ],
        compiler_params=pltpu.CompilerParams(collective_id=collective_id, has_side_effects=True),
    )(x)


def _swap_pair(x):
    return lax.ppermute(x, "core", [(0, 1), (1, 0)])


def body(
    tokens,
    cotangent,
    expert_ids,
    route_weight,
    forget_mask,
    lengths,
    gate_weight,
    up_weight,
    down_weight,
):
    tok_rows = tokens.shape[0]
    features = tokens.shape[1]
    half = features // 2
    top_count = expert_ids.shape[1]
    owners = lax.axis_size("dp")
    groups = lax.axis_size("zh")
    block = features // (2 * groups)
    capacity = 5 * tok_rows * top_count // (4 * owners)
    core = lax.axis_index("core")
    is_first = core == 0

    seq_count = lengths.shape[0]
    seq_len = tok_rows * owners // seq_count
    token_index = lax.axis_index("dp") * tok_rows + jnp.arange(tok_rows, dtype=jnp.int32)
    seq_id = token_index // seq_len
    seq_pos = token_index - seq_id * seq_len
    in_seq = seq_id[:, None] == jnp.arange(seq_count, dtype=jnp.int32)[None, :]
    limits = jnp.sum(jnp.where(in_seq, lengths[None, :], 0), axis=1)
    is_valid = (seq_pos < limits).astype(jnp.int32)
    forget = is_valid * forget_mask
    retain = is_valid - forget

    shares = route_weight / jnp.sum(route_weight, axis=1, keepdims=True)
    share_flat = shares.reshape(-1)
    assigned = tok_rows * top_count
    flat_ids = expert_ids.reshape(-1)
    one_hot = (flat_ids[:, None] == jnp.arange(owners, dtype=jnp.int32)[None, :]).astype(jnp.int32)
    before = jnp.cumsum(one_hot, axis=0) - one_hot
    slot_id = jnp.sum(before * one_hot, axis=1)
    target = flat_ids * capacity + slot_id
    slots_all = owners * capacity
    hit = target[None, :] == jnp.arange(slots_all, dtype=jnp.int32)[:, None]
    hit_tok = jnp.any(hit.reshape(slots_all, tok_rows, top_count), axis=2)

    slot_share = jnp.sum(jnp.where(hit, share_flat[None, :], 0.0), axis=1)
    share_hi = lax.reduce_precision(slot_share, exponent_bits=8, mantissa_bits=7)
    rest = slot_share - share_hi
    share_mid = lax.reduce_precision(rest, exponent_bits=8, mantissa_bits=7)
    share_lo = rest - share_mid
    slot_forget = jnp.sum(jnp.where(hit_tok, forget[None, :], 0), axis=1).astype(jnp.float32)
    slot_retain = jnp.sum(jnp.where(hit_tok, retain[None, :], 0), axis=1).astype(jnp.float32)
    per_slot = jnp.stack([share_hi, share_mid, share_lo, slot_forget, slot_retain], axis=1)
    per_slot = per_slot.reshape(owners, capacity * 5)
    local_counts = jnp.stack([jnp.sum(forget), jnp.sum(retain)]).astype(jnp.float32)
    meta = jnp.concatenate(
        [
            per_slot,
            jnp.broadcast_to(local_counts[None, :], (owners, 2)),
            jnp.zeros((owners, features - capacity * 5 - 2), jnp.float32),
        ],
        axis=1,
    ).astype(jnp.bfloat16)
    my_tokens = lax.dynamic_slice_in_dim(tokens, core * half, half, axis=1)
    my_cotan = lax.dynamic_slice_in_dim(cotangent, core * half, half, axis=1)
    both = jnp.concatenate([my_tokens, my_cotan], axis=1)
    send = jnp.dot(hit_tok.astype(both.dtype), both, preferred_element_type=jnp.float32).astype(both.dtype)
    lanes = 128
    send = jnp.concatenate(
        [send.reshape(owners, capacity * features // lanes, lanes), meta.reshape(owners, features // lanes, lanes)],
        axis=1,
    )
    recv = _exchange(send, 0)
    got = recv[:, : capacity * features // lanes, :].reshape(slots_all, features)
    got_meta = recv[:, capacity * features // lanes :, :].reshape(owners, features).astype(jnp.float32)
    other = _swap_pair(got)
    lower = jnp.where(is_first, got, other)
    upper = jnp.where(is_first, other, got)
    rows_in = jnp.concatenate([lower[:, :half], upper[:, :half]], axis=1)
    cot_in = jnp.concatenate([lower[:, half:], upper[:, half:]], axis=1)

    n_forget = jnp.sum(got_meta[:, capacity * 5])
    n_retain = jnp.sum(got_meta[:, capacity * 5 + 1])
    slot_meta = got_meta[:, : capacity * 5].reshape(slots_all, 5)
    got_share = (slot_meta[:, 0] + slot_meta[:, 1]) + slot_meta[:, 2]
    coefficient = float(top_count * tok_rows) * (
        slot_meta[:, 4] / n_retain - slot_meta[:, 3] / n_forget
    )
    routed = ((coefficient * got_share)[:, None] * cot_in.astype(jnp.float32)).astype(jnp.bfloat16)

    contract_last = (((1,), (1,)), ((), ()))
    contract_first = (((0,), (0,)), ((), ()))
    gate_pre = lax.dot_general(
        gate_weight[0], rows_in, contract_last, preferred_element_type=jnp.float32
    )
    up_pre = lax.dot_general(
        up_weight[0], rows_in, contract_last, preferred_element_type=jnp.float32
    )
    sigmoid_gate = jax.nn.sigmoid(gate_pre)
    hidden = (gate_pre * sigmoid_gate * up_pre).astype(jnp.bfloat16)
    partial_out = lax.dot_general(
        hidden, down_weight[0], contract_first, preferred_element_type=jnp.float32
    ).astype(jnp.bfloat16)
    pieces = partial_out.reshape(slots_all, groups, 2, block)
    keep = jnp.where(is_first, pieces[:, :, 0, :], pieces[:, :, 1, :])
    give = jnp.where(is_first, pieces[:, :, 1, :], pieces[:, :, 0, :])
    pair_sum = (keep.astype(jnp.float32) + _swap_pair(give).astype(jnp.float32)).astype(jnp.bfloat16)
    returned = _exchange(pair_sum.reshape(owners, capacity * groups * block // lanes, lanes), 1)
    picked = jnp.dot(
        hit.T.astype(returned.dtype),
        returned.reshape(slots_all, groups * block),
        preferred_element_type=jnp.float32,
    ) * share_flat[:, None]
    token_terms = jnp.sum(picked.reshape(tok_rows, top_count, groups, block), axis=1)
    by_group = _exchange(jnp.transpose(token_terms, (1, 0, 2)), 2, axis="zh")
    mixed_out = jnp.sum(by_group, axis=0).astype(jnp.bfloat16)

    grad_down = jnp.dot(hidden, routed, preferred_element_type=jnp.float32)
    dhidden = lax.dot_general(
        down_weight[0], routed, contract_last, preferred_element_type=jnp.float32
    )
    dgate = (dhidden * up_pre * sigmoid_gate * (1.0 + gate_pre * (1.0 - sigmoid_gate))).astype(
        jnp.bfloat16
    )
    dup = (dhidden * gate_pre * sigmoid_gate).astype(jnp.bfloat16)
    grad_gate = jnp.dot(dgate, rows_in, preferred_element_type=jnp.float32)
    grad_up = jnp.dot(dup, rows_in, preferred_element_type=jnp.float32)
    return (
        mixed_out,
        grad_gate.astype(jnp.bfloat16)[None],
        grad_up.astype(jnp.bfloat16)[None],
        grad_down.astype(jnp.bfloat16)[None],
    )


def solution(mesh):
    n_dp = mesh.shape["dp"]
    n_tensor = mesh.shape["tensor"]
    fine = Mesh(
        np.asarray(mesh.devices).reshape(n_dp, n_tensor // 2, 2), ("dp", "zh", "core")
    )
    tp = ("zh", "core")
    in_specs = (
        P("dp", None),
        P("dp", None),
        P("dp", None),
        P("dp", None),
        P("dp"),
        P(),
        P("dp", tp, None),
        P("dp", tp, None),
        P("dp", tp, None),
    )
    out_specs = (
        P("dp", tp),
        P("dp", tp, None),
        P("dp", tp, None),
        P("dp", tp, None),
    )
    return jax.shard_map(body, mesh=fine, in_specs=in_specs, out_specs=out_specs, check_vma=False)
```

```python
import functools

import jax
import jax.numpy as jnp
import numpy as np
from jax import lax
from jax.experimental import pallas as pl
from jax.experimental.pallas import tpu as pltpu
from jax.sharding import Mesh
from jax.sharding import PartitionSpec as P


MESH = pl.DeviceIdType.MESH


def _exchange_kernel(n, axis, x_ref, y_ref, send_sem, recv_sem, own_sem):
    me = lax.axis_index(axis)

    def copy_to(peer):
        return pltpu.make_async_remote_copy(
            src_ref=x_ref.at[peer],
            dst_ref=y_ref.at[me],
            send_sem=send_sem.at[peer],
            recv_sem=recv_sem.at[me],
            device_id={axis: peer},
            device_id_type=MESH,
        )

    def copy_from(source):
        return pltpu.make_async_remote_copy(
            src_ref=x_ref.at[source],
            dst_ref=y_ref.at[source],
            send_sem=send_sem.at[source],
            recv_sem=recv_sem.at[source],
            device_id={axis: source},
            device_id_type=MESH,
        )

    barrier = pltpu.get_barrier_semaphore()

    def greet(i, carry):
        pl.semaphore_signal(barrier, inc=1, device_id={axis: lax.rem(me + i, n)}, device_id_type=MESH)
        return carry

    lax.fori_loop(1, n, greet, 0)
    pl.semaphore_wait(barrier, n - 1)
    own = pltpu.make_async_copy(x_ref.at[me], y_ref.at[me], own_sem)
    own.start()

    def send(i, carry):
        copy_to(lax.rem(me + i, n)).start()
        return carry

    lax.fori_loop(1, n, send, 0)

    def finish(i, carry):
        copy_to(lax.rem(me + i, n)).wait_send()
        copy_from(lax.rem(me + n - i, n)).wait_recv()
        return carry

    lax.fori_loop(1, n, finish, 0)
    own.wait()


def _exchange(x, collective_id, axis="dp"):
    n = x.shape[0]
    return pl.pallas_call(
        functools.partial(_exchange_kernel, n, axis),
        out_shape=jax.ShapeDtypeStruct(x.shape, x.dtype),
        in_specs=[pl.BlockSpec(memory_space=pl.ANY)],
        out_specs=pl.BlockSpec(memory_space=pl.ANY),
        scratch_shapes=[
            pltpu.SemaphoreType.DMA((n,)),
            pltpu.SemaphoreType.DMA((n,)),
            pltpu.SemaphoreType.DMA(()),
        ],
        compiler_params=pltpu.CompilerParams(collective_id=collective_id, has_side_effects=True),
    )(x)


def _swap_pair(x):
    return lax.ppermute(x, "core", [(0, 1), (1, 0)])


def body(
    tokens,
    cotangent,
    expert_ids,
    route_weight,
    forget_mask,
    lengths,
    gate_weight,
    up_weight,
    down_weight,
):
    tok_rows = tokens.shape[0]
    features = tokens.shape[1]
    half = features // 2
    top_count = expert_ids.shape[1]
    owners = lax.axis_size("dp")
    groups = lax.axis_size("zh")
    block = features // (2 * groups)
    capacity = 5 * tok_rows * top_count // (4 * owners)
    core = lax.axis_index("core")
    is_first = core == 0

    seq_count = lengths.shape[0]
    seq_len = tok_rows * owners // seq_count
    token_index = lax.axis_index("dp") * tok_rows + jnp.arange(tok_rows, dtype=jnp.int32)
    seq_id = token_index // seq_len
    seq_pos = token_index - seq_id * seq_len
    in_seq = seq_id[:, None] == jnp.arange(seq_count, dtype=jnp.int32)[None, :]
    limits = jnp.sum(jnp.where(in_seq, lengths[None, :], 0), axis=1)
    is_valid = (seq_pos < limits).astype(jnp.int32)
    forget = is_valid * forget_mask
    retain = is_valid - forget

    shares = route_weight / jnp.sum(route_weight, axis=1, keepdims=True)
    share_flat = shares.reshape(-1)
    assigned = tok_rows * top_count
    flat_ids = expert_ids.reshape(-1)
    one_hot = (flat_ids[:, None] == jnp.arange(owners, dtype=jnp.int32)[None, :]).astype(jnp.int32)
    before = jnp.cumsum(one_hot, axis=0) - one_hot
    slot_id = jnp.sum(before * one_hot, axis=1)
    target = flat_ids * capacity + slot_id
    slots_all = owners * capacity
    hit = target[None, :] == jnp.arange(slots_all, dtype=jnp.int32)[:, None]
    hit_tok = jnp.any(hit.reshape(slots_all, tok_rows, top_count), axis=2)

    slot_share = jnp.sum(jnp.where(hit, share_flat[None, :], 0.0), axis=1)
    share_hi = lax.reduce_precision(slot_share, exponent_bits=8, mantissa_bits=7)
    rest = slot_share - share_hi
    share_mid = lax.reduce_precision(rest, exponent_bits=8, mantissa_bits=7)
    share_lo = rest - share_mid
    slot_forget = jnp.sum(jnp.where(hit_tok, forget[None, :], 0), axis=1).astype(jnp.float32)
    slot_retain = jnp.sum(jnp.where(hit_tok, retain[None, :], 0), axis=1).astype(jnp.float32)
    per_slot = jnp.stack([share_hi, share_mid, share_lo, slot_forget, slot_retain], axis=1)
    per_slot = per_slot.reshape(owners, capacity * 5)
    local_counts = jnp.stack([jnp.sum(forget), jnp.sum(retain)]).astype(jnp.float32)
    meta = jnp.concatenate(
        [
            per_slot,
            jnp.broadcast_to(local_counts[None, :], (owners, 2)),
            jnp.zeros((owners, features - capacity * 5 - 2), jnp.float32),
        ],
        axis=1,
    ).astype(jnp.bfloat16)
    my_tokens = lax.dynamic_slice_in_dim(tokens, core * half, half, axis=1)
    my_cotan = lax.dynamic_slice_in_dim(cotangent, core * half, half, axis=1)
    both = jnp.concatenate([my_tokens, my_cotan], axis=1)
    send = jnp.dot(hit_tok.astype(both.dtype), both, preferred_element_type=jnp.float32).astype(both.dtype)
    lanes = 128
    send = jnp.concatenate(
        [send.reshape(owners, capacity * features // lanes, lanes), meta.reshape(owners, features // lanes, lanes)],
        axis=1,
    )
    recv = _exchange(send, 0)
    got = recv[:, : capacity * features // lanes, :].reshape(slots_all, features)
    got_meta = recv[:, capacity * features // lanes :, :].reshape(owners, features).astype(jnp.float32)
    other = _swap_pair(got)
    lower = jnp.where(is_first, got, other)
    upper = jnp.where(is_first, other, got)
    rows_in = jnp.concatenate([lower[:, :half], upper[:, :half]], axis=1)
    cot_in = jnp.concatenate([lower[:, half:], upper[:, half:]], axis=1)

    n_forget = jnp.sum(got_meta[:, capacity * 5])
    n_retain = jnp.sum(got_meta[:, capacity * 5 + 1])
    slot_meta = got_meta[:, : capacity * 5].reshape(slots_all, 5)
    got_share = (slot_meta[:, 0] + slot_meta[:, 1]) + slot_meta[:, 2]
    coefficient = float(top_count * tok_rows) * (
        slot_meta[:, 4] / n_retain - slot_meta[:, 3] / n_forget
    )
    routed = ((coefficient * got_share)[:, None] * cot_in.astype(jnp.float32)).astype(jnp.bfloat16)

    contract_last = (((1,), (1,)), ((), ()))
    contract_first = (((0,), (0,)), ((), ()))
    gate_pre = lax.dot_general(
        gate_weight[0], rows_in, contract_last, preferred_element_type=jnp.float32
    )
    up_pre = lax.dot_general(
        up_weight[0], rows_in, contract_last, preferred_element_type=jnp.float32
    )
    sigmoid_gate = jax.nn.sigmoid(gate_pre)
    hidden = (gate_pre * sigmoid_gate * up_pre).astype(jnp.bfloat16)
    partial_out = lax.dot_general(
        hidden, down_weight[0], contract_first, preferred_element_type=jnp.float32
    ).astype(jnp.bfloat16)
    pieces = partial_out.reshape(slots_all, groups, 2, block)
    keep = jnp.where(is_first, pieces[:, :, 0, :], pieces[:, :, 1, :])
    give = jnp.where(is_first, pieces[:, :, 1, :], pieces[:, :, 0, :])
    pair_sum = (keep.astype(jnp.float32) + _swap_pair(give).astype(jnp.float32)).astype(jnp.bfloat16)
    slice_sum = lax.psum_scatter(
        jnp.transpose(pair_sum, (1, 0, 2)), "zh", scatter_dimension=0, tiled=True
    ).reshape(slots_all, block)
    returned = _exchange(slice_sum.reshape(owners, capacity * block // lanes, lanes), 1)
    picked = jnp.dot(
        hit.T.astype(returned.dtype),
        returned.reshape(slots_all, block),
        preferred_element_type=jnp.float32,
    ) * share_flat[:, None]
    mixed_out = jnp.sum(picked.reshape(tok_rows, top_count, block), axis=1).astype(jnp.bfloat16)

    grad_down = jnp.dot(hidden, routed, preferred_element_type=jnp.float32)
    dhidden = lax.dot_general(
        down_weight[0], routed, contract_last, preferred_element_type=jnp.float32
    )
    dgate = (dhidden * up_pre * sigmoid_gate * (1.0 + gate_pre * (1.0 - sigmoid_gate))).astype(
        jnp.bfloat16
    )
    dup = (dhidden * gate_pre * sigmoid_gate).astype(jnp.bfloat16)
    grad_gate = jnp.dot(dgate, rows_in, preferred_element_type=jnp.float32)
    grad_up = jnp.dot(dup, rows_in, preferred_element_type=jnp.float32)
    return (
        mixed_out,
        grad_gate.astype(jnp.bfloat16)[None],
        grad_up.astype(jnp.bfloat16)[None],
        grad_down.astype(jnp.bfloat16)[None],
    )


def solution(mesh):
    n_dp = mesh.shape["dp"]
    n_tensor = mesh.shape["tensor"]
    fine = Mesh(
        np.asarray(mesh.devices).reshape(n_dp, n_tensor // 2, 2), ("dp", "zh", "core")
    )
    tp = ("zh", "core")
    in_specs = (
        P("dp", None),
        P("dp", None),
        P("dp", None),
        P("dp", None),
        P("dp"),
        P(),
        P("dp", tp, None),
        P("dp", tp, None),
        P("dp", tp, None),
    )
    out_specs = (
        P("dp", tp),
        P("dp", tp, None),
        P("dp", tp, None),
        P("dp", tp, None),
    )
    return jax.shard_map(body, mesh=fine, in_specs=in_specs, out_specs=out_specs, check_vma=False)
```

```python
import functools

import jax
import jax.numpy as jnp
import numpy as np
from jax import lax
from jax.experimental import pallas as pl
from jax.experimental.pallas import tpu as pltpu
from jax.sharding import Mesh
from jax.sharding import PartitionSpec as P


MESH = pl.DeviceIdType.MESH


def _exchange_kernel(n, axis, x_ref, y_ref, send_sem, recv_sem, own_sem):
    me = lax.axis_index(axis)

    def copy_to(peer):
        return pltpu.make_async_remote_copy(
            src_ref=x_ref.at[peer],
            dst_ref=y_ref.at[me],
            send_sem=send_sem.at[peer],
            recv_sem=recv_sem.at[me],
            device_id={axis: peer},
            device_id_type=MESH,
        )

    def copy_from(source):
        return pltpu.make_async_remote_copy(
            src_ref=x_ref.at[source],
            dst_ref=y_ref.at[source],
            send_sem=send_sem.at[source],
            recv_sem=recv_sem.at[source],
            device_id={axis: source},
            device_id_type=MESH,
        )

    barrier = pltpu.get_barrier_semaphore()

    def greet(i, carry):
        pl.semaphore_signal(barrier, inc=1, device_id={axis: lax.rem(me + i, n)}, device_id_type=MESH)
        return carry

    lax.fori_loop(1, n, greet, 0)
    pl.semaphore_wait(barrier, n - 1)
    own = pltpu.make_async_copy(x_ref.at[me], y_ref.at[me], own_sem)
    own.start()

    def send(i, carry):
        copy_to(lax.rem(me + i, n)).start()
        return carry

    lax.fori_loop(1, n, send, 0)

    def finish(i, carry):
        copy_to(lax.rem(me + i, n)).wait_send()
        copy_from(lax.rem(me + n - i, n)).wait_recv()
        return carry

    lax.fori_loop(1, n, finish, 0)
    own.wait()


def _exchange(x, collective_id, axis="dp"):
    n = x.shape[0]
    return pl.pallas_call(
        functools.partial(_exchange_kernel, n, axis),
        out_shape=jax.ShapeDtypeStruct(x.shape, x.dtype),
        in_specs=[pl.BlockSpec(memory_space=pl.ANY)],
        out_specs=pl.BlockSpec(memory_space=pl.ANY),
        scratch_shapes=[
            pltpu.SemaphoreType.DMA((n,)),
            pltpu.SemaphoreType.DMA((n,)),
            pltpu.SemaphoreType.DMA(()),
        ],
        compiler_params=pltpu.CompilerParams(collective_id=collective_id, has_side_effects=True),
    )(x)


def _ring4_kernel(axis, x_ref, y_ref, relay_up, relay_down, send_sem, recv_sem, own_sem):
    me = lax.axis_index(axis)
    up, down, across = lax.rem(me + 1, 4), lax.rem(me + 3, 4), lax.rem(me + 2, 4)
    rows = x_ref.shape[1] // 2

    def remote(src, dst, slot, peer):
        return pltpu.make_async_remote_copy(
            src_ref=src,
            dst_ref=dst,
            send_sem=send_sem.at[slot],
            recv_sem=recv_sem.at[slot],
            device_id={axis: peer},
            device_id_type=MESH,
        )

    barrier = pltpu.get_barrier_semaphore()
    for peer in (up, down):
        pl.semaphore_signal(barrier, inc=1, device_id={axis: peer}, device_id_type=MESH)
    pl.semaphore_wait(barrier, 2)

    own = pltpu.make_async_copy(x_ref.at[me], y_ref.at[me], own_sem)
    own.start()
    to_up = remote(x_ref.at[up], y_ref.at[me], 0, up)
    to_down = remote(x_ref.at[down], y_ref.at[me], 1, down)
    lift = remote(x_ref.at[across, pl.ds(0, rows)], relay_up, 2, up)
    drop = remote(x_ref.at[across, pl.ds(rows, rows)], relay_down, 3, down)
    for copy in (to_up, to_down, lift, drop):
        copy.start()
    lift.wait_recv()
    pass_up = remote(relay_up, y_ref.at[down, pl.ds(0, rows)], 4, up)
    pass_up.start()
    drop.wait_recv()
    pass_down = remote(relay_down, y_ref.at[up, pl.ds(rows, rows)], 5, down)
    pass_down.start()
    for copy in (to_up, to_down, lift, drop, pass_up, pass_down):
        copy.wait_send()
    to_up.wait_recv()
    to_down.wait_recv()
    pass_up.wait_recv()
    pass_down.wait_recv()
    own.wait()


def _ring4_exchange(x, collective_id, axis):
    rows = x.shape[1] // 2
    return pl.pallas_call(
        functools.partial(_ring4_kernel, axis),
        out_shape=jax.ShapeDtypeStruct(x.shape, x.dtype),
        in_specs=[pl.BlockSpec(memory_space=pl.ANY)],
        out_specs=pl.BlockSpec(memory_space=pl.ANY),
        scratch_shapes=[
            pltpu.VMEM((rows,) + x.shape[2:], x.dtype),
            pltpu.VMEM((rows,) + x.shape[2:], x.dtype),
            pltpu.SemaphoreType.DMA((6,)),
            pltpu.SemaphoreType.DMA((6,)),
            pltpu.SemaphoreType.DMA(()),
        ],
        compiler_params=pltpu.CompilerParams(collective_id=collective_id, has_side_effects=True),
    )(x)


def _swap_pair(x):
    return lax.ppermute(x, "core", [(0, 1), (1, 0)])


def body(
    tokens,
    cotangent,
    expert_ids,
    route_weight,
    forget_mask,
    lengths,
    gate_weight,
    up_weight,
    down_weight,
):
    tok_rows = tokens.shape[0]
    features = tokens.shape[1]
    half = features // 2
    top_count = expert_ids.shape[1]
    owners = lax.axis_size("dp")
    groups = lax.axis_size("zh")
    block = features // (2 * groups)
    capacity = 5 * tok_rows * top_count // (4 * owners)
    core = lax.axis_index("core")
    is_first = core == 0

    seq_count = lengths.shape[0]
    seq_len = tok_rows * owners // seq_count
    token_index = lax.axis_index("dp") * tok_rows + jnp.arange(tok_rows, dtype=jnp.int32)
    seq_id = token_index // seq_len
    seq_pos = token_index - seq_id * seq_len
    in_seq = seq_id[:, None] == jnp.arange(seq_count, dtype=jnp.int32)[None, :]
    limits = jnp.sum(jnp.where(in_seq, lengths[None, :], 0), axis=1)
    is_valid = (seq_pos < limits).astype(jnp.int32)
    forget = is_valid * forget_mask
    retain = is_valid - forget

    shares = route_weight / jnp.sum(route_weight, axis=1, keepdims=True)
    share_flat = shares.reshape(-1)
    assigned = tok_rows * top_count
    flat_ids = expert_ids.reshape(-1)
    one_hot = (flat_ids[:, None] == jnp.arange(owners, dtype=jnp.int32)[None, :]).astype(jnp.int32)
    before = jnp.cumsum(one_hot, axis=0) - one_hot
    slot_id = jnp.sum(before * one_hot, axis=1)
    target = flat_ids * capacity + slot_id
    slots_all = owners * capacity
    hit = target[None, :] == jnp.arange(slots_all, dtype=jnp.int32)[:, None]
    hit_tok = jnp.any(hit.reshape(slots_all, tok_rows, top_count), axis=2)

    slot_share = jnp.sum(jnp.where(hit, share_flat[None, :], 0.0), axis=1)
    share_hi = lax.reduce_precision(slot_share, exponent_bits=8, mantissa_bits=7)
    rest = slot_share - share_hi
    share_mid = lax.reduce_precision(rest, exponent_bits=8, mantissa_bits=7)
    share_lo = rest - share_mid
    slot_forget = jnp.sum(jnp.where(hit_tok, forget[None, :], 0), axis=1).astype(jnp.float32)
    slot_retain = jnp.sum(jnp.where(hit_tok, retain[None, :], 0), axis=1).astype(jnp.float32)
    per_slot = jnp.stack([share_hi, share_mid, share_lo, slot_forget, slot_retain], axis=1)
    per_slot = per_slot.reshape(owners, capacity * 5)
    local_counts = jnp.stack([jnp.sum(forget), jnp.sum(retain)]).astype(jnp.float32)
    meta = jnp.concatenate(
        [
            per_slot,
            jnp.broadcast_to(local_counts[None, :], (owners, 2)),
            jnp.zeros((owners, features - capacity * 5 - 2), jnp.float32),
        ],
        axis=1,
    ).astype(jnp.bfloat16)
    my_tokens = lax.dynamic_slice_in_dim(tokens, core * half, half, axis=1)
    my_cotan = lax.dynamic_slice_in_dim(cotangent, core * half, half, axis=1)
    both = jnp.concatenate([my_tokens, my_cotan], axis=1)
    send = jnp.dot(hit_tok.astype(both.dtype), both, preferred_element_type=jnp.float32).astype(both.dtype)
    lanes = 128
    send = jnp.concatenate(
        [send.reshape(owners, capacity * features // lanes, lanes), meta.reshape(owners, features // lanes, lanes)],
        axis=1,
    )
    recv = _exchange(send, 0)
    got = recv[:, : capacity * features // lanes, :].reshape(slots_all, features)
    got_meta = recv[:, capacity * features // lanes :, :].reshape(owners, features).astype(jnp.float32)
    other = _swap_pair(got)
    lower = jnp.where(is_first, got, other)
    upper = jnp.where(is_first, other, got)
    rows_in = jnp.concatenate([lower[:, :half], upper[:, :half]], axis=1)
    cot_in = jnp.concatenate([lower[:, half:], upper[:, half:]], axis=1)

    n_forget = jnp.sum(got_meta[:, capacity * 5])
    n_retain = jnp.sum(got_meta[:, capacity * 5 + 1])
    slot_meta = got_meta[:, : capacity * 5].reshape(slots_all, 5)
    got_share = (slot_meta[:, 0] + slot_meta[:, 1]) + slot_meta[:, 2]
    coefficient = float(top_count * tok_rows) * (
        slot_meta[:, 4] / n_retain - slot_meta[:, 3] / n_forget
    )
    routed = ((coefficient * got_share)[:, None] * cot_in.astype(jnp.float32)).astype(jnp.bfloat16)

    contract_last = (((1,), (1,)), ((), ()))
    contract_first = (((0,), (0,)), ((), ()))
    gate_pre = lax.dot_general(
        gate_weight[0], rows_in, contract_last, preferred_element_type=jnp.float32
    )
    up_pre = lax.dot_general(
        up_weight[0], rows_in, contract_last, preferred_element_type=jnp.float32
    )
    sigmoid_gate = jax.nn.sigmoid(gate_pre)
    hidden = (gate_pre * sigmoid_gate * up_pre).astype(jnp.bfloat16)
    partial_out = lax.dot_general(
        hidden, down_weight[0], contract_first, preferred_element_type=jnp.float32
    ).astype(jnp.bfloat16)
    pieces = partial_out.reshape(slots_all, groups, 2, block)
    keep = jnp.where(is_first, pieces[:, :, 0, :], pieces[:, :, 1, :])
    give = jnp.where(is_first, pieces[:, :, 1, :], pieces[:, :, 0, :])
    pair_sum = (keep.astype(jnp.float32) + _swap_pair(give).astype(jnp.float32)).astype(jnp.bfloat16)
    by_group = _ring4_exchange(jnp.transpose(pair_sum, (1, 0, 2)), 2, "zh")
    slice_sum = jnp.sum(by_group.astype(jnp.float32), axis=0).astype(jnp.bfloat16)
    returned = _exchange(slice_sum.reshape(owners, capacity * block // lanes, lanes), 1)
    picked = jnp.dot(
        hit.T.astype(returned.dtype),
        returned.reshape(slots_all, block),
        preferred_element_type=jnp.float32,
    ) * share_flat[:, None]
    mixed_out = jnp.sum(picked.reshape(tok_rows, top_count, block), axis=1).astype(jnp.bfloat16)

    grad_down = jnp.dot(hidden, routed, preferred_element_type=jnp.float32)
    dhidden = lax.dot_general(
        down_weight[0], routed, contract_last, preferred_element_type=jnp.float32
    )
    dgate = (dhidden * up_pre * sigmoid_gate * (1.0 + gate_pre * (1.0 - sigmoid_gate))).astype(
        jnp.bfloat16
    )
    dup = (dhidden * gate_pre * sigmoid_gate).astype(jnp.bfloat16)
    grad_gate = jnp.dot(dgate, rows_in, preferred_element_type=jnp.float32)
    grad_up = jnp.dot(dup, rows_in, preferred_element_type=jnp.float32)
    return (
        mixed_out,
        grad_gate.astype(jnp.bfloat16)[None],
        grad_up.astype(jnp.bfloat16)[None],
        grad_down.astype(jnp.bfloat16)[None],
    )


def solution(mesh):
    n_dp = mesh.shape["dp"]
    n_tensor = mesh.shape["tensor"]
    fine = Mesh(
        np.asarray(mesh.devices).reshape(n_dp, n_tensor // 2, 2), ("dp", "zh", "core")
    )
    tp = ("zh", "core")
    in_specs = (
        P("dp", None),
        P("dp", None),
        P("dp", None),
        P("dp", None),
        P("dp"),
        P(),
        P("dp", tp, None),
        P("dp", tp, None),
        P("dp", tp, None),
    )
    out_specs = (
        P("dp", tp),
        P("dp", tp, None),
        P("dp", tp, None),
        P("dp", tp, None),
    )
    return jax.shard_map(body, mesh=fine, in_specs=in_specs, out_specs=out_specs, check_vma=False)
```

```python
import functools

import jax
import jax.numpy as jnp
import numpy as np
from jax import lax
from jax.experimental import pallas as pl
from jax.experimental.pallas import tpu as pltpu
from jax.sharding import Mesh
from jax.sharding import PartitionSpec as P


MESH = pl.DeviceIdType.MESH


def _exchange_kernel(n, axis, x_ref, y_ref, send_sem, recv_sem, own_sem):
    me = lax.axis_index(axis)

    def copy_to(peer):
        return pltpu.make_async_remote_copy(
            src_ref=x_ref.at[peer],
            dst_ref=y_ref.at[me],
            send_sem=send_sem.at[peer],
            recv_sem=recv_sem.at[me],
            device_id={axis: peer},
            device_id_type=MESH,
        )

    def copy_from(source):
        return pltpu.make_async_remote_copy(
            src_ref=x_ref.at[source],
            dst_ref=y_ref.at[source],
            send_sem=send_sem.at[source],
            recv_sem=recv_sem.at[source],
            device_id={axis: source},
            device_id_type=MESH,
        )

    barrier = pltpu.get_barrier_semaphore()

    def greet(i, carry):
        pl.semaphore_signal(barrier, inc=1, device_id={axis: lax.rem(me + i, n)}, device_id_type=MESH)
        return carry

    lax.fori_loop(1, n, greet, 0)
    pl.semaphore_wait(barrier, n - 1)
    own = pltpu.make_async_copy(x_ref.at[me], y_ref.at[me], own_sem)
    own.start()

    def send(i, carry):
        copy_to(lax.rem(me + i, n)).start()
        return carry

    lax.fori_loop(1, n, send, 0)

    def finish(i, carry):
        copy_to(lax.rem(me + i, n)).wait_send()
        copy_from(lax.rem(me + n - i, n)).wait_recv()
        return carry

    lax.fori_loop(1, n, finish, 0)
    own.wait()


def _exchange(x, collective_id, axis="dp"):
    n = x.shape[0]
    return pl.pallas_call(
        functools.partial(_exchange_kernel, n, axis),
        out_shape=jax.ShapeDtypeStruct(x.shape, x.dtype),
        in_specs=[pl.BlockSpec(memory_space=pl.ANY)],
        out_specs=pl.BlockSpec(memory_space=pl.ANY),
        scratch_shapes=[
            pltpu.SemaphoreType.DMA((n,)),
            pltpu.SemaphoreType.DMA((n,)),
            pltpu.SemaphoreType.DMA(()),
        ],
        compiler_params=pltpu.CompilerParams(collective_id=collective_id, has_side_effects=True),
    )(x)


def _ring4_kernel(axis, x_ref, y_ref, relay_up, relay_down, send_sem, recv_sem, own_sem):
    me = lax.axis_index(axis)
    up, down, across = lax.rem(me + 1, 4), lax.rem(me + 3, 4), lax.rem(me + 2, 4)
    rows = x_ref.shape[1] // 2

    def remote(src, dst, slot, peer):
        return pltpu.make_async_remote_copy(
            src_ref=src,
            dst_ref=dst,
            send_sem=send_sem.at[slot],
            recv_sem=recv_sem.at[slot],
            device_id={axis: peer},
            device_id_type=MESH,
        )

    barrier = pltpu.get_barrier_semaphore()
    for peer in (up, down):
        pl.semaphore_signal(barrier, inc=1, device_id={axis: peer}, device_id_type=MESH)
    pl.semaphore_wait(barrier, 2)

    own = pltpu.make_async_copy(x_ref.at[me], y_ref.at[me], own_sem)
    own.start()
    to_up = remote(x_ref.at[up], y_ref.at[me], 0, up)
    to_down = remote(x_ref.at[down], y_ref.at[me], 1, down)
    lift = remote(x_ref.at[across, pl.ds(0, rows)], relay_up, 2, up)
    drop = remote(x_ref.at[across, pl.ds(rows, rows)], relay_down, 3, down)
    for copy in (to_up, to_down, lift, drop):
        copy.start()
    lift.wait_recv()
    pass_up = remote(relay_up, y_ref.at[down, pl.ds(0, rows)], 4, up)
    pass_up.start()
    drop.wait_recv()
    pass_down = remote(relay_down, y_ref.at[up, pl.ds(rows, rows)], 5, down)
    pass_down.start()
    for copy in (to_up, to_down, lift, drop, pass_up, pass_down):
        copy.wait_send()
    to_up.wait_recv()
    to_down.wait_recv()
    pass_up.wait_recv()
    pass_down.wait_recv()
    own.wait()


def _ring4_exchange(x, collective_id, axis):
    rows = x.shape[1] // 2
    return pl.pallas_call(
        functools.partial(_ring4_kernel, axis),
        out_shape=jax.ShapeDtypeStruct(x.shape, x.dtype),
        in_specs=[pl.BlockSpec(memory_space=pl.ANY)],
        out_specs=pl.BlockSpec(memory_space=pl.ANY),
        scratch_shapes=[
            pltpu.VMEM((rows,) + x.shape[2:], x.dtype),
            pltpu.VMEM((rows,) + x.shape[2:], x.dtype),
            pltpu.SemaphoreType.DMA((6,)),
            pltpu.SemaphoreType.DMA((6,)),
            pltpu.SemaphoreType.DMA(()),
        ],
        compiler_params=pltpu.CompilerParams(collective_id=collective_id, has_side_effects=True),
    )(x)


def _swap_pair(x):
    return lax.ppermute(x, "core", [(0, 1), (1, 0)])


def body(
    tokens,
    cotangent,
    expert_ids,
    route_weight,
    forget_mask,
    lengths,
    gate_weight,
    up_weight,
    down_weight,
):
    tok_rows = tokens.shape[0]
    features = tokens.shape[1]
    half = features // 2
    top_count = expert_ids.shape[1]
    owners = lax.axis_size("dp")
    groups = lax.axis_size("zh")
    block = features // (2 * groups)
    capacity = 5 * tok_rows * top_count // (4 * owners)
    core = lax.axis_index("core")
    is_first = core == 0

    seq_count = lengths.shape[0]
    seq_len = tok_rows * owners // seq_count
    token_index = lax.axis_index("dp") * tok_rows + jnp.arange(tok_rows, dtype=jnp.int32)
    seq_id = token_index // seq_len
    seq_pos = token_index - seq_id * seq_len
    in_seq = seq_id[:, None] == jnp.arange(seq_count, dtype=jnp.int32)[None, :]
    limits = jnp.sum(jnp.where(in_seq, lengths[None, :], 0), axis=1)
    is_valid = (seq_pos < limits).astype(jnp.int32)
    forget = is_valid * forget_mask
    retain = is_valid - forget

    shares = route_weight / jnp.sum(route_weight, axis=1, keepdims=True)
    share_flat = shares.reshape(-1)
    assigned = tok_rows * top_count
    flat_ids = expert_ids.reshape(-1)
    one_hot = (flat_ids[:, None] == jnp.arange(owners, dtype=jnp.int32)[None, :]).astype(jnp.int32)
    before = jnp.cumsum(one_hot, axis=0) - one_hot
    slot_id = jnp.sum(before * one_hot, axis=1)
    target = flat_ids * capacity + slot_id
    slots_all = owners * capacity
    hit = target[None, :] == jnp.arange(slots_all, dtype=jnp.int32)[:, None]
    hit_tok = jnp.any(hit.reshape(slots_all, tok_rows, top_count), axis=2)

    slot_share = jnp.sum(jnp.where(hit, share_flat[None, :], 0.0), axis=1)
    share_hi = lax.reduce_precision(slot_share, exponent_bits=8, mantissa_bits=7)
    rest = slot_share - share_hi
    share_mid = lax.reduce_precision(rest, exponent_bits=8, mantissa_bits=7)
    share_lo = rest - share_mid
    slot_forget = jnp.sum(jnp.where(hit_tok, forget[None, :], 0), axis=1).astype(jnp.float32)
    slot_retain = jnp.sum(jnp.where(hit_tok, retain[None, :], 0), axis=1).astype(jnp.float32)
    per_slot = jnp.stack([share_hi, share_mid, share_lo, slot_forget, slot_retain], axis=1)
    per_slot = per_slot.reshape(owners, capacity * 5)
    local_counts = jnp.stack([jnp.sum(forget), jnp.sum(retain)]).astype(jnp.float32)
    meta = jnp.concatenate(
        [
            per_slot,
            jnp.broadcast_to(local_counts[None, :], (owners, 2)),
            jnp.zeros((owners, features - capacity * 5 - 2), jnp.float32),
        ],
        axis=1,
    ).astype(jnp.bfloat16)
    my_tokens = lax.dynamic_slice_in_dim(tokens, core * half, half, axis=1)
    my_cotan = lax.dynamic_slice_in_dim(cotangent, core * half, half, axis=1)
    both = jnp.concatenate([my_tokens, my_cotan], axis=1)
    send = jnp.dot(hit_tok.astype(both.dtype), both, preferred_element_type=jnp.float32).astype(both.dtype)
    lanes = 128
    send = jnp.concatenate(
        [send.reshape(owners, capacity * features // lanes, lanes), meta.reshape(owners, features // lanes, lanes)],
        axis=1,
    )
    recv = _exchange(send, 0)
    got = recv[:, : capacity * features // lanes, :].reshape(slots_all, features)
    got_meta = recv[:, capacity * features // lanes :, :].reshape(owners, features).astype(jnp.float32)
    other = _swap_pair(got)
    lower = jnp.where(is_first, got, other)
    upper = jnp.where(is_first, other, got)
    rows_in = jnp.concatenate([lower[:, :half], upper[:, :half]], axis=1)
    cot_in = jnp.concatenate([lower[:, half:], upper[:, half:]], axis=1)

    n_forget = jnp.sum(got_meta[:, capacity * 5])
    n_retain = jnp.sum(got_meta[:, capacity * 5 + 1])
    slot_meta = got_meta[:, : capacity * 5].reshape(slots_all, 5)
    got_share = (slot_meta[:, 0] + slot_meta[:, 1]) + slot_meta[:, 2]
    coefficient = float(top_count * tok_rows) * (
        slot_meta[:, 4] / n_retain - slot_meta[:, 3] / n_forget
    )
    routed = ((coefficient * got_share)[:, None] * cot_in.astype(jnp.float32)).astype(jnp.bfloat16)

    contract_last = (((1,), (1,)), ((), ()))
    contract_first = (((0,), (0,)), ((), ()))
    gate_pre = lax.dot_general(
        gate_weight[0], rows_in, contract_last, preferred_element_type=jnp.float32
    )
    up_pre = lax.dot_general(
        up_weight[0], rows_in, contract_last, preferred_element_type=jnp.float32
    )
    sigmoid_gate = jax.nn.sigmoid(gate_pre)
    hidden = (gate_pre * sigmoid_gate * up_pre).astype(jnp.bfloat16)
    down_groups = down_weight[0].reshape(down_weight.shape[1], groups, 2, block)
    keep_w = jnp.where(is_first, down_groups[:, :, 0, :], down_groups[:, :, 1, :])
    give_w = jnp.where(is_first, down_groups[:, :, 1, :], down_groups[:, :, 0, :])
    keep = jnp.einsum("hr,hzb->zrb", hidden, keep_w, preferred_element_type=jnp.float32).astype(jnp.bfloat16)
    give = jnp.einsum("hr,hzb->zrb", hidden, give_w, preferred_element_type=jnp.float32).astype(jnp.bfloat16)
    pair_sum = (keep.astype(jnp.float32) + _swap_pair(give).astype(jnp.float32)).astype(jnp.bfloat16)
    by_group = _ring4_exchange(pair_sum, 2, "zh")
    slice_sum = jnp.sum(by_group.astype(jnp.float32), axis=0).astype(jnp.bfloat16)
    returned = _exchange(slice_sum.reshape(owners, capacity * block // lanes, lanes), 1)
    picked = jnp.dot(
        hit.T.astype(returned.dtype),
        returned.reshape(slots_all, block),
        preferred_element_type=jnp.float32,
    ) * share_flat[:, None]
    mixed_out = jnp.sum(picked.reshape(tok_rows, top_count, block), axis=1).astype(jnp.bfloat16)

    grad_down = jnp.dot(hidden, routed, preferred_element_type=jnp.float32)
    dhidden = lax.dot_general(
        down_weight[0], routed, contract_last, preferred_element_type=jnp.float32
    )
    dgate = (dhidden * up_pre * sigmoid_gate * (1.0 + gate_pre * (1.0 - sigmoid_gate))).astype(
        jnp.bfloat16
    )
    dup = (dhidden * gate_pre * sigmoid_gate).astype(jnp.bfloat16)
    grad_gate = jnp.dot(dgate, rows_in, preferred_element_type=jnp.float32)
    grad_up = jnp.dot(dup, rows_in, preferred_element_type=jnp.float32)
    return (
        mixed_out,
        grad_gate.astype(jnp.bfloat16)[None],
        grad_up.astype(jnp.bfloat16)[None],
        grad_down.astype(jnp.bfloat16)[None],
    )


def solution(mesh):
    n_dp = mesh.shape["dp"]
    n_tensor = mesh.shape["tensor"]
    fine = Mesh(
        np.asarray(mesh.devices).reshape(n_dp, n_tensor // 2, 2), ("dp", "zh", "core")
    )
    tp = ("zh", "core")
    in_specs = (
        P("dp", None),
        P("dp", None),
        P("dp", None),
        P("dp", None),
        P("dp"),
        P(),
        P("dp", tp, None),
        P("dp", tp, None),
        P("dp", tp, None),
    )
    out_specs = (
        P("dp", tp),
        P("dp", tp, None),
        P("dp", tp, None),
        P("dp", tp, None),
    )
    return jax.shard_map(body, mesh=fine, in_specs=in_specs, out_specs=out_specs, check_vma=False)
```

```python
import functools

import jax
import jax.numpy as jnp
import numpy as np
from jax import lax
from jax.experimental import pallas as pl
from jax.experimental.pallas import tpu as pltpu
from jax.sharding import Mesh
from jax.sharding import PartitionSpec as P


MESH = pl.DeviceIdType.MESH


def _exchange_kernel(n, axis, x_ref, y_ref, send_sem, recv_sem, own_sem):
    me = lax.axis_index(axis)

    def copy_to(peer):
        return pltpu.make_async_remote_copy(
            src_ref=x_ref.at[peer],
            dst_ref=y_ref.at[me],
            send_sem=send_sem.at[peer],
            recv_sem=recv_sem.at[me],
            device_id={axis: peer},
            device_id_type=MESH,
        )

    def copy_from(source):
        return pltpu.make_async_remote_copy(
            src_ref=x_ref.at[source],
            dst_ref=y_ref.at[source],
            send_sem=send_sem.at[source],
            recv_sem=recv_sem.at[source],
            device_id={axis: source},
            device_id_type=MESH,
        )

    barrier = pltpu.get_barrier_semaphore()

    def greet(i, carry):
        pl.semaphore_signal(barrier, inc=1, device_id={axis: lax.rem(me + i, n)}, device_id_type=MESH)
        return carry

    lax.fori_loop(1, n, greet, 0)
    pl.semaphore_wait(barrier, n - 1)
    own = pltpu.make_async_copy(x_ref.at[me], y_ref.at[me], own_sem)
    own.start()

    def send(i, carry):
        copy_to(lax.rem(me + i, n)).start()
        return carry

    lax.fori_loop(1, n, send, 0)

    def finish(i, carry):
        copy_to(lax.rem(me + i, n)).wait_send()
        copy_from(lax.rem(me + n - i, n)).wait_recv()
        return carry

    lax.fori_loop(1, n, finish, 0)
    own.wait()


def _exchange(x, collective_id, axis="dp"):
    n = x.shape[0]
    return pl.pallas_call(
        functools.partial(_exchange_kernel, n, axis),
        out_shape=jax.ShapeDtypeStruct(x.shape, x.dtype),
        in_specs=[pl.BlockSpec(memory_space=pl.ANY)],
        out_specs=pl.BlockSpec(memory_space=pl.ANY),
        scratch_shapes=[
            pltpu.SemaphoreType.DMA((n,)),
            pltpu.SemaphoreType.DMA((n,)),
            pltpu.SemaphoreType.DMA(()),
        ],
        compiler_params=pltpu.CompilerParams(collective_id=collective_id, has_side_effects=True),
    )(x)


def _ring4_kernel(axis, x_ref, y_ref, relay_up, relay_down, send_sem, recv_sem, own_sem):
    me = lax.axis_index(axis)
    up, down, across = lax.rem(me + 1, 4), lax.rem(me + 3, 4), lax.rem(me + 2, 4)
    rows = x_ref.shape[1] // 2

    def remote(src, dst, slot, peer):
        return pltpu.make_async_remote_copy(
            src_ref=src,
            dst_ref=dst,
            send_sem=send_sem.at[slot],
            recv_sem=recv_sem.at[slot],
            device_id={axis: peer},
            device_id_type=MESH,
        )

    barrier = pltpu.get_barrier_semaphore()
    for peer in (up, down):
        pl.semaphore_signal(barrier, inc=1, device_id={axis: peer}, device_id_type=MESH)
    pl.semaphore_wait(barrier, 2)

    own = pltpu.make_async_copy(x_ref.at[me], y_ref.at[me], own_sem)
    own.start()
    to_up = remote(x_ref.at[up], y_ref.at[me], 0, up)
    to_down = remote(x_ref.at[down], y_ref.at[me], 1, down)
    lift = remote(x_ref.at[across, pl.ds(0, rows)], relay_up, 2, up)
    drop = remote(x_ref.at[across, pl.ds(rows, rows)], relay_down, 3, down)
    for copy in (to_up, to_down, lift, drop):
        copy.start()
    lift.wait_recv()
    pass_up = remote(relay_up, y_ref.at[down, pl.ds(0, rows)], 4, up)
    pass_up.start()
    drop.wait_recv()
    pass_down = remote(relay_down, y_ref.at[up, pl.ds(rows, rows)], 5, down)
    pass_down.start()
    for copy in (to_up, to_down, lift, drop, pass_up, pass_down):
        copy.wait_send()
    to_up.wait_recv()
    to_down.wait_recv()
    pass_up.wait_recv()
    pass_down.wait_recv()
    own.wait()


def _ring4_exchange(x, collective_id, axis):
    rows = x.shape[1] // 2
    return pl.pallas_call(
        functools.partial(_ring4_kernel, axis),
        out_shape=jax.ShapeDtypeStruct(x.shape, x.dtype),
        in_specs=[pl.BlockSpec(memory_space=pl.ANY)],
        out_specs=pl.BlockSpec(memory_space=pl.ANY),
        scratch_shapes=[
            pltpu.VMEM((rows,) + x.shape[2:], x.dtype),
            pltpu.VMEM((rows,) + x.shape[2:], x.dtype),
            pltpu.SemaphoreType.DMA((6,)),
            pltpu.SemaphoreType.DMA((6,)),
            pltpu.SemaphoreType.DMA(()),
        ],
        compiler_params=pltpu.CompilerParams(collective_id=collective_id, has_side_effects=True),
    )(x)


def _both_kernel(n, a_ref, b_ref, ya_ref, yb_ref, a_send, a_recv, a_own, relay_up, relay_down, b_send, b_recv, b_own):
    me = lax.axis_index("dp")
    at = lax.axis_index("zh")
    up, down, across = lax.rem(at + 1, 4), lax.rem(at + 3, 4), lax.rem(at + 2, 4)
    rows = b_ref.shape[1] // 2

    def dp_copy(src, dst, slot_send, slot_recv, peer):
        return pltpu.make_async_remote_copy(
            src_ref=src,
            dst_ref=dst,
            send_sem=a_send.at[slot_send],
            recv_sem=a_recv.at[slot_recv],
            device_id={"dp": peer},
            device_id_type=MESH,
        )

    def zh_copy(src, dst, slot, peer):
        return pltpu.make_async_remote_copy(
            src_ref=src,
            dst_ref=dst,
            send_sem=b_send.at[slot],
            recv_sem=b_recv.at[slot],
            device_id={"zh": peer},
            device_id_type=MESH,
        )

    barrier = pltpu.get_barrier_semaphore()

    def greet(i, carry):
        pl.semaphore_signal(barrier, inc=1, device_id={"dp": lax.rem(me + i, n)}, device_id_type=MESH)
        return carry

    lax.fori_loop(1, n, greet, 0)
    for peer in (up, down):
        pl.semaphore_signal(barrier, inc=1, device_id={"zh": peer}, device_id_type=MESH)
    pl.semaphore_wait(barrier, n + 1)

    own_a = pltpu.make_async_copy(a_ref.at[me], ya_ref.at[me], a_own)
    own_a.start()
    own_b = pltpu.make_async_copy(b_ref.at[at], yb_ref.at[at], b_own)
    own_b.start()
    to_up = zh_copy(b_ref.at[up], yb_ref.at[at], 0, up)
    to_down = zh_copy(b_ref.at[down], yb_ref.at[at], 1, down)
    lift = zh_copy(b_ref.at[across, pl.ds(0, rows)], relay_up, 2, up)
    drop = zh_copy(b_ref.at[across, pl.ds(rows, rows)], relay_down, 3, down)
    for copy in (to_up, to_down, lift, drop):
        copy.start()

    def send(i, carry):
        peer = lax.rem(me + i, n)
        dp_copy(a_ref.at[peer], ya_ref.at[me], peer, me, peer).start()
        return carry

    lax.fori_loop(1, n, send, 0)
    lift.wait_recv()
    pass_up = zh_copy(relay_up, yb_ref.at[down, pl.ds(0, rows)], 4, up)
    pass_up.start()
    drop.wait_recv()
    pass_down = zh_copy(relay_down, yb_ref.at[up, pl.ds(rows, rows)], 5, down)
    pass_down.start()

    def finish(i, carry):
        peer = lax.rem(me + i, n)
        source = lax.rem(me + n - i, n)
        dp_copy(a_ref.at[peer], ya_ref.at[me], peer, me, peer).wait_send()
        dp_copy(a_ref.at[source], ya_ref.at[source], source, source, source).wait_recv()
        return carry

    lax.fori_loop(1, n, finish, 0)
    for copy in (to_up, to_down, lift, drop, pass_up, pass_down):
        copy.wait_send()
    for copy in (to_up, to_down, pass_up, pass_down):
        copy.wait_recv()
    own_a.wait()
    own_b.wait()


def _exchange_both(a, b, collective_id):
    n = a.shape[0]
    rows = b.shape[1] // 2
    return pl.pallas_call(
        functools.partial(_both_kernel, n),
        out_shape=(jax.ShapeDtypeStruct(a.shape, a.dtype), jax.ShapeDtypeStruct(b.shape, b.dtype)),
        in_specs=[pl.BlockSpec(memory_space=pl.ANY)] * 2,
        out_specs=(pl.BlockSpec(memory_space=pl.ANY), pl.BlockSpec(memory_space=pl.ANY)),
        scratch_shapes=[
            pltpu.SemaphoreType.DMA((n,)),
            pltpu.SemaphoreType.DMA((n,)),
            pltpu.SemaphoreType.DMA(()),
            pltpu.VMEM((rows,) + b.shape[2:], b.dtype),
            pltpu.VMEM((rows,) + b.shape[2:], b.dtype),
            pltpu.SemaphoreType.DMA((6,)),
            pltpu.SemaphoreType.DMA((6,)),
            pltpu.SemaphoreType.DMA(()),
        ],
        compiler_params=pltpu.CompilerParams(collective_id=collective_id, has_side_effects=True),
    )(a, b)


def _swap_pair(x):
    return lax.ppermute(x, "core", [(0, 1), (1, 0)])


def body(
    tokens,
    cotangent,
    expert_ids,
    route_weight,
    forget_mask,
    lengths,
    gate_weight,
    up_weight,
    down_weight,
):
    tok_rows = tokens.shape[0]
    features = tokens.shape[1]
    half = features // 2
    top_count = expert_ids.shape[1]
    owners = lax.axis_size("dp")
    groups = lax.axis_size("zh")
    block = features // (2 * groups)
    capacity = 5 * tok_rows * top_count // (4 * owners)
    core = lax.axis_index("core")
    is_first = core == 0

    seq_count = lengths.shape[0]
    seq_len = tok_rows * owners // seq_count
    token_index = lax.axis_index("dp") * tok_rows + jnp.arange(tok_rows, dtype=jnp.int32)
    seq_id = token_index // seq_len
    seq_pos = token_index - seq_id * seq_len
    in_seq = seq_id[:, None] == jnp.arange(seq_count, dtype=jnp.int32)[None, :]
    limits = jnp.sum(jnp.where(in_seq, lengths[None, :], 0), axis=1)
    is_valid = (seq_pos < limits).astype(jnp.int32)
    forget = is_valid * forget_mask
    retain = is_valid - forget

    shares = route_weight / jnp.sum(route_weight, axis=1, keepdims=True)
    share_flat = shares.reshape(-1)
    assigned = tok_rows * top_count
    flat_ids = expert_ids.reshape(-1)
    one_hot = (flat_ids[:, None] == jnp.arange(owners, dtype=jnp.int32)[None, :]).astype(jnp.int32)
    before = jnp.cumsum(one_hot, axis=0) - one_hot
    slot_id = jnp.sum(before * one_hot, axis=1)
    target = flat_ids * capacity + slot_id
    slots_all = owners * capacity
    hit = target[None, :] == jnp.arange(slots_all, dtype=jnp.int32)[:, None]
    hit_tok = jnp.any(hit.reshape(slots_all, tok_rows, top_count), axis=2)

    slot_share = jnp.sum(jnp.where(hit, share_flat[None, :], 0.0), axis=1)
    share_hi = lax.reduce_precision(slot_share, exponent_bits=8, mantissa_bits=7)
    rest = slot_share - share_hi
    share_mid = lax.reduce_precision(rest, exponent_bits=8, mantissa_bits=7)
    share_lo = rest - share_mid
    slot_forget = jnp.sum(jnp.where(hit_tok, forget[None, :], 0), axis=1).astype(jnp.float32)
    slot_retain = jnp.sum(jnp.where(hit_tok, retain[None, :], 0), axis=1).astype(jnp.float32)
    per_slot = jnp.stack([share_hi, share_mid, share_lo, slot_forget, slot_retain], axis=1)
    per_slot = per_slot.reshape(owners, capacity * 5)
    local_counts = jnp.stack([jnp.sum(forget), jnp.sum(retain)]).astype(jnp.float32)
    meta = jnp.concatenate(
        [
            per_slot,
            jnp.broadcast_to(local_counts[None, :], (owners, 2)),
            jnp.zeros((owners, features - capacity * 5 - 2), jnp.float32),
        ],
        axis=1,
    ).astype(jnp.bfloat16)
    my_tokens = lax.dynamic_slice_in_dim(tokens, core * half, half, axis=1)
    my_cotan = lax.dynamic_slice_in_dim(cotangent, core * half, half, axis=1)
    lanes = 128
    pick = hit_tok.astype(tokens.dtype)
    send_tok = jnp.dot(pick, my_tokens, preferred_element_type=jnp.float32).astype(tokens.dtype)
    send_cot = jnp.dot(pick, my_cotan, preferred_element_type=jnp.float32).astype(tokens.dtype)
    send = jnp.concatenate(
        [send_tok.reshape(owners, capacity * half // lanes, lanes), meta.reshape(owners, features // lanes, lanes)],
        axis=1,
    )
    recv = _exchange(send, 0)
    got = recv[:, : capacity * half // lanes, :].reshape(slots_all, half)
    got_meta = recv[:, capacity * half // lanes :, :].reshape(owners, features).astype(jnp.float32)
    other = _swap_pair(got)
    rows_in = jnp.concatenate(
        [jnp.where(is_first, got, other), jnp.where(is_first, other, got)], axis=1
    )

    contract_last = (((1,), (1,)), ((), ()))
    contract_first = (((0,), (0,)), ((), ()))
    gate_pre = lax.dot_general(
        gate_weight[0], rows_in, contract_last, preferred_element_type=jnp.float32
    )
    up_pre = lax.dot_general(
        up_weight[0], rows_in, contract_last, preferred_element_type=jnp.float32
    )
    sigmoid_gate = jax.nn.sigmoid(gate_pre)
    hidden = (gate_pre * sigmoid_gate * up_pre).astype(jnp.bfloat16)
    down_groups = down_weight[0].reshape(down_weight.shape[1], groups, 2, block)
    keep_w = jnp.where(is_first, down_groups[:, :, 0, :], down_groups[:, :, 1, :])
    give_w = jnp.where(is_first, down_groups[:, :, 1, :], down_groups[:, :, 0, :])
    keep = jnp.einsum("hr,hzb->zrb", hidden, keep_w, preferred_element_type=jnp.float32).astype(jnp.bfloat16)
    give = jnp.einsum("hr,hzb->zrb", hidden, give_w, preferred_element_type=jnp.float32).astype(jnp.bfloat16)
    pair_sum = (keep.astype(jnp.float32) + _swap_pair(give).astype(jnp.float32)).astype(jnp.bfloat16)
    got_cot, by_group = _exchange_both(send_cot.reshape(owners, capacity * half // lanes, lanes), pair_sum, 3)
    got_cot = got_cot.reshape(slots_all, half)
    other_cot = _swap_pair(got_cot)
    cot_in = jnp.concatenate(
        [jnp.where(is_first, got_cot, other_cot), jnp.where(is_first, other_cot, got_cot)], axis=1
    )
    n_forget = jnp.sum(got_meta[:, capacity * 5])
    n_retain = jnp.sum(got_meta[:, capacity * 5 + 1])
    slot_meta = got_meta[:, : capacity * 5].reshape(slots_all, 5)
    got_share = (slot_meta[:, 0] + slot_meta[:, 1]) + slot_meta[:, 2]
    coefficient = float(top_count * tok_rows) * (
        slot_meta[:, 4] / n_retain - slot_meta[:, 3] / n_forget
    )
    routed = ((coefficient * got_share)[:, None] * cot_in.astype(jnp.float32)).astype(jnp.bfloat16)
    slice_sum = jnp.sum(by_group.astype(jnp.float32), axis=0).astype(jnp.bfloat16)
    returned = _exchange(slice_sum.reshape(owners, capacity * block // lanes, lanes), 1)
    picked = jnp.dot(
        hit.T.astype(returned.dtype),
        returned.reshape(slots_all, block),
        preferred_element_type=jnp.float32,
    ) * share_flat[:, None]
    mixed_out = jnp.sum(picked.reshape(tok_rows, top_count, block), axis=1).astype(jnp.bfloat16)

    grad_down = jnp.dot(hidden, routed, preferred_element_type=jnp.float32)
    dhidden = lax.dot_general(
        down_weight[0], routed, contract_last, preferred_element_type=jnp.float32
    )
    dgate = (dhidden * up_pre * sigmoid_gate * (1.0 + gate_pre * (1.0 - sigmoid_gate))).astype(
        jnp.bfloat16
    )
    dup = (dhidden * gate_pre * sigmoid_gate).astype(jnp.bfloat16)
    grad_gate = jnp.dot(dgate, rows_in, preferred_element_type=jnp.float32)
    grad_up = jnp.dot(dup, rows_in, preferred_element_type=jnp.float32)
    return (
        mixed_out,
        grad_gate.astype(jnp.bfloat16)[None],
        grad_up.astype(jnp.bfloat16)[None],
        grad_down.astype(jnp.bfloat16)[None],
    )


def solution(mesh):
    n_dp = mesh.shape["dp"]
    n_tensor = mesh.shape["tensor"]
    fine = Mesh(
        np.asarray(mesh.devices).reshape(n_dp, n_tensor // 2, 2), ("dp", "zh", "core")
    )
    tp = ("zh", "core")
    in_specs = (
        P("dp", None),
        P("dp", None),
        P("dp", None),
        P("dp", None),
        P("dp"),
        P(),
        P("dp", tp, None),
        P("dp", tp, None),
        P("dp", tp, None),
    )
    out_specs = (
        P("dp", tp),
        P("dp", tp, None),
        P("dp", tp, None),
        P("dp", tp, None),
    )
    return jax.shard_map(body, mesh=fine, in_specs=in_specs, out_specs=out_specs, check_vma=False)
```

```python
import functools

import jax
import jax.numpy as jnp
import numpy as np
from jax import lax
from jax.experimental import pallas as pl
from jax.experimental.pallas import tpu as pltpu
from jax.sharding import Mesh
from jax.sharding import PartitionSpec as P


MESH = pl.DeviceIdType.MESH


def _exchange_kernel(n, axis, x_ref, y_ref, send_sem, recv_sem, own_sem):
    me = lax.axis_index(axis)

    def copy_to(peer):
        return pltpu.make_async_remote_copy(
            src_ref=x_ref.at[peer],
            dst_ref=y_ref.at[me],
            send_sem=send_sem.at[peer],
            recv_sem=recv_sem.at[me],
            device_id={axis: peer},
            device_id_type=MESH,
        )

    def copy_from(source):
        return pltpu.make_async_remote_copy(
            src_ref=x_ref.at[source],
            dst_ref=y_ref.at[source],
            send_sem=send_sem.at[source],
            recv_sem=recv_sem.at[source],
            device_id={axis: source},
            device_id_type=MESH,
        )

    barrier = pltpu.get_barrier_semaphore()

    def greet(i, carry):
        pl.semaphore_signal(barrier, inc=1, device_id={axis: lax.rem(me + i, n)}, device_id_type=MESH)
        return carry

    lax.fori_loop(1, n, greet, 0)
    pl.semaphore_wait(barrier, n - 1)
    own = pltpu.make_async_copy(x_ref.at[me], y_ref.at[me], own_sem)
    own.start()

    def send(i, carry):
        copy_to(lax.rem(me + i, n)).start()
        return carry

    lax.fori_loop(1, n, send, 0)

    def finish(i, carry):
        copy_to(lax.rem(me + i, n)).wait_send()
        copy_from(lax.rem(me + n - i, n)).wait_recv()
        return carry

    lax.fori_loop(1, n, finish, 0)
    own.wait()


def _exchange(x, collective_id, axis="dp"):
    n = x.shape[0]
    return pl.pallas_call(
        functools.partial(_exchange_kernel, n, axis),
        out_shape=jax.ShapeDtypeStruct(x.shape, x.dtype),
        in_specs=[pl.BlockSpec(memory_space=pl.ANY)],
        out_specs=pl.BlockSpec(memory_space=pl.ANY),
        scratch_shapes=[
            pltpu.SemaphoreType.DMA((n,)),
            pltpu.SemaphoreType.DMA((n,)),
            pltpu.SemaphoreType.DMA(()),
        ],
        compiler_params=pltpu.CompilerParams(collective_id=collective_id, has_side_effects=True),
    )(x)


def _ring4_kernel(axis, x_ref, y_ref, relay_up, relay_down, send_sem, recv_sem, own_sem):
    me = lax.axis_index(axis)
    up, down, across = lax.rem(me + 1, 4), lax.rem(me + 3, 4), lax.rem(me + 2, 4)
    rows = x_ref.shape[1] // 2

    def remote(src, dst, slot, peer):
        return pltpu.make_async_remote_copy(
            src_ref=src,
            dst_ref=dst,
            send_sem=send_sem.at[slot],
            recv_sem=recv_sem.at[slot],
            device_id={axis: peer},
            device_id_type=MESH,
        )

    barrier = pltpu.get_barrier_semaphore()
    for peer in (up, down):
        pl.semaphore_signal(barrier, inc=1, device_id={axis: peer}, device_id_type=MESH)
    pl.semaphore_wait(barrier, 2)

    own = pltpu.make_async_copy(x_ref.at[me], y_ref.at[me], own_sem)
    own.start()
    to_up = remote(x_ref.at[up], y_ref.at[me], 0, up)
    to_down = remote(x_ref.at[down], y_ref.at[me], 1, down)
    lift = remote(x_ref.at[across, pl.ds(0, rows)], relay_up, 2, up)
    drop = remote(x_ref.at[across, pl.ds(rows, rows)], relay_down, 3, down)
    for copy in (to_up, to_down, lift, drop):
        copy.start()
    lift.wait_recv()
    pass_up = remote(relay_up, y_ref.at[down, pl.ds(0, rows)], 4, up)
    pass_up.start()
    drop.wait_recv()
    pass_down = remote(relay_down, y_ref.at[up, pl.ds(rows, rows)], 5, down)
    pass_down.start()
    for copy in (to_up, to_down, lift, drop, pass_up, pass_down):
        copy.wait_send()
    to_up.wait_recv()
    to_down.wait_recv()
    pass_up.wait_recv()
    pass_down.wait_recv()
    own.wait()


def _ring4_exchange(x, collective_id, axis):
    rows = x.shape[1] // 2
    return pl.pallas_call(
        functools.partial(_ring4_kernel, axis),
        out_shape=jax.ShapeDtypeStruct(x.shape, x.dtype),
        in_specs=[pl.BlockSpec(memory_space=pl.ANY)],
        out_specs=pl.BlockSpec(memory_space=pl.ANY),
        scratch_shapes=[
            pltpu.VMEM((rows,) + x.shape[2:], x.dtype),
            pltpu.VMEM((rows,) + x.shape[2:], x.dtype),
            pltpu.SemaphoreType.DMA((6,)),
            pltpu.SemaphoreType.DMA((6,)),
            pltpu.SemaphoreType.DMA(()),
        ],
        compiler_params=pltpu.CompilerParams(collective_id=collective_id, has_side_effects=True),
    )(x)


def _both_kernel(n, a_ref, b_ref, ya_ref, yb_ref, a_send, a_recv, a_own, relay_up, relay_down, b_send, b_recv, b_own):
    me = lax.axis_index("dp")
    at = lax.axis_index("zh")
    up, down, across = lax.rem(at + 1, 4), lax.rem(at + 3, 4), lax.rem(at + 2, 4)
    rows = b_ref.shape[1] // 2

    def dp_copy(src, dst, slot_send, slot_recv, peer):
        return pltpu.make_async_remote_copy(
            src_ref=src,
            dst_ref=dst,
            send_sem=a_send.at[slot_send],
            recv_sem=a_recv.at[slot_recv],
            device_id={"dp": peer},
            device_id_type=MESH,
        )

    def zh_copy(src, dst, slot, peer):
        return pltpu.make_async_remote_copy(
            src_ref=src,
            dst_ref=dst,
            send_sem=b_send.at[slot],
            recv_sem=b_recv.at[slot],
            device_id={"zh": peer},
            device_id_type=MESH,
        )

    barrier = pltpu.get_barrier_semaphore()

    def greet(i, carry):
        pl.semaphore_signal(barrier, inc=1, device_id={"dp": lax.rem(me + i, n)}, device_id_type=MESH)
        return carry

    lax.fori_loop(1, n, greet, 0)
    for peer in (up, down):
        pl.semaphore_signal(barrier, inc=1, device_id={"zh": peer}, device_id_type=MESH)
    pl.semaphore_wait(barrier, n + 1)

    own_a = pltpu.make_async_copy(a_ref.at[me], ya_ref.at[me], a_own)
    own_a.start()
    own_b = pltpu.make_async_copy(b_ref.at[at], yb_ref.at[at], b_own)
    own_b.start()
    to_up = zh_copy(b_ref.at[up], yb_ref.at[at], 0, up)
    to_down = zh_copy(b_ref.at[down], yb_ref.at[at], 1, down)
    lift = zh_copy(b_ref.at[across, pl.ds(0, rows)], relay_up, 2, up)
    drop = zh_copy(b_ref.at[across, pl.ds(rows, rows)], relay_down, 3, down)
    for copy in (to_up, to_down, lift, drop):
        copy.start()

    def send(i, carry):
        peer = lax.rem(me + i, n)
        dp_copy(a_ref.at[peer], ya_ref.at[me], peer, me, peer).start()
        return carry

    lax.fori_loop(1, n, send, 0)
    lift.wait_recv()
    pass_up = zh_copy(relay_up, yb_ref.at[down, pl.ds(0, rows)], 4, up)
    pass_up.start()
    drop.wait_recv()
    pass_down = zh_copy(relay_down, yb_ref.at[up, pl.ds(rows, rows)], 5, down)
    pass_down.start()

    def finish(i, carry):
        peer = lax.rem(me + i, n)
        source = lax.rem(me + n - i, n)
        dp_copy(a_ref.at[peer], ya_ref.at[me], peer, me, peer).wait_send()
        dp_copy(a_ref.at[source], ya_ref.at[source], source, source, source).wait_recv()
        return carry

    lax.fori_loop(1, n, finish, 0)
    for copy in (to_up, to_down, lift, drop, pass_up, pass_down):
        copy.wait_send()
    for copy in (to_up, to_down, pass_up, pass_down):
        copy.wait_recv()
    own_a.wait()
    own_b.wait()


def _exchange_both(a, b, collective_id):
    n = a.shape[0]
    rows = b.shape[1] // 2
    return pl.pallas_call(
        functools.partial(_both_kernel, n),
        out_shape=(jax.ShapeDtypeStruct(a.shape, a.dtype), jax.ShapeDtypeStruct(b.shape, b.dtype)),
        in_specs=[pl.BlockSpec(memory_space=pl.ANY)] * 2,
        out_specs=(pl.BlockSpec(memory_space=pl.ANY), pl.BlockSpec(memory_space=pl.ANY)),
        scratch_shapes=[
            pltpu.SemaphoreType.DMA((n,)),
            pltpu.SemaphoreType.DMA((n,)),
            pltpu.SemaphoreType.DMA(()),
            pltpu.VMEM((rows,) + b.shape[2:], b.dtype),
            pltpu.VMEM((rows,) + b.shape[2:], b.dtype),
            pltpu.SemaphoreType.DMA((6,)),
            pltpu.SemaphoreType.DMA((6,)),
            pltpu.SemaphoreType.DMA(()),
        ],
        compiler_params=pltpu.CompilerParams(collective_id=collective_id, has_side_effects=True),
    )(a, b)


def _swap_pair(x):
    return lax.ppermute(x, "core", [(0, 1), (1, 0)])


def body(
    tokens,
    cotangent,
    expert_ids,
    route_weight,
    forget_mask,
    lengths,
    gate_weight,
    up_weight,
    down_weight,
):
    tok_rows = tokens.shape[0]
    features = tokens.shape[1]
    half = features // 2
    top_count = expert_ids.shape[1]
    owners = lax.axis_size("dp")
    groups = lax.axis_size("zh")
    block = features // (2 * groups)
    capacity = 5 * tok_rows * top_count // (4 * owners)
    core = lax.axis_index("core")
    is_first = core == 0

    seq_count = lengths.shape[0]
    seq_len = tok_rows * owners // seq_count
    token_index = lax.axis_index("dp") * tok_rows + jnp.arange(tok_rows, dtype=jnp.int32)
    seq_id = token_index // seq_len
    seq_pos = token_index - seq_id * seq_len
    in_seq = seq_id[:, None] == jnp.arange(seq_count, dtype=jnp.int32)[None, :]
    limits = jnp.sum(jnp.where(in_seq, lengths[None, :], 0), axis=1)
    is_valid = (seq_pos < limits).astype(jnp.int32)
    forget = is_valid * forget_mask
    retain = is_valid - forget

    shares = route_weight / jnp.sum(route_weight, axis=1, keepdims=True)
    share_flat = shares.reshape(-1)
    assigned = tok_rows * top_count
    flat_ids = expert_ids.reshape(-1)
    one_hot = (flat_ids[:, None] == jnp.arange(owners, dtype=jnp.int32)[None, :]).astype(jnp.int32)
    before = jnp.cumsum(one_hot, axis=0) - one_hot
    slot_id = jnp.sum(before * one_hot, axis=1)
    target = flat_ids * capacity + slot_id
    slots_all = owners * capacity
    hit = target[None, :] == jnp.arange(slots_all, dtype=jnp.int32)[:, None]
    hit_tok = jnp.any(hit.reshape(slots_all, tok_rows, top_count), axis=2)

    slot_share = jnp.sum(jnp.where(hit, share_flat[None, :], 0.0), axis=1)
    share_hi = lax.reduce_precision(slot_share, exponent_bits=8, mantissa_bits=7)
    rest = slot_share - share_hi
    share_mid = lax.reduce_precision(rest, exponent_bits=8, mantissa_bits=7)
    share_lo = rest - share_mid
    slot_forget = jnp.sum(jnp.where(hit_tok, forget[None, :], 0), axis=1).astype(jnp.float32)
    slot_retain = jnp.sum(jnp.where(hit_tok, retain[None, :], 0), axis=1).astype(jnp.float32)
    per_slot = jnp.stack([share_hi, share_mid, share_lo, slot_forget, slot_retain], axis=1)
    per_slot = per_slot.reshape(owners, capacity * 5)
    local_counts = jnp.stack([jnp.sum(forget), jnp.sum(retain)]).astype(jnp.float32)
    meta = jnp.concatenate(
        [
            per_slot,
            jnp.broadcast_to(local_counts[None, :], (owners, 2)),
            jnp.zeros((owners, features - capacity * 5 - 2), jnp.float32),
        ],
        axis=1,
    ).astype(jnp.bfloat16)
    my_tokens = lax.dynamic_slice_in_dim(tokens, core * half, half, axis=1)
    my_cotan = lax.dynamic_slice_in_dim(cotangent, core * half, half, axis=1)
    lanes = 128
    pick = hit_tok.astype(tokens.dtype)
    send_tok = jnp.dot(pick, my_tokens, preferred_element_type=jnp.float32).astype(tokens.dtype)
    send_cot = jnp.dot(pick, my_cotan, preferred_element_type=jnp.float32).astype(tokens.dtype)
    got = _exchange(send_tok.reshape(owners, capacity * half // lanes, lanes), 0).reshape(slots_all, half)
    other = _swap_pair(got)
    rows_in = jnp.concatenate(
        [jnp.where(is_first, got, other), jnp.where(is_first, other, got)], axis=1
    )

    contract_last = (((1,), (1,)), ((), ()))
    contract_first = (((0,), (0,)), ((), ()))
    gate_pre = lax.dot_general(
        gate_weight[0], rows_in, contract_last, preferred_element_type=jnp.float32
    )
    up_pre = lax.dot_general(
        up_weight[0], rows_in, contract_last, preferred_element_type=jnp.float32
    )
    sigmoid_gate = jax.nn.sigmoid(gate_pre)
    hidden = (gate_pre * sigmoid_gate * up_pre).astype(jnp.bfloat16)
    down_groups = down_weight[0].reshape(down_weight.shape[1], groups, 2, block)
    keep_w = jnp.where(is_first, down_groups[:, :, 0, :], down_groups[:, :, 1, :])
    give_w = jnp.where(is_first, down_groups[:, :, 1, :], down_groups[:, :, 0, :])
    keep = jnp.einsum("hr,hzb->zrb", hidden, keep_w, preferred_element_type=jnp.float32).astype(jnp.bfloat16)
    give = jnp.einsum("hr,hzb->zrb", hidden, give_w, preferred_element_type=jnp.float32).astype(jnp.bfloat16)
    pair_sum = (keep.astype(jnp.float32) + _swap_pair(give).astype(jnp.float32)).astype(jnp.bfloat16)
    send = jnp.concatenate(
        [send_cot.reshape(owners, capacity * half // lanes, lanes), meta.reshape(owners, features // lanes, lanes)],
        axis=1,
    )
    recv, by_group = _exchange_both(send, pair_sum, 3)
    got_cot = recv[:, : capacity * half // lanes, :].reshape(slots_all, half)
    got_meta = recv[:, capacity * half // lanes :, :].reshape(owners, features).astype(jnp.float32)
    other_cot = _swap_pair(got_cot)
    cot_in = jnp.concatenate(
        [jnp.where(is_first, got_cot, other_cot), jnp.where(is_first, other_cot, got_cot)], axis=1
    )
    n_forget = jnp.sum(got_meta[:, capacity * 5])
    n_retain = jnp.sum(got_meta[:, capacity * 5 + 1])
    slot_meta = got_meta[:, : capacity * 5].reshape(slots_all, 5)
    got_share = (slot_meta[:, 0] + slot_meta[:, 1]) + slot_meta[:, 2]
    coefficient = float(top_count * tok_rows) * (
        slot_meta[:, 4] / n_retain - slot_meta[:, 3] / n_forget
    )
    routed = ((coefficient * got_share)[:, None] * cot_in.astype(jnp.float32)).astype(jnp.bfloat16)
    slice_sum = jnp.sum(by_group.astype(jnp.float32), axis=0).astype(jnp.bfloat16)
    returned = _exchange(slice_sum.reshape(owners, capacity * block // lanes, lanes), 1)
    picked = jnp.dot(
        hit.T.astype(returned.dtype),
        returned.reshape(slots_all, block),
        preferred_element_type=jnp.float32,
    ) * share_flat[:, None]
    mixed_out = jnp.sum(picked.reshape(tok_rows, top_count, block), axis=1).astype(jnp.bfloat16)

    grad_down = jnp.dot(hidden, routed, preferred_element_type=jnp.float32)
    dhidden = lax.dot_general(
        down_weight[0], routed, contract_last, preferred_element_type=jnp.float32
    )
    dgate = (dhidden * up_pre * sigmoid_gate * (1.0 + gate_pre * (1.0 - sigmoid_gate))).astype(
        jnp.bfloat16
    )
    dup = (dhidden * gate_pre * sigmoid_gate).astype(jnp.bfloat16)
    grad_gate = jnp.dot(dgate, rows_in, preferred_element_type=jnp.float32)
    grad_up = jnp.dot(dup, rows_in, preferred_element_type=jnp.float32)
    return (
        mixed_out,
        grad_gate.astype(jnp.bfloat16)[None],
        grad_up.astype(jnp.bfloat16)[None],
        grad_down.astype(jnp.bfloat16)[None],
    )


def solution(mesh):
    n_dp = mesh.shape["dp"]
    n_tensor = mesh.shape["tensor"]
    fine = Mesh(
        np.asarray(mesh.devices).reshape(n_dp, n_tensor // 2, 2), ("dp", "zh", "core")
    )
    tp = ("zh", "core")
    in_specs = (
        P("dp", None),
        P("dp", None),
        P("dp", None),
        P("dp", None),
        P("dp"),
        P(),
        P("dp", tp, None),
        P("dp", tp, None),
        P("dp", tp, None),
    )
    out_specs = (
        P("dp", tp),
        P("dp", tp, None),
        P("dp", tp, None),
        P("dp", tp, None),
    )
    return jax.shard_map(body, mesh=fine, in_specs=in_specs, out_specs=out_specs, check_vma=False)
```

```python
import functools

import jax
import jax.numpy as jnp
import numpy as np
from jax import lax
from jax.experimental import pallas as pl
from jax.experimental.pallas import tpu as pltpu
from jax.sharding import Mesh
from jax.sharding import PartitionSpec as P


MESH = pl.DeviceIdType.MESH


def _exchange_kernel(n, axis, x_ref, y_ref, send_sem, recv_sem, own_sem):
    me = lax.axis_index(axis)

    def copy_to(peer):
        return pltpu.make_async_remote_copy(
            src_ref=x_ref.at[peer],
            dst_ref=y_ref.at[me],
            send_sem=send_sem.at[peer],
            recv_sem=recv_sem.at[me],
            device_id={axis: peer},
            device_id_type=MESH,
        )

    def copy_from(source):
        return pltpu.make_async_remote_copy(
            src_ref=x_ref.at[source],
            dst_ref=y_ref.at[source],
            send_sem=send_sem.at[source],
            recv_sem=recv_sem.at[source],
            device_id={axis: source},
            device_id_type=MESH,
        )

    barrier = pltpu.get_barrier_semaphore()

    def greet(i, carry):
        pl.semaphore_signal(barrier, inc=1, device_id={axis: lax.rem(me + i, n)}, device_id_type=MESH)
        return carry

    lax.fori_loop(1, n, greet, 0)
    pl.semaphore_wait(barrier, n - 1)
    own = pltpu.make_async_copy(x_ref.at[me], y_ref.at[me], own_sem)
    own.start()

    def send(i, carry):
        copy_to(lax.rem(me + i, n)).start()
        return carry

    lax.fori_loop(1, n, send, 0)

    def finish(i, carry):
        copy_to(lax.rem(me + i, n)).wait_send()
        copy_from(lax.rem(me + n - i, n)).wait_recv()
        return carry

    lax.fori_loop(1, n, finish, 0)
    own.wait()


def _exchange(x, collective_id, axis="dp"):
    n = x.shape[0]
    return pl.pallas_call(
        functools.partial(_exchange_kernel, n, axis),
        out_shape=jax.ShapeDtypeStruct(x.shape, x.dtype),
        in_specs=[pl.BlockSpec(memory_space=pl.ANY)],
        out_specs=pl.BlockSpec(memory_space=pl.ANY),
        scratch_shapes=[
            pltpu.SemaphoreType.DMA((n,)),
            pltpu.SemaphoreType.DMA((n,)),
            pltpu.SemaphoreType.DMA(()),
        ],
        compiler_params=pltpu.CompilerParams(collective_id=collective_id, has_side_effects=True),
    )(x)


def _ring4_kernel(axis, x_ref, y_ref, relay_up, relay_down, send_sem, recv_sem, own_sem):
    me = lax.axis_index(axis)
    up, down, across = lax.rem(me + 1, 4), lax.rem(me + 3, 4), lax.rem(me + 2, 4)
    rows = x_ref.shape[1] // 2

    def remote(src, dst, slot, peer):
        return pltpu.make_async_remote_copy(
            src_ref=src,
            dst_ref=dst,
            send_sem=send_sem.at[slot],
            recv_sem=recv_sem.at[slot],
            device_id={axis: peer},
            device_id_type=MESH,
        )

    barrier = pltpu.get_barrier_semaphore()
    for peer in (up, down):
        pl.semaphore_signal(barrier, inc=1, device_id={axis: peer}, device_id_type=MESH)
    pl.semaphore_wait(barrier, 2)

    own = pltpu.make_async_copy(x_ref.at[me], y_ref.at[me], own_sem)
    own.start()
    to_up = remote(x_ref.at[up], y_ref.at[me], 0, up)
    to_down = remote(x_ref.at[down], y_ref.at[me], 1, down)
    lift = remote(x_ref.at[across, pl.ds(0, rows)], relay_up, 2, up)
    drop = remote(x_ref.at[across, pl.ds(rows, rows)], relay_down, 3, down)
    for copy in (to_up, to_down, lift, drop):
        copy.start()
    lift.wait_recv()
    pass_up = remote(relay_up, y_ref.at[down, pl.ds(0, rows)], 4, up)
    pass_up.start()
    drop.wait_recv()
    pass_down = remote(relay_down, y_ref.at[up, pl.ds(rows, rows)], 5, down)
    pass_down.start()
    for copy in (to_up, to_down, lift, drop, pass_up, pass_down):
        copy.wait_send()
    to_up.wait_recv()
    to_down.wait_recv()
    pass_up.wait_recv()
    pass_down.wait_recv()
    own.wait()


def _ring4_exchange(x, collective_id, axis):
    rows = x.shape[1] // 2
    return pl.pallas_call(
        functools.partial(_ring4_kernel, axis),
        out_shape=jax.ShapeDtypeStruct(x.shape, x.dtype),
        in_specs=[pl.BlockSpec(memory_space=pl.ANY)],
        out_specs=pl.BlockSpec(memory_space=pl.ANY),
        scratch_shapes=[
            pltpu.VMEM((rows,) + x.shape[2:], x.dtype),
            pltpu.VMEM((rows,) + x.shape[2:], x.dtype),
            pltpu.SemaphoreType.DMA((6,)),
            pltpu.SemaphoreType.DMA((6,)),
            pltpu.SemaphoreType.DMA(()),
        ],
        compiler_params=pltpu.CompilerParams(collective_id=collective_id, has_side_effects=True),
    )(x)


def _both_kernel(n, a_ref, b_ref, ya_ref, yb_ref, a_send, a_recv, a_own, relay_up, relay_down, b_send, b_recv, b_own):
    me = lax.axis_index("dp")
    at = lax.axis_index("zh")
    up, down, across = lax.rem(at + 1, 4), lax.rem(at + 3, 4), lax.rem(at + 2, 4)
    rows = b_ref.shape[1] // 2

    def dp_copy(src, dst, slot_send, slot_recv, peer):
        return pltpu.make_async_remote_copy(
            src_ref=src,
            dst_ref=dst,
            send_sem=a_send.at[slot_send],
            recv_sem=a_recv.at[slot_recv],
            device_id={"dp": peer},
            device_id_type=MESH,
        )

    def zh_copy(src, dst, slot, peer):
        return pltpu.make_async_remote_copy(
            src_ref=src,
            dst_ref=dst,
            send_sem=b_send.at[slot],
            recv_sem=b_recv.at[slot],
            device_id={"zh": peer},
            device_id_type=MESH,
        )

    barrier = pltpu.get_barrier_semaphore()

    def greet(i, carry):
        pl.semaphore_signal(barrier, inc=1, device_id={"dp": lax.rem(me + i, n)}, device_id_type=MESH)
        return carry

    lax.fori_loop(1, n, greet, 0)
    for peer in (up, down):
        pl.semaphore_signal(barrier, inc=1, device_id={"zh": peer}, device_id_type=MESH)
    pl.semaphore_wait(barrier, n + 1)

    own_a = pltpu.make_async_copy(a_ref.at[me], ya_ref.at[me], a_own)
    own_a.start()
    own_b = pltpu.make_async_copy(b_ref.at[at], yb_ref.at[at], b_own)
    own_b.start()
    to_up = zh_copy(b_ref.at[up], yb_ref.at[at], 0, up)
    to_down = zh_copy(b_ref.at[down], yb_ref.at[at], 1, down)
    lift = zh_copy(b_ref.at[across, pl.ds(0, rows)], relay_up, 2, up)
    drop = zh_copy(b_ref.at[across, pl.ds(rows, rows)], relay_down, 3, down)
    for copy in (to_up, to_down, lift, drop):
        copy.start()

    def send(i, carry):
        peer = lax.rem(me + i, n)
        dp_copy(a_ref.at[peer], ya_ref.at[me], peer, me, peer).start()
        return carry

    lax.fori_loop(1, n, send, 0)
    lift.wait_recv()
    pass_up = zh_copy(relay_up, yb_ref.at[down, pl.ds(0, rows)], 4, up)
    pass_up.start()
    drop.wait_recv()
    pass_down = zh_copy(relay_down, yb_ref.at[up, pl.ds(rows, rows)], 5, down)
    pass_down.start()

    def finish(i, carry):
        peer = lax.rem(me + i, n)
        source = lax.rem(me + n - i, n)
        dp_copy(a_ref.at[peer], ya_ref.at[me], peer, me, peer).wait_send()
        dp_copy(a_ref.at[source], ya_ref.at[source], source, source, source).wait_recv()
        return carry

    lax.fori_loop(1, n, finish, 0)
    for copy in (to_up, to_down, lift, drop, pass_up, pass_down):
        copy.wait_send()
    for copy in (to_up, to_down, pass_up, pass_down):
        copy.wait_recv()
    own_a.wait()
    own_b.wait()


def _exchange_both(a, b, collective_id):
    n = a.shape[0]
    rows = b.shape[1] // 2
    return pl.pallas_call(
        functools.partial(_both_kernel, n),
        out_shape=(jax.ShapeDtypeStruct(a.shape, a.dtype), jax.ShapeDtypeStruct(b.shape, b.dtype)),
        in_specs=[pl.BlockSpec(memory_space=pl.ANY)] * 2,
        out_specs=(pl.BlockSpec(memory_space=pl.ANY), pl.BlockSpec(memory_space=pl.ANY)),
        scratch_shapes=[
            pltpu.SemaphoreType.DMA((n,)),
            pltpu.SemaphoreType.DMA((n,)),
            pltpu.SemaphoreType.DMA(()),
            pltpu.VMEM((rows,) + b.shape[2:], b.dtype),
            pltpu.VMEM((rows,) + b.shape[2:], b.dtype),
            pltpu.SemaphoreType.DMA((6,)),
            pltpu.SemaphoreType.DMA((6,)),
            pltpu.SemaphoreType.DMA(()),
        ],
        compiler_params=pltpu.CompilerParams(collective_id=collective_id, has_side_effects=True),
    )(a, b)


def _swap_pair(x):
    return lax.ppermute(x, "core", [(0, 1), (1, 0)])


def body(
    tokens,
    cotangent,
    expert_ids,
    route_weight,
    forget_mask,
    lengths,
    gate_weight,
    up_weight,
    down_weight,
):
    tok_rows = tokens.shape[0]
    features = tokens.shape[1]
    half = features // 2
    top_count = expert_ids.shape[1]
    owners = lax.axis_size("dp")
    groups = lax.axis_size("zh")
    block = features // (2 * groups)
    capacity = 5 * tok_rows * top_count // (4 * owners)
    core = lax.axis_index("core")
    is_first = core == 0

    seq_count = lengths.shape[0]
    seq_len = tok_rows * owners // seq_count
    token_index = lax.axis_index("dp") * tok_rows + jnp.arange(tok_rows, dtype=jnp.int32)
    seq_id = token_index // seq_len
    seq_pos = token_index - seq_id * seq_len
    in_seq = seq_id[:, None] == jnp.arange(seq_count, dtype=jnp.int32)[None, :]
    limits = jnp.sum(jnp.where(in_seq, lengths[None, :], 0), axis=1)
    is_valid = (seq_pos < limits).astype(jnp.int32)
    forget = is_valid * forget_mask
    retain = is_valid - forget

    shares = route_weight / jnp.sum(route_weight, axis=1, keepdims=True)
    share_flat = shares.reshape(-1)
    assigned = tok_rows * top_count
    flat_ids = expert_ids.reshape(-1)
    one_hot = (flat_ids[:, None] == jnp.arange(owners, dtype=jnp.int32)[None, :]).astype(jnp.int32)
    before = jnp.cumsum(one_hot, axis=0) - one_hot
    slot_id = jnp.sum(before * one_hot, axis=1)
    target = flat_ids * capacity + slot_id
    slots_all = owners * capacity
    hit = target[None, :] == jnp.arange(slots_all, dtype=jnp.int32)[:, None]
    hit_tok = jnp.any(hit.reshape(slots_all, tok_rows, top_count), axis=2)

    slot_share = jnp.sum(jnp.where(hit, share_flat[None, :], 0.0), axis=1)
    share_hi = lax.reduce_precision(slot_share, exponent_bits=8, mantissa_bits=7)
    rest = slot_share - share_hi
    share_mid = lax.reduce_precision(rest, exponent_bits=8, mantissa_bits=7)
    share_lo = rest - share_mid
    slot_forget = jnp.sum(jnp.where(hit_tok, forget[None, :], 0), axis=1).astype(jnp.float32)
    slot_retain = jnp.sum(jnp.where(hit_tok, retain[None, :], 0), axis=1).astype(jnp.float32)
    per_slot = jnp.stack([share_hi, share_mid, share_lo, slot_forget, slot_retain], axis=1)
    per_slot = per_slot.reshape(owners, capacity * 5)
    local_counts = jnp.stack([jnp.sum(forget), jnp.sum(retain)]).astype(jnp.float32)
    meta = jnp.concatenate(
        [
            per_slot,
            jnp.broadcast_to(local_counts[None, :], (owners, 2)),
            jnp.zeros((owners, features - capacity * 5 - 2), jnp.float32),
        ],
        axis=1,
    ).astype(jnp.bfloat16)
    my_tokens = lax.dynamic_slice_in_dim(tokens, core * half, half, axis=1)
    my_cotan = lax.dynamic_slice_in_dim(cotangent, core * half, half, axis=1)
    lanes = 128
    pick = hit_tok.astype(tokens.dtype)
    send_tok = jnp.dot(pick, my_tokens, preferred_element_type=jnp.float32).astype(tokens.dtype)
    send_cot = jnp.dot(pick, my_cotan, preferred_element_type=jnp.float32).astype(tokens.dtype)
    got = _exchange(send_tok.reshape(owners, capacity * half // lanes, lanes), 0).reshape(slots_all, half)
    other = _swap_pair(got)
    rows_in = jnp.concatenate(
        [jnp.where(is_first, got, other), jnp.where(is_first, other, got)], axis=1
    )

    contract_last = (((1,), (1,)), ((), ()))
    contract_first = (((0,), (0,)), ((), ()))
    gate_pre = lax.dot_general(
        gate_weight[0], rows_in, contract_last, preferred_element_type=jnp.float32
    )
    up_pre = lax.dot_general(
        up_weight[0], rows_in, contract_last, preferred_element_type=jnp.float32
    )
    sigmoid_gate = jax.nn.sigmoid(gate_pre)
    hidden = (gate_pre * sigmoid_gate * up_pre).astype(jnp.bfloat16)
    down_groups = down_weight[0].reshape(down_weight.shape[1], groups, 2, block)
    keep_w = jnp.where(is_first, down_groups[:, :, 0, :], down_groups[:, :, 1, :])
    give_w = jnp.where(is_first, down_groups[:, :, 1, :], down_groups[:, :, 0, :])
    keep = jnp.einsum("hr,hzb->zrb", hidden, keep_w, preferred_element_type=jnp.float32).astype(jnp.bfloat16)
    give = jnp.einsum("hr,hzb->zrb", hidden, give_w, preferred_element_type=jnp.float32).astype(jnp.bfloat16)
    pair_sum = (keep.astype(jnp.float32) + _swap_pair(give).astype(jnp.float32)).astype(jnp.bfloat16)
    send = jnp.concatenate(
        [send_cot.reshape(owners, capacity * half // lanes, lanes), meta.reshape(owners, features // lanes, lanes)],
        axis=1,
    )
    recv, by_group = _exchange_both(send, pair_sum, 3)
    got_cot = recv[:, : capacity * half // lanes, :].reshape(slots_all, half)
    got_meta = recv[:, capacity * half // lanes :, :].reshape(owners, features).astype(jnp.float32)
    other_cot = _swap_pair(got_cot)
    cot_in = jnp.concatenate(
        [jnp.where(is_first, got_cot, other_cot), jnp.where(is_first, other_cot, got_cot)], axis=1
    )
    n_forget = jnp.sum(got_meta[:, capacity * 5])
    n_retain = jnp.sum(got_meta[:, capacity * 5 + 1])
    slot_meta = got_meta[:, : capacity * 5].reshape(slots_all, 5)
    got_share = (slot_meta[:, 0] + slot_meta[:, 1]) + slot_meta[:, 2]
    coefficient = float(top_count * tok_rows) * (
        slot_meta[:, 4] / n_retain - slot_meta[:, 3] / n_forget
    )
    routed = ((coefficient * got_share)[:, None] * cot_in.astype(jnp.float32)).astype(jnp.bfloat16)
    slice_sum = jnp.sum(by_group.astype(jnp.float32), axis=0).astype(jnp.bfloat16)
    returned = lax.all_to_all(
        slice_sum.reshape(owners, capacity, block), "dp", split_axis=0, concat_axis=0, tiled=True
    )
    picked = jnp.dot(
        hit.T.astype(returned.dtype),
        returned.reshape(slots_all, block),
        preferred_element_type=jnp.float32,
    ) * share_flat[:, None]
    mixed_out = jnp.sum(picked.reshape(tok_rows, top_count, block), axis=1).astype(jnp.bfloat16)

    grad_down = jnp.dot(hidden, routed, preferred_element_type=jnp.float32)
    dhidden = lax.dot_general(
        down_weight[0], routed, contract_last, preferred_element_type=jnp.float32
    )
    dgate = (dhidden * up_pre * sigmoid_gate * (1.0 + gate_pre * (1.0 - sigmoid_gate))).astype(
        jnp.bfloat16
    )
    dup = (dhidden * gate_pre * sigmoid_gate).astype(jnp.bfloat16)
    grad_gate = jnp.dot(dgate, rows_in, preferred_element_type=jnp.float32)
    grad_up = jnp.dot(dup, rows_in, preferred_element_type=jnp.float32)
    return (
        mixed_out,
        grad_gate.astype(jnp.bfloat16)[None],
        grad_up.astype(jnp.bfloat16)[None],
        grad_down.astype(jnp.bfloat16)[None],
    )


def solution(mesh):
    n_dp = mesh.shape["dp"]
    n_tensor = mesh.shape["tensor"]
    fine = Mesh(
        np.asarray(mesh.devices).reshape(n_dp, n_tensor // 2, 2), ("dp", "zh", "core")
    )
    tp = ("zh", "core")
    in_specs = (
        P("dp", None),
        P("dp", None),
        P("dp", None),
        P("dp", None),
        P("dp"),
        P(),
        P("dp", tp, None),
        P("dp", tp, None),
        P("dp", tp, None),
    )
    out_specs = (
        P("dp", tp),
        P("dp", tp, None),
        P("dp", tp, None),
        P("dp", tp, None),
    )
    return jax.shard_map(body, mesh=fine, in_specs=in_specs, out_specs=out_specs, check_vma=False)
```

```python
import functools

import jax
import jax.numpy as jnp
import numpy as np
from jax import lax
from jax.experimental import pallas as pl
from jax.experimental.pallas import tpu as pltpu
from jax.sharding import Mesh
from jax.sharding import PartitionSpec as P


MESH = pl.DeviceIdType.MESH


def _exchange_kernel(n, axis, x_ref, y_ref, send_sem, recv_sem, own_sem):
    me = lax.axis_index(axis)

    def copy_to(peer):
        return pltpu.make_async_remote_copy(
            src_ref=x_ref.at[peer],
            dst_ref=y_ref.at[me],
            send_sem=send_sem.at[peer],
            recv_sem=recv_sem.at[me],
            device_id={axis: peer},
            device_id_type=MESH,
        )

    def copy_from(source):
        return pltpu.make_async_remote_copy(
            src_ref=x_ref.at[source],
            dst_ref=y_ref.at[source],
            send_sem=send_sem.at[source],
            recv_sem=recv_sem.at[source],
            device_id={axis: source},
            device_id_type=MESH,
        )

    barrier = pltpu.get_barrier_semaphore()

    def greet(i, carry):
        pl.semaphore_signal(barrier, inc=1, device_id={axis: lax.rem(me + i, n)}, device_id_type=MESH)
        return carry

    lax.fori_loop(1, n, greet, 0)
    pl.semaphore_wait(barrier, n - 1)
    own = pltpu.make_async_copy(x_ref.at[me], y_ref.at[me], own_sem)
    own.start()

    def send(i, carry):
        copy_to(lax.rem(me + i, n)).start()
        return carry

    lax.fori_loop(1, n, send, 0)

    def finish(i, carry):
        copy_to(lax.rem(me + i, n)).wait_send()
        copy_from(lax.rem(me + n - i, n)).wait_recv()
        return carry

    lax.fori_loop(1, n, finish, 0)
    own.wait()


def _exchange(x, collective_id, axis="dp"):
    n = x.shape[0]
    return pl.pallas_call(
        functools.partial(_exchange_kernel, n, axis),
        out_shape=jax.ShapeDtypeStruct(x.shape, x.dtype),
        in_specs=[pl.BlockSpec(memory_space=pl.ANY)],
        out_specs=pl.BlockSpec(memory_space=pl.ANY),
        scratch_shapes=[
            pltpu.SemaphoreType.DMA((n,)),
            pltpu.SemaphoreType.DMA((n,)),
            pltpu.SemaphoreType.DMA(()),
        ],
        compiler_params=pltpu.CompilerParams(collective_id=collective_id, has_side_effects=True),
    )(x)


def _ring4_kernel(axis, x_ref, y_ref, relay_up, relay_down, send_sem, recv_sem, own_sem):
    me = lax.axis_index(axis)
    up, down, across = lax.rem(me + 1, 4), lax.rem(me + 3, 4), lax.rem(me + 2, 4)
    rows = x_ref.shape[1] // 2

    def remote(src, dst, slot, peer):
        return pltpu.make_async_remote_copy(
            src_ref=src,
            dst_ref=dst,
            send_sem=send_sem.at[slot],
            recv_sem=recv_sem.at[slot],
            device_id={axis: peer},
            device_id_type=MESH,
        )

    barrier = pltpu.get_barrier_semaphore()
    for peer in (up, down):
        pl.semaphore_signal(barrier, inc=1, device_id={axis: peer}, device_id_type=MESH)
    pl.semaphore_wait(barrier, 2)

    own = pltpu.make_async_copy(x_ref.at[me], y_ref.at[me], own_sem)
    own.start()
    to_up = remote(x_ref.at[up], y_ref.at[me], 0, up)
    to_down = remote(x_ref.at[down], y_ref.at[me], 1, down)
    lift = remote(x_ref.at[across, pl.ds(0, rows)], relay_up, 2, up)
    drop = remote(x_ref.at[across, pl.ds(rows, rows)], relay_down, 3, down)
    for copy in (to_up, to_down, lift, drop):
        copy.start()
    lift.wait_recv()
    pass_up = remote(relay_up, y_ref.at[down, pl.ds(0, rows)], 4, up)
    pass_up.start()
    drop.wait_recv()
    pass_down = remote(relay_down, y_ref.at[up, pl.ds(rows, rows)], 5, down)
    pass_down.start()
    for copy in (to_up, to_down, lift, drop, pass_up, pass_down):
        copy.wait_send()
    to_up.wait_recv()
    to_down.wait_recv()
    pass_up.wait_recv()
    pass_down.wait_recv()
    own.wait()


def _ring4_exchange(x, collective_id, axis):
    rows = x.shape[1] // 2
    return pl.pallas_call(
        functools.partial(_ring4_kernel, axis),
        out_shape=jax.ShapeDtypeStruct(x.shape, x.dtype),
        in_specs=[pl.BlockSpec(memory_space=pl.ANY)],
        out_specs=pl.BlockSpec(memory_space=pl.ANY),
        scratch_shapes=[
            pltpu.VMEM((rows,) + x.shape[2:], x.dtype),
            pltpu.VMEM((rows,) + x.shape[2:], x.dtype),
            pltpu.SemaphoreType.DMA((6,)),
            pltpu.SemaphoreType.DMA((6,)),
            pltpu.SemaphoreType.DMA(()),
        ],
        compiler_params=pltpu.CompilerParams(collective_id=collective_id, has_side_effects=True),
    )(x)


def _both_kernel(n, a_ref, b_ref, ya_ref, yb_ref, yp_ref, a_send, a_recv, a_own, relay_up, relay_down, b_send, b_recv, b_own, p_sem):
    me = lax.axis_index("dp")
    at = lax.axis_index("zh")
    up, down, across = lax.rem(at + 1, 4), lax.rem(at + 3, 4), lax.rem(at + 2, 4)
    rows = b_ref.shape[1] // 2

    def dp_copy(src, dst, slot_send, slot_recv, peer):
        return pltpu.make_async_remote_copy(
            src_ref=src,
            dst_ref=dst,
            send_sem=a_send.at[slot_send],
            recv_sem=a_recv.at[slot_recv],
            device_id={"dp": peer},
            device_id_type=MESH,
        )

    def zh_copy(src, dst, slot, peer):
        return pltpu.make_async_remote_copy(
            src_ref=src,
            dst_ref=dst,
            send_sem=b_send.at[slot],
            recv_sem=b_recv.at[slot],
            device_id={"zh": peer},
            device_id_type=MESH,
        )

    barrier = pltpu.get_barrier_semaphore()

    def greet(i, carry):
        pl.semaphore_signal(barrier, inc=1, device_id={"dp": lax.rem(me + i, n)}, device_id_type=MESH)
        return carry

    lax.fori_loop(1, n, greet, 0)
    for peer in (up, down):
        pl.semaphore_signal(barrier, inc=1, device_id={"zh": peer}, device_id_type=MESH)
    partner = 1 - lax.axis_index("core")
    pl.semaphore_signal(barrier, inc=1, device_id={"core": partner}, device_id_type=MESH)
    pl.semaphore_wait(barrier, n + 2)

    own_a = pltpu.make_async_copy(a_ref.at[me], ya_ref.at[me], a_own)
    own_a.start()
    own_b = pltpu.make_async_copy(b_ref.at[at], yb_ref.at[at], b_own)
    own_b.start()
    to_up = zh_copy(b_ref.at[up], yb_ref.at[at], 0, up)
    to_down = zh_copy(b_ref.at[down], yb_ref.at[at], 1, down)
    lift = zh_copy(b_ref.at[across, pl.ds(0, rows)], relay_up, 2, up)
    drop = zh_copy(b_ref.at[across, pl.ds(rows, rows)], relay_down, 3, down)
    for copy in (to_up, to_down, lift, drop):
        copy.start()

    def send(i, carry):
        peer = lax.rem(me + i, n)
        dp_copy(a_ref.at[peer], ya_ref.at[me], peer, me, peer).start()
        return carry

    lax.fori_loop(1, n, send, 0)
    lift.wait_recv()
    pass_up = zh_copy(relay_up, yb_ref.at[down, pl.ds(0, rows)], 4, up)
    pass_up.start()
    drop.wait_recv()
    pass_down = zh_copy(relay_down, yb_ref.at[up, pl.ds(rows, rows)], 5, down)
    pass_down.start()

    def finish(i, carry):
        peer = lax.rem(me + i, n)
        source = lax.rem(me + n - i, n)
        dp_copy(a_ref.at[peer], ya_ref.at[me], peer, me, peer).wait_send()
        dp_copy(a_ref.at[source], ya_ref.at[source], source, source, source).wait_recv()
        return carry

    lax.fori_loop(1, n, finish, 0)
    own_a.wait()
    to_partner = pltpu.make_async_remote_copy(
        src_ref=ya_ref,
        dst_ref=yp_ref,
        send_sem=p_sem.at[0],
        recv_sem=p_sem.at[1],
        device_id={"core": partner},
        device_id_type=MESH,
    )
    to_partner.start()
    for copy in (to_up, to_down, lift, drop, pass_up, pass_down):
        copy.wait_send()
    for copy in (to_up, to_down, pass_up, pass_down):
        copy.wait_recv()
    own_b.wait()
    to_partner.wait()


def _exchange_both(a, b, collective_id):
    n = a.shape[0]
    rows = b.shape[1] // 2
    return pl.pallas_call(
        functools.partial(_both_kernel, n),
        out_shape=(
            jax.ShapeDtypeStruct(a.shape, a.dtype),
            jax.ShapeDtypeStruct(b.shape, b.dtype),
            jax.ShapeDtypeStruct(a.shape, a.dtype),
        ),
        in_specs=[pl.BlockSpec(memory_space=pl.ANY)] * 2,
        out_specs=(pl.BlockSpec(memory_space=pl.ANY),) * 3,
        scratch_shapes=[
            pltpu.SemaphoreType.DMA((n,)),
            pltpu.SemaphoreType.DMA((n,)),
            pltpu.SemaphoreType.DMA(()),
            pltpu.VMEM((rows,) + b.shape[2:], b.dtype),
            pltpu.VMEM((rows,) + b.shape[2:], b.dtype),
            pltpu.SemaphoreType.DMA((6,)),
            pltpu.SemaphoreType.DMA((6,)),
            pltpu.SemaphoreType.DMA(()),
            pltpu.SemaphoreType.DMA((2,)),
        ],
        compiler_params=pltpu.CompilerParams(collective_id=collective_id, has_side_effects=True),
    )(a, b)


def _swap_pair(x):
    return lax.ppermute(x, "core", [(0, 1), (1, 0)])


def body(
    tokens,
    cotangent,
    expert_ids,
    route_weight,
    forget_mask,
    lengths,
    gate_weight,
    up_weight,
    down_weight,
):
    tok_rows = tokens.shape[0]
    features = tokens.shape[1]
    half = features // 2
    top_count = expert_ids.shape[1]
    owners = lax.axis_size("dp")
    groups = lax.axis_size("zh")
    block = features // (2 * groups)
    capacity = 5 * tok_rows * top_count // (4 * owners)
    core = lax.axis_index("core")
    is_first = core == 0

    seq_count = lengths.shape[0]
    seq_len = tok_rows * owners // seq_count
    token_index = lax.axis_index("dp") * tok_rows + jnp.arange(tok_rows, dtype=jnp.int32)
    seq_id = token_index // seq_len
    seq_pos = token_index - seq_id * seq_len
    in_seq = seq_id[:, None] == jnp.arange(seq_count, dtype=jnp.int32)[None, :]
    limits = jnp.sum(jnp.where(in_seq, lengths[None, :], 0), axis=1)
    is_valid = (seq_pos < limits).astype(jnp.int32)
    forget = is_valid * forget_mask
    retain = is_valid - forget

    shares = route_weight / jnp.sum(route_weight, axis=1, keepdims=True)
    share_flat = shares.reshape(-1)
    assigned = tok_rows * top_count
    flat_ids = expert_ids.reshape(-1)
    one_hot = (flat_ids[:, None] == jnp.arange(owners, dtype=jnp.int32)[None, :]).astype(jnp.int32)
    before = jnp.cumsum(one_hot, axis=0) - one_hot
    slot_id = jnp.sum(before * one_hot, axis=1)
    target = flat_ids * capacity + slot_id
    slots_all = owners * capacity
    hit = target[None, :] == jnp.arange(slots_all, dtype=jnp.int32)[:, None]
    hit_tok = jnp.any(hit.reshape(slots_all, tok_rows, top_count), axis=2)

    slot_share = jnp.sum(jnp.where(hit, share_flat[None, :], 0.0), axis=1)
    share_hi = lax.reduce_precision(slot_share, exponent_bits=8, mantissa_bits=7)
    rest = slot_share - share_hi
    share_mid = lax.reduce_precision(rest, exponent_bits=8, mantissa_bits=7)
    share_lo = rest - share_mid
    slot_forget = jnp.sum(jnp.where(hit_tok, forget[None, :], 0), axis=1).astype(jnp.float32)
    slot_retain = jnp.sum(jnp.where(hit_tok, retain[None, :], 0), axis=1).astype(jnp.float32)
    per_slot = jnp.stack([share_hi, share_mid, share_lo, slot_forget, slot_retain], axis=1)
    per_slot = per_slot.reshape(owners, capacity * 5)
    local_counts = jnp.stack([jnp.sum(forget), jnp.sum(retain)]).astype(jnp.float32)
    meta = jnp.concatenate(
        [
            per_slot,
            jnp.broadcast_to(local_counts[None, :], (owners, 2)),
            jnp.zeros((owners, features - capacity * 5 - 2), jnp.float32),
        ],
        axis=1,
    ).astype(jnp.bfloat16)
    my_tokens = lax.dynamic_slice_in_dim(tokens, core * half, half, axis=1)
    my_cotan = lax.dynamic_slice_in_dim(cotangent, core * half, half, axis=1)
    lanes = 128
    pick = hit_tok.astype(tokens.dtype)
    send_tok = jnp.dot(pick, my_tokens, preferred_element_type=jnp.float32).astype(tokens.dtype)
    send_cot = jnp.dot(pick, my_cotan, preferred_element_type=jnp.float32).astype(tokens.dtype)
    got = _exchange(send_tok.reshape(owners, capacity * half // lanes, lanes), 0).reshape(slots_all, half)
    other = _swap_pair(got)
    rows_in = jnp.concatenate(
        [jnp.where(is_first, got, other), jnp.where(is_first, other, got)], axis=1
    )

    contract_last = (((1,), (1,)), ((), ()))
    contract_first = (((0,), (0,)), ((), ()))
    gate_pre = lax.dot_general(
        gate_weight[0], rows_in, contract_last, preferred_element_type=jnp.float32
    )
    up_pre = lax.dot_general(
        up_weight[0], rows_in, contract_last, preferred_element_type=jnp.float32
    )
    sigmoid_gate = jax.nn.sigmoid(gate_pre)
    hidden = (gate_pre * sigmoid_gate * up_pre).astype(jnp.bfloat16)
    down_groups = down_weight[0].reshape(down_weight.shape[1], groups, 2, block)
    keep_w = jnp.where(is_first, down_groups[:, :, 0, :], down_groups[:, :, 1, :])
    give_w = jnp.where(is_first, down_groups[:, :, 1, :], down_groups[:, :, 0, :])
    keep = jnp.einsum("hr,hzb->zrb", hidden, keep_w, preferred_element_type=jnp.float32).astype(jnp.bfloat16)
    give = jnp.einsum("hr,hzb->zrb", hidden, give_w, preferred_element_type=jnp.float32).astype(jnp.bfloat16)
    pair_sum = (keep.astype(jnp.float32) + _swap_pair(give).astype(jnp.float32)).astype(jnp.bfloat16)
    send = jnp.concatenate(
        [send_cot.reshape(owners, capacity * half // lanes, lanes), meta.reshape(owners, features // lanes, lanes)],
        axis=1,
    )
    recv, by_group, recv_other = _exchange_both(send, pair_sum, 3)
    got_cot = recv[:, : capacity * half // lanes, :].reshape(slots_all, half)
    got_meta = recv[:, capacity * half // lanes :, :].reshape(owners, features).astype(jnp.float32)
    other_cot = recv_other[:, : capacity * half // lanes, :].reshape(slots_all, half)
    cot_in = jnp.concatenate(
        [jnp.where(is_first, got_cot, other_cot), jnp.where(is_first, other_cot, got_cot)], axis=1
    )
    n_forget = jnp.sum(got_meta[:, capacity * 5])
    n_retain = jnp.sum(got_meta[:, capacity * 5 + 1])
    slot_meta = got_meta[:, : capacity * 5].reshape(slots_all, 5)
    got_share = (slot_meta[:, 0] + slot_meta[:, 1]) + slot_meta[:, 2]
    coefficient = float(top_count * tok_rows) * (
        slot_meta[:, 4] / n_retain - slot_meta[:, 3] / n_forget
    )
    routed = ((coefficient * got_share)[:, None] * cot_in.astype(jnp.float32)).astype(jnp.bfloat16)
    slice_sum = jnp.sum(by_group.astype(jnp.float32), axis=0).astype(jnp.bfloat16)
    returned = lax.all_to_all(
        slice_sum.reshape(owners, capacity, block), "dp", split_axis=0, concat_axis=0, tiled=True
    )
    picked = jnp.dot(
        hit.T.astype(returned.dtype),
        returned.reshape(slots_all, block),
        preferred_element_type=jnp.float32,
    ) * share_flat[:, None]
    mixed_out = jnp.sum(picked.reshape(tok_rows, top_count, block), axis=1).astype(jnp.bfloat16)

    grad_down = jnp.dot(hidden, routed, preferred_element_type=jnp.float32)
    dhidden = lax.dot_general(
        down_weight[0], routed, contract_last, preferred_element_type=jnp.float32
    )
    dgate = (dhidden * up_pre * sigmoid_gate * (1.0 + gate_pre * (1.0 - sigmoid_gate))).astype(
        jnp.bfloat16
    )
    dup = (dhidden * gate_pre * sigmoid_gate).astype(jnp.bfloat16)
    grad_gate = jnp.dot(dgate, rows_in, preferred_element_type=jnp.float32)
    grad_up = jnp.dot(dup, rows_in, preferred_element_type=jnp.float32)
    return (
        mixed_out,
        grad_gate.astype(jnp.bfloat16)[None],
        grad_up.astype(jnp.bfloat16)[None],
        grad_down.astype(jnp.bfloat16)[None],
    )


def solution(mesh):
    n_dp = mesh.shape["dp"]
    n_tensor = mesh.shape["tensor"]
    fine = Mesh(
        np.asarray(mesh.devices).reshape(n_dp, n_tensor // 2, 2), ("dp", "zh", "core")
    )
    tp = ("zh", "core")
    in_specs = (
        P("dp", None),
        P("dp", None),
        P("dp", None),
        P("dp", None),
        P("dp"),
        P(),
        P("dp", tp, None),
        P("dp", tp, None),
        P("dp", tp, None),
    )
    out_specs = (
        P("dp", tp),
        P("dp", tp, None),
        P("dp", tp, None),
        P("dp", tp, None),
    )
    return jax.shard_map(body, mesh=fine, in_specs=in_specs, out_specs=out_specs, check_vma=False)
```

```python
import functools

import jax
import jax.numpy as jnp
import numpy as np
from jax import lax
from jax.experimental import pallas as pl
from jax.experimental.pallas import tpu as pltpu
from jax.sharding import Mesh
from jax.sharding import PartitionSpec as P


MESH = pl.DeviceIdType.MESH


def _exchange_kernel(n, axis, x_ref, y_ref, yp_ref, send_sem, recv_sem, own_sem, p_sem):
    me = lax.axis_index(axis)

    def copy_to(peer):
        return pltpu.make_async_remote_copy(
            src_ref=x_ref.at[peer],
            dst_ref=y_ref.at[me],
            send_sem=send_sem.at[peer],
            recv_sem=recv_sem.at[me],
            device_id={axis: peer},
            device_id_type=MESH,
        )

    def copy_from(source):
        return pltpu.make_async_remote_copy(
            src_ref=x_ref.at[source],
            dst_ref=y_ref.at[source],
            send_sem=send_sem.at[source],
            recv_sem=recv_sem.at[source],
            device_id={axis: source},
            device_id_type=MESH,
        )

    barrier = pltpu.get_barrier_semaphore()

    def greet(i, carry):
        pl.semaphore_signal(barrier, inc=1, device_id={axis: lax.rem(me + i, n)}, device_id_type=MESH)
        return carry

    lax.fori_loop(1, n, greet, 0)
    partner = 1 - lax.axis_index("core")
    pl.semaphore_signal(barrier, inc=1, device_id={"core": partner}, device_id_type=MESH)
    pl.semaphore_wait(barrier, n)
    own = pltpu.make_async_copy(x_ref.at[me], y_ref.at[me], own_sem)
    own.start()

    def send(i, carry):
        copy_to(lax.rem(me + i, n)).start()
        return carry

    lax.fori_loop(1, n, send, 0)

    def finish(i, carry):
        copy_to(lax.rem(me + i, n)).wait_send()
        copy_from(lax.rem(me + n - i, n)).wait_recv()
        return carry

    lax.fori_loop(1, n, finish, 0)
    own.wait()
    to_partner = pltpu.make_async_remote_copy(
        src_ref=y_ref,
        dst_ref=yp_ref,
        send_sem=p_sem.at[0],
        recv_sem=p_sem.at[1],
        device_id={"core": partner},
        device_id_type=MESH,
    )
    to_partner.start()
    to_partner.wait()


def _exchange(x, collective_id, axis="dp"):
    n = x.shape[0]
    return pl.pallas_call(
        functools.partial(_exchange_kernel, n, axis),
        out_shape=(jax.ShapeDtypeStruct(x.shape, x.dtype), jax.ShapeDtypeStruct(x.shape, x.dtype)),
        in_specs=[pl.BlockSpec(memory_space=pl.ANY)],
        out_specs=(pl.BlockSpec(memory_space=pl.ANY), pl.BlockSpec(memory_space=pl.ANY)),
        scratch_shapes=[
            pltpu.SemaphoreType.DMA((n,)),
            pltpu.SemaphoreType.DMA((n,)),
            pltpu.SemaphoreType.DMA(()),
            pltpu.SemaphoreType.DMA((2,)),
        ],
        compiler_params=pltpu.CompilerParams(collective_id=collective_id, has_side_effects=True),
    )(x)


def _ring4_kernel(axis, x_ref, y_ref, relay_up, relay_down, send_sem, recv_sem, own_sem):
    me = lax.axis_index(axis)
    up, down, across = lax.rem(me + 1, 4), lax.rem(me + 3, 4), lax.rem(me + 2, 4)
    rows = x_ref.shape[1] // 2

    def remote(src, dst, slot, peer):
        return pltpu.make_async_remote_copy(
            src_ref=src,
            dst_ref=dst,
            send_sem=send_sem.at[slot],
            recv_sem=recv_sem.at[slot],
            device_id={axis: peer},
            device_id_type=MESH,
        )

    barrier = pltpu.get_barrier_semaphore()
    for peer in (up, down):
        pl.semaphore_signal(barrier, inc=1, device_id={axis: peer}, device_id_type=MESH)
    pl.semaphore_wait(barrier, 2)

    own = pltpu.make_async_copy(x_ref.at[me], y_ref.at[me], own_sem)
    own.start()
    to_up = remote(x_ref.at[up], y_ref.at[me], 0, up)
    to_down = remote(x_ref.at[down], y_ref.at[me], 1, down)
    lift = remote(x_ref.at[across, pl.ds(0, rows)], relay_up, 2, up)
    drop = remote(x_ref.at[across, pl.ds(rows, rows)], relay_down, 3, down)
    for copy in (to_up, to_down, lift, drop):
        copy.start()
    lift.wait_recv()
    pass_up = remote(relay_up, y_ref.at[down, pl.ds(0, rows)], 4, up)
    pass_up.start()
    drop.wait_recv()
    pass_down = remote(relay_down, y_ref.at[up, pl.ds(rows, rows)], 5, down)
    pass_down.start()
    for copy in (to_up, to_down, lift, drop, pass_up, pass_down):
        copy.wait_send()
    to_up.wait_recv()
    to_down.wait_recv()
    pass_up.wait_recv()
    pass_down.wait_recv()
    own.wait()


def _ring4_exchange(x, collective_id, axis):
    rows = x.shape[1] // 2
    return pl.pallas_call(
        functools.partial(_ring4_kernel, axis),
        out_shape=jax.ShapeDtypeStruct(x.shape, x.dtype),
        in_specs=[pl.BlockSpec(memory_space=pl.ANY)],
        out_specs=pl.BlockSpec(memory_space=pl.ANY),
        scratch_shapes=[
            pltpu.VMEM((rows,) + x.shape[2:], x.dtype),
            pltpu.VMEM((rows,) + x.shape[2:], x.dtype),
            pltpu.SemaphoreType.DMA((6,)),
            pltpu.SemaphoreType.DMA((6,)),
            pltpu.SemaphoreType.DMA(()),
        ],
        compiler_params=pltpu.CompilerParams(collective_id=collective_id, has_side_effects=True),
    )(x)


def _both_kernel(n, a_ref, b_ref, ya_ref, yb_ref, yp_ref, a_send, a_recv, a_own, relay_up, relay_down, b_send, b_recv, b_own, p_sem):
    me = lax.axis_index("dp")
    at = lax.axis_index("zh")
    up, down, across = lax.rem(at + 1, 4), lax.rem(at + 3, 4), lax.rem(at + 2, 4)
    rows = b_ref.shape[1] // 2

    def dp_copy(src, dst, slot_send, slot_recv, peer):
        return pltpu.make_async_remote_copy(
            src_ref=src,
            dst_ref=dst,
            send_sem=a_send.at[slot_send],
            recv_sem=a_recv.at[slot_recv],
            device_id={"dp": peer},
            device_id_type=MESH,
        )

    def zh_copy(src, dst, slot, peer):
        return pltpu.make_async_remote_copy(
            src_ref=src,
            dst_ref=dst,
            send_sem=b_send.at[slot],
            recv_sem=b_recv.at[slot],
            device_id={"zh": peer},
            device_id_type=MESH,
        )

    barrier = pltpu.get_barrier_semaphore()

    def greet(i, carry):
        pl.semaphore_signal(barrier, inc=1, device_id={"dp": lax.rem(me + i, n)}, device_id_type=MESH)
        return carry

    lax.fori_loop(1, n, greet, 0)
    for peer in (up, down):
        pl.semaphore_signal(barrier, inc=1, device_id={"zh": peer}, device_id_type=MESH)
    partner = 1 - lax.axis_index("core")
    pl.semaphore_signal(barrier, inc=1, device_id={"core": partner}, device_id_type=MESH)
    pl.semaphore_wait(barrier, n + 2)

    own_a = pltpu.make_async_copy(a_ref.at[me], ya_ref.at[me], a_own)
    own_a.start()
    own_b = pltpu.make_async_copy(b_ref.at[at], yb_ref.at[at], b_own)
    own_b.start()
    to_up = zh_copy(b_ref.at[up], yb_ref.at[at], 0, up)
    to_down = zh_copy(b_ref.at[down], yb_ref.at[at], 1, down)
    lift = zh_copy(b_ref.at[across, pl.ds(0, rows)], relay_up, 2, up)
    drop = zh_copy(b_ref.at[across, pl.ds(rows, rows)], relay_down, 3, down)
    for copy in (to_up, to_down, lift, drop):
        copy.start()

    def send(i, carry):
        peer = lax.rem(me + i, n)
        dp_copy(a_ref.at[peer], ya_ref.at[me], peer, me, peer).start()
        return carry

    lax.fori_loop(1, n, send, 0)
    lift.wait_recv()
    pass_up = zh_copy(relay_up, yb_ref.at[down, pl.ds(0, rows)], 4, up)
    pass_up.start()
    drop.wait_recv()
    pass_down = zh_copy(relay_down, yb_ref.at[up, pl.ds(rows, rows)], 5, down)
    pass_down.start()

    def finish(i, carry):
        peer = lax.rem(me + i, n)
        source = lax.rem(me + n - i, n)
        dp_copy(a_ref.at[peer], ya_ref.at[me], peer, me, peer).wait_send()
        dp_copy(a_ref.at[source], ya_ref.at[source], source, source, source).wait_recv()
        return carry

    lax.fori_loop(1, n, finish, 0)
    own_a.wait()
    to_partner = pltpu.make_async_remote_copy(
        src_ref=ya_ref,
        dst_ref=yp_ref,
        send_sem=p_sem.at[0],
        recv_sem=p_sem.at[1],
        device_id={"core": partner},
        device_id_type=MESH,
    )
    to_partner.start()
    for copy in (to_up, to_down, lift, drop, pass_up, pass_down):
        copy.wait_send()
    for copy in (to_up, to_down, pass_up, pass_down):
        copy.wait_recv()
    own_b.wait()
    to_partner.wait()


def _exchange_both(a, b, collective_id):
    n = a.shape[0]
    rows = b.shape[1] // 2
    return pl.pallas_call(
        functools.partial(_both_kernel, n),
        out_shape=(
            jax.ShapeDtypeStruct(a.shape, a.dtype),
            jax.ShapeDtypeStruct(b.shape, b.dtype),
            jax.ShapeDtypeStruct(a.shape, a.dtype),
        ),
        in_specs=[pl.BlockSpec(memory_space=pl.ANY)] * 2,
        out_specs=(pl.BlockSpec(memory_space=pl.ANY),) * 3,
        scratch_shapes=[
            pltpu.SemaphoreType.DMA((n,)),
            pltpu.SemaphoreType.DMA((n,)),
            pltpu.SemaphoreType.DMA(()),
            pltpu.VMEM((rows,) + b.shape[2:], b.dtype),
            pltpu.VMEM((rows,) + b.shape[2:], b.dtype),
            pltpu.SemaphoreType.DMA((6,)),
            pltpu.SemaphoreType.DMA((6,)),
            pltpu.SemaphoreType.DMA(()),
            pltpu.SemaphoreType.DMA((2,)),
        ],
        compiler_params=pltpu.CompilerParams(collective_id=collective_id, has_side_effects=True),
    )(a, b)


def _swap_pair(x):
    return lax.ppermute(x, "core", [(0, 1), (1, 0)])


def body(
    tokens,
    cotangent,
    expert_ids,
    route_weight,
    forget_mask,
    lengths,
    gate_weight,
    up_weight,
    down_weight,
):
    tok_rows = tokens.shape[0]
    features = tokens.shape[1]
    half = features // 2
    top_count = expert_ids.shape[1]
    owners = lax.axis_size("dp")
    groups = lax.axis_size("zh")
    block = features // (2 * groups)
    capacity = 5 * tok_rows * top_count // (4 * owners)
    core = lax.axis_index("core")
    is_first = core == 0

    seq_count = lengths.shape[0]
    seq_len = tok_rows * owners // seq_count
    token_index = lax.axis_index("dp") * tok_rows + jnp.arange(tok_rows, dtype=jnp.int32)
    seq_id = token_index // seq_len
    seq_pos = token_index - seq_id * seq_len
    in_seq = seq_id[:, None] == jnp.arange(seq_count, dtype=jnp.int32)[None, :]
    limits = jnp.sum(jnp.where(in_seq, lengths[None, :], 0), axis=1)
    is_valid = (seq_pos < limits).astype(jnp.int32)
    forget = is_valid * forget_mask
    retain = is_valid - forget

    shares = route_weight / jnp.sum(route_weight, axis=1, keepdims=True)
    share_flat = shares.reshape(-1)
    assigned = tok_rows * top_count
    flat_ids = expert_ids.reshape(-1)
    one_hot = (flat_ids[:, None] == jnp.arange(owners, dtype=jnp.int32)[None, :]).astype(jnp.int32)
    before = jnp.cumsum(one_hot, axis=0) - one_hot
    slot_id = jnp.sum(before * one_hot, axis=1)
    target = flat_ids * capacity + slot_id
    slots_all = owners * capacity
    hit = target[None, :] == jnp.arange(slots_all, dtype=jnp.int32)[:, None]
    hit_tok = jnp.any(hit.reshape(slots_all, tok_rows, top_count), axis=2)

    slot_share = jnp.sum(jnp.where(hit, share_flat[None, :], 0.0), axis=1)
    share_hi = lax.reduce_precision(slot_share, exponent_bits=8, mantissa_bits=7)
    rest = slot_share - share_hi
    share_mid = lax.reduce_precision(rest, exponent_bits=8, mantissa_bits=7)
    share_lo = rest - share_mid
    slot_forget = jnp.sum(jnp.where(hit_tok, forget[None, :], 0), axis=1).astype(jnp.float32)
    slot_retain = jnp.sum(jnp.where(hit_tok, retain[None, :], 0), axis=1).astype(jnp.float32)
    per_slot = jnp.stack([share_hi, share_mid, share_lo, slot_forget, slot_retain], axis=1)
    per_slot = per_slot.reshape(owners, capacity * 5)
    local_counts = jnp.stack([jnp.sum(forget), jnp.sum(retain)]).astype(jnp.float32)
    meta = jnp.concatenate(
        [
            per_slot,
            jnp.broadcast_to(local_counts[None, :], (owners, 2)),
            jnp.zeros((owners, features - capacity * 5 - 2), jnp.float32),
        ],
        axis=1,
    ).astype(jnp.bfloat16)
    my_tokens = lax.dynamic_slice_in_dim(tokens, core * half, half, axis=1)
    my_cotan = lax.dynamic_slice_in_dim(cotangent, core * half, half, axis=1)
    lanes = 128
    pick = hit_tok.astype(tokens.dtype)
    send_tok = jnp.dot(pick, my_tokens, preferred_element_type=jnp.float32).astype(tokens.dtype)
    send_cot = jnp.dot(pick, my_cotan, preferred_element_type=jnp.float32).astype(tokens.dtype)
    got, other = _exchange(send_tok.reshape(owners, capacity * half // lanes, lanes), 0)
    got = got.reshape(slots_all, half)
    other = other.reshape(slots_all, half)
    rows_in = jnp.concatenate(
        [jnp.where(is_first, got, other), jnp.where(is_first, other, got)], axis=1
    )

    contract_last = (((1,), (1,)), ((), ()))
    contract_first = (((0,), (0,)), ((), ()))
    gate_pre = lax.dot_general(
        gate_weight[0], rows_in, contract_last, preferred_element_type=jnp.float32
    )
    up_pre = lax.dot_general(
        up_weight[0], rows_in, contract_last, preferred_element_type=jnp.float32
    )
    sigmoid_gate = jax.nn.sigmoid(gate_pre)
    hidden = (gate_pre * sigmoid_gate * up_pre).astype(jnp.bfloat16)
    down_groups = down_weight[0].reshape(down_weight.shape[1], groups, 2, block)
    keep_w = jnp.where(is_first, down_groups[:, :, 0, :], down_groups[:, :, 1, :])
    give_w = jnp.where(is_first, down_groups[:, :, 1, :], down_groups[:, :, 0, :])
    keep = jnp.einsum("hr,hzb->zrb", hidden, keep_w, preferred_element_type=jnp.float32).astype(jnp.bfloat16)
    give = jnp.einsum("hr,hzb->zrb", hidden, give_w, preferred_element_type=jnp.float32).astype(jnp.bfloat16)
    pair_sum = (keep.astype(jnp.float32) + _swap_pair(give).astype(jnp.float32)).astype(jnp.bfloat16)
    send = jnp.concatenate(
        [send_cot.reshape(owners, capacity * half // lanes, lanes), meta.reshape(owners, features // lanes, lanes)],
        axis=1,
    )
    recv, by_group, recv_other = _exchange_both(send, pair_sum, 3)
    got_cot = recv[:, : capacity * half // lanes, :].reshape(slots_all, half)
    got_meta = recv[:, capacity * half // lanes :, :].reshape(owners, features).astype(jnp.float32)
    other_cot = recv_other[:, : capacity * half // lanes, :].reshape(slots_all, half)
    cot_in = jnp.concatenate(
        [jnp.where(is_first, got_cot, other_cot), jnp.where(is_first, other_cot, got_cot)], axis=1
    )
    n_forget = jnp.sum(got_meta[:, capacity * 5])
    n_retain = jnp.sum(got_meta[:, capacity * 5 + 1])
    slot_meta = got_meta[:, : capacity * 5].reshape(slots_all, 5)
    got_share = (slot_meta[:, 0] + slot_meta[:, 1]) + slot_meta[:, 2]
    coefficient = float(top_count * tok_rows) * (
        slot_meta[:, 4] / n_retain - slot_meta[:, 3] / n_forget
    )
    routed = ((coefficient * got_share)[:, None] * cot_in.astype(jnp.float32)).astype(jnp.bfloat16)
    slice_sum = jnp.sum(by_group.astype(jnp.float32), axis=0).astype(jnp.bfloat16)
    returned = lax.all_to_all(
        slice_sum.reshape(owners, capacity, block), "dp", split_axis=0, concat_axis=0, tiled=True
    )
    picked = jnp.dot(
        hit.T.astype(returned.dtype),
        returned.reshape(slots_all, block),
        preferred_element_type=jnp.float32,
    ) * share_flat[:, None]
    mixed_out = jnp.sum(picked.reshape(tok_rows, top_count, block), axis=1).astype(jnp.bfloat16)

    grad_down = jnp.dot(hidden, routed, preferred_element_type=jnp.float32)
    dhidden = lax.dot_general(
        down_weight[0], routed, contract_last, preferred_element_type=jnp.float32
    )
    dgate = (dhidden * up_pre * sigmoid_gate * (1.0 + gate_pre * (1.0 - sigmoid_gate))).astype(
        jnp.bfloat16
    )
    dup = (dhidden * gate_pre * sigmoid_gate).astype(jnp.bfloat16)
    grad_gate = jnp.dot(dgate, rows_in, preferred_element_type=jnp.float32)
    grad_up = jnp.dot(dup, rows_in, preferred_element_type=jnp.float32)
    return (
        mixed_out,
        grad_gate.astype(jnp.bfloat16)[None],
        grad_up.astype(jnp.bfloat16)[None],
        grad_down.astype(jnp.bfloat16)[None],
    )


def solution(mesh):
    n_dp = mesh.shape["dp"]
    n_tensor = mesh.shape["tensor"]
    fine = Mesh(
        np.asarray(mesh.devices).reshape(n_dp, n_tensor // 2, 2), ("dp", "zh", "core")
    )
    tp = ("zh", "core")
    in_specs = (
        P("dp", None),
        P("dp", None),
        P("dp", None),
        P("dp", None),
        P("dp"),
        P(),
        P("dp", tp, None),
        P("dp", tp, None),
        P("dp", tp, None),
    )
    out_specs = (
        P("dp", tp),
        P("dp", tp, None),
        P("dp", tp, None),
        P("dp", tp, None),
    )
    return jax.shard_map(body, mesh=fine, in_specs=in_specs, out_specs=out_specs, check_vma=False)
```

```python
import functools

import jax
import jax.numpy as jnp
import numpy as np
from jax import lax
from jax.experimental import pallas as pl
from jax.experimental.pallas import tpu as pltpu
from jax.sharding import Mesh
from jax.sharding import PartitionSpec as P


MESH = pl.DeviceIdType.MESH


def _exchange_kernel(n, axis, x_ref, y_ref, send_sem, recv_sem, own_sem):
    me = lax.axis_index(axis)

    def copy_to(peer):
        return pltpu.make_async_remote_copy(
            src_ref=x_ref.at[peer],
            dst_ref=y_ref.at[me],
            send_sem=send_sem.at[peer],
            recv_sem=recv_sem.at[me],
            device_id={axis: peer},
            device_id_type=MESH,
        )

    def copy_from(source):
        return pltpu.make_async_remote_copy(
            src_ref=x_ref.at[source],
            dst_ref=y_ref.at[source],
            send_sem=send_sem.at[source],
            recv_sem=recv_sem.at[source],
            device_id={axis: source},
            device_id_type=MESH,
        )

    barrier = pltpu.get_barrier_semaphore()

    def greet(i, carry):
        pl.semaphore_signal(barrier, inc=1, device_id={axis: lax.rem(me + i, n)}, device_id_type=MESH)
        return carry

    lax.fori_loop(1, n, greet, 0)
    pl.semaphore_wait(barrier, n - 1)
    own = pltpu.make_async_copy(x_ref.at[me], y_ref.at[me], own_sem)
    own.start()

    def send(i, carry):
        copy_to(lax.rem(me + i, n)).start()
        return carry

    lax.fori_loop(1, n, send, 0)

    def finish(i, carry):
        copy_to(lax.rem(me + i, n)).wait_send()
        copy_from(lax.rem(me + n - i, n)).wait_recv()
        return carry

    lax.fori_loop(1, n, finish, 0)
    own.wait()


def _exchange(x, collective_id, axis="dp"):
    n = x.shape[0]
    return pl.pallas_call(
        functools.partial(_exchange_kernel, n, axis),
        out_shape=jax.ShapeDtypeStruct(x.shape, x.dtype),
        in_specs=[pl.BlockSpec(memory_space=pl.ANY)],
        out_specs=pl.BlockSpec(memory_space=pl.ANY),
        scratch_shapes=[
            pltpu.SemaphoreType.DMA((n,)),
            pltpu.SemaphoreType.DMA((n,)),
            pltpu.SemaphoreType.DMA(()),
        ],
        compiler_params=pltpu.CompilerParams(collective_id=collective_id, has_side_effects=True),
    )(x)


def _ring4_kernel(axis, x_ref, y_ref, relay_up, relay_down, send_sem, recv_sem, own_sem):
    me = lax.axis_index(axis)
    up, down, across = lax.rem(me + 1, 4), lax.rem(me + 3, 4), lax.rem(me + 2, 4)
    rows = x_ref.shape[1] // 2

    def remote(src, dst, slot, peer):
        return pltpu.make_async_remote_copy(
            src_ref=src,
            dst_ref=dst,
            send_sem=send_sem.at[slot],
            recv_sem=recv_sem.at[slot],
            device_id={axis: peer},
            device_id_type=MESH,
        )

    barrier = pltpu.get_barrier_semaphore()
    for peer in (up, down):
        pl.semaphore_signal(barrier, inc=1, device_id={axis: peer}, device_id_type=MESH)
    pl.semaphore_wait(barrier, 2)

    own = pltpu.make_async_copy(x_ref.at[me], y_ref.at[me], own_sem)
    own.start()
    to_up = remote(x_ref.at[up], y_ref.at[me], 0, up)
    to_down = remote(x_ref.at[down], y_ref.at[me], 1, down)
    lift = remote(x_ref.at[across, pl.ds(0, rows)], relay_up, 2, up)
    drop = remote(x_ref.at[across, pl.ds(rows, rows)], relay_down, 3, down)
    for copy in (to_up, to_down, lift, drop):
        copy.start()
    lift.wait_recv()
    pass_up = remote(relay_up, y_ref.at[down, pl.ds(0, rows)], 4, up)
    pass_up.start()
    drop.wait_recv()
    pass_down = remote(relay_down, y_ref.at[up, pl.ds(rows, rows)], 5, down)
    pass_down.start()
    for copy in (to_up, to_down, lift, drop, pass_up, pass_down):
        copy.wait_send()
    to_up.wait_recv()
    to_down.wait_recv()
    pass_up.wait_recv()
    pass_down.wait_recv()
    own.wait()


def _ring4_exchange(x, collective_id, axis):
    rows = x.shape[1] // 2
    return pl.pallas_call(
        functools.partial(_ring4_kernel, axis),
        out_shape=jax.ShapeDtypeStruct(x.shape, x.dtype),
        in_specs=[pl.BlockSpec(memory_space=pl.ANY)],
        out_specs=pl.BlockSpec(memory_space=pl.ANY),
        scratch_shapes=[
            pltpu.VMEM((rows,) + x.shape[2:], x.dtype),
            pltpu.VMEM((rows,) + x.shape[2:], x.dtype),
            pltpu.SemaphoreType.DMA((6,)),
            pltpu.SemaphoreType.DMA((6,)),
            pltpu.SemaphoreType.DMA(()),
        ],
        compiler_params=pltpu.CompilerParams(collective_id=collective_id, has_side_effects=True),
    )(x)


def _both_kernel(n, a_ref, b_ref, ya_ref, yb_ref, yp_ref, a_send, a_recv, a_own, relay_up, relay_down, b_send, b_recv, b_own, p_send, p_recv):
    me = lax.axis_index("dp")
    at = lax.axis_index("zh")
    up, down, across = lax.rem(at + 1, 4), lax.rem(at + 3, 4), lax.rem(at + 2, 4)
    rows = b_ref.shape[1] // 2

    def dp_copy(src, dst, slot_send, slot_recv, peer):
        return pltpu.make_async_remote_copy(
            src_ref=src,
            dst_ref=dst,
            send_sem=a_send.at[slot_send],
            recv_sem=a_recv.at[slot_recv],
            device_id={"dp": peer},
            device_id_type=MESH,
        )

    def zh_copy(src, dst, slot, peer):
        return pltpu.make_async_remote_copy(
            src_ref=src,
            dst_ref=dst,
            send_sem=b_send.at[slot],
            recv_sem=b_recv.at[slot],
            device_id={"zh": peer},
            device_id_type=MESH,
        )

    barrier = pltpu.get_barrier_semaphore()

    def greet(i, carry):
        pl.semaphore_signal(barrier, inc=1, device_id={"dp": lax.rem(me + i, n)}, device_id_type=MESH)
        return carry

    lax.fori_loop(1, n, greet, 0)
    for peer in (up, down):
        pl.semaphore_signal(barrier, inc=1, device_id={"zh": peer}, device_id_type=MESH)
    partner = 1 - lax.axis_index("core")
    pl.semaphore_signal(barrier, inc=1, device_id={"core": partner}, device_id_type=MESH)
    pl.semaphore_wait(barrier, n + 2)

    own_a = pltpu.make_async_copy(a_ref.at[me], ya_ref.at[me], a_own)
    own_a.start()
    own_b = pltpu.make_async_copy(b_ref.at[at], yb_ref.at[at], b_own)
    own_b.start()
    to_up = zh_copy(b_ref.at[up], yb_ref.at[at], 0, up)
    to_down = zh_copy(b_ref.at[down], yb_ref.at[at], 1, down)
    lift = zh_copy(b_ref.at[across, pl.ds(0, rows)], relay_up, 2, up)
    drop = zh_copy(b_ref.at[across, pl.ds(rows, rows)], relay_down, 3, down)
    for copy in (to_up, to_down, lift, drop):
        copy.start()

    def send(i, carry):
        peer = lax.rem(me + i, n)
        dp_copy(a_ref.at[peer], ya_ref.at[me], peer, me, peer).start()
        return carry

    lax.fori_loop(1, n, send, 0)
    lift.wait_recv()
    pass_up = zh_copy(relay_up, yb_ref.at[down, pl.ds(0, rows)], 4, up)
    pass_up.start()
    drop.wait_recv()
    pass_down = zh_copy(relay_down, yb_ref.at[up, pl.ds(rows, rows)], 5, down)
    pass_down.start()

    def hand(source):
        return pltpu.make_async_remote_copy(
            src_ref=ya_ref.at[source],
            dst_ref=yp_ref.at[source],
            send_sem=p_send.at[source],
            recv_sem=p_recv.at[source],
            device_id={"core": partner},
            device_id_type=MESH,
        )

    def finish(i, carry):
        peer = lax.rem(me + i, n)
        source = lax.rem(me + n - i, n)
        dp_copy(a_ref.at[peer], ya_ref.at[me], peer, me, peer).wait_send()
        dp_copy(a_ref.at[source], ya_ref.at[source], source, source, source).wait_recv()
        hand(source).start()
        return carry

    lax.fori_loop(1, n, finish, 0)
    own_a.wait()
    hand(me).start()
    for copy in (to_up, to_down, lift, drop, pass_up, pass_down):
        copy.wait_send()
    for copy in (to_up, to_down, pass_up, pass_down):
        copy.wait_recv()
    own_b.wait()

    def handed(i, carry):
        hand(i).wait_send()
        hand(i).wait_recv()
        return carry

    lax.fori_loop(0, n, handed, 0)


def _exchange_both(a, b, collective_id):
    n = a.shape[0]
    rows = b.shape[1] // 2
    return pl.pallas_call(
        functools.partial(_both_kernel, n),
        out_shape=(
            jax.ShapeDtypeStruct(a.shape, a.dtype),
            jax.ShapeDtypeStruct(b.shape, b.dtype),
            jax.ShapeDtypeStruct(a.shape, a.dtype),
        ),
        in_specs=[pl.BlockSpec(memory_space=pl.ANY)] * 2,
        out_specs=(pl.BlockSpec(memory_space=pl.ANY),) * 3,
        scratch_shapes=[
            pltpu.SemaphoreType.DMA((n,)),
            pltpu.SemaphoreType.DMA((n,)),
            pltpu.SemaphoreType.DMA(()),
            pltpu.VMEM((rows,) + b.shape[2:], b.dtype),
            pltpu.VMEM((rows,) + b.shape[2:], b.dtype),
            pltpu.SemaphoreType.DMA((6,)),
            pltpu.SemaphoreType.DMA((6,)),
            pltpu.SemaphoreType.DMA(()),
            pltpu.SemaphoreType.DMA((n,)),
            pltpu.SemaphoreType.DMA((n,)),
        ],
        compiler_params=pltpu.CompilerParams(collective_id=collective_id, has_side_effects=True),
    )(a, b)


def _swap_pair(x):
    return lax.ppermute(x, "core", [(0, 1), (1, 0)])


def body(
    tokens,
    cotangent,
    expert_ids,
    route_weight,
    forget_mask,
    lengths,
    gate_weight,
    up_weight,
    down_weight,
):
    tok_rows = tokens.shape[0]
    features = tokens.shape[1]
    half = features // 2
    top_count = expert_ids.shape[1]
    owners = lax.axis_size("dp")
    groups = lax.axis_size("zh")
    block = features // (2 * groups)
    capacity = 5 * tok_rows * top_count // (4 * owners)
    core = lax.axis_index("core")
    is_first = core == 0

    seq_count = lengths.shape[0]
    seq_len = tok_rows * owners // seq_count
    token_index = lax.axis_index("dp") * tok_rows + jnp.arange(tok_rows, dtype=jnp.int32)
    seq_id = token_index // seq_len
    seq_pos = token_index - seq_id * seq_len
    in_seq = seq_id[:, None] == jnp.arange(seq_count, dtype=jnp.int32)[None, :]
    limits = jnp.sum(jnp.where(in_seq, lengths[None, :], 0), axis=1)
    is_valid = (seq_pos < limits).astype(jnp.int32)
    forget = is_valid * forget_mask
    retain = is_valid - forget

    shares = route_weight / jnp.sum(route_weight, axis=1, keepdims=True)
    share_flat = shares.reshape(-1)
    assigned = tok_rows * top_count
    flat_ids = expert_ids.reshape(-1)
    one_hot = (flat_ids[:, None] == jnp.arange(owners, dtype=jnp.int32)[None, :]).astype(jnp.int32)
    before = jnp.cumsum(one_hot, axis=0) - one_hot
    slot_id = jnp.sum(before * one_hot, axis=1)
    target = flat_ids * capacity + slot_id
    slots_all = owners * capacity
    hit = target[None, :] == jnp.arange(slots_all, dtype=jnp.int32)[:, None]
    hit_tok = jnp.any(hit.reshape(slots_all, tok_rows, top_count), axis=2)

    slot_share = jnp.sum(jnp.where(hit, share_flat[None, :], 0.0), axis=1)
    share_hi = lax.reduce_precision(slot_share, exponent_bits=8, mantissa_bits=7)
    rest = slot_share - share_hi
    share_mid = lax.reduce_precision(rest, exponent_bits=8, mantissa_bits=7)
    share_lo = rest - share_mid
    slot_forget = jnp.sum(jnp.where(hit_tok, forget[None, :], 0), axis=1).astype(jnp.float32)
    slot_retain = jnp.sum(jnp.where(hit_tok, retain[None, :], 0), axis=1).astype(jnp.float32)
    per_slot = jnp.stack([share_hi, share_mid, share_lo, slot_forget, slot_retain], axis=1)
    per_slot = per_slot.reshape(owners, capacity * 5)
    local_counts = jnp.stack([jnp.sum(forget), jnp.sum(retain)]).astype(jnp.float32)
    meta = jnp.concatenate(
        [
            per_slot,
            jnp.broadcast_to(local_counts[None, :], (owners, 2)),
            jnp.zeros((owners, features - capacity * 5 - 2), jnp.float32),
        ],
        axis=1,
    ).astype(jnp.bfloat16)
    my_tokens = lax.dynamic_slice_in_dim(tokens, core * half, half, axis=1)
    my_cotan = lax.dynamic_slice_in_dim(cotangent, core * half, half, axis=1)
    lanes = 128
    pick = hit_tok.astype(tokens.dtype)
    send_tok = jnp.dot(pick, my_tokens, preferred_element_type=jnp.float32).astype(tokens.dtype)
    send_cot = jnp.dot(pick, my_cotan, preferred_element_type=jnp.float32).astype(tokens.dtype)
    got = _exchange(send_tok.reshape(owners, capacity * half // lanes, lanes), 0).reshape(slots_all, half)
    other = _swap_pair(got)
    rows_in = jnp.concatenate(
        [jnp.where(is_first, got, other), jnp.where(is_first, other, got)], axis=1
    )

    contract_last = (((1,), (1,)), ((), ()))
    contract_first = (((0,), (0,)), ((), ()))
    gate_pre = lax.dot_general(
        gate_weight[0], rows_in, contract_last, preferred_element_type=jnp.float32
    )
    up_pre = lax.dot_general(
        up_weight[0], rows_in, contract_last, preferred_element_type=jnp.float32
    )
    sigmoid_gate = jax.nn.sigmoid(gate_pre)
    hidden = (gate_pre * sigmoid_gate * up_pre).astype(jnp.bfloat16)
    down_groups = down_weight[0].reshape(down_weight.shape[1], groups, 2, block)
    keep_w = jnp.where(is_first, down_groups[:, :, 0, :], down_groups[:, :, 1, :])
    give_w = jnp.where(is_first, down_groups[:, :, 1, :], down_groups[:, :, 0, :])
    keep = jnp.einsum("hr,hzb->zrb", hidden, keep_w, preferred_element_type=jnp.float32).astype(jnp.bfloat16)
    give = jnp.einsum("hr,hzb->zrb", hidden, give_w, preferred_element_type=jnp.float32).astype(jnp.bfloat16)
    pair_sum = (keep.astype(jnp.float32) + _swap_pair(give).astype(jnp.float32)).astype(jnp.bfloat16)
    send = jnp.concatenate(
        [send_cot.reshape(owners, capacity * half // lanes, lanes), meta.reshape(owners, features // lanes, lanes)],
        axis=1,
    )
    recv, by_group, recv_other = _exchange_both(send, pair_sum, 3)
    got_cot = recv[:, : capacity * half // lanes, :].reshape(slots_all, half)
    got_meta = recv[:, capacity * half // lanes :, :].reshape(owners, features).astype(jnp.float32)
    other_cot = recv_other[:, : capacity * half // lanes, :].reshape(slots_all, half)
    cot_in = jnp.concatenate(
        [jnp.where(is_first, got_cot, other_cot), jnp.where(is_first, other_cot, got_cot)], axis=1
    )
    n_forget = jnp.sum(got_meta[:, capacity * 5])
    n_retain = jnp.sum(got_meta[:, capacity * 5 + 1])
    slot_meta = got_meta[:, : capacity * 5].reshape(slots_all, 5)
    got_share = (slot_meta[:, 0] + slot_meta[:, 1]) + slot_meta[:, 2]
    coefficient = float(top_count * tok_rows) * (
        slot_meta[:, 4] / n_retain - slot_meta[:, 3] / n_forget
    )
    routed = ((coefficient * got_share)[:, None] * cot_in.astype(jnp.float32)).astype(jnp.bfloat16)
    slice_sum = jnp.sum(by_group.astype(jnp.float32), axis=0).astype(jnp.bfloat16)
    returned = lax.all_to_all(
        slice_sum.reshape(owners, capacity, block), "dp", split_axis=0, concat_axis=0, tiled=True
    )
    picked = jnp.dot(
        hit.T.astype(returned.dtype),
        returned.reshape(slots_all, block),
        preferred_element_type=jnp.float32,
    ) * share_flat[:, None]
    mixed_out = jnp.sum(picked.reshape(tok_rows, top_count, block), axis=1).astype(jnp.bfloat16)

    grad_down = jnp.dot(hidden, routed, preferred_element_type=jnp.float32)
    dhidden = lax.dot_general(
        down_weight[0], routed, contract_last, preferred_element_type=jnp.float32
    )
    dgate = (dhidden * up_pre * sigmoid_gate * (1.0 + gate_pre * (1.0 - sigmoid_gate))).astype(
        jnp.bfloat16
    )
    dup = (dhidden * gate_pre * sigmoid_gate).astype(jnp.bfloat16)
    grad_gate = jnp.dot(dgate, rows_in, preferred_element_type=jnp.float32)
    grad_up = jnp.dot(dup, rows_in, preferred_element_type=jnp.float32)
    return (
        mixed_out,
        grad_gate.astype(jnp.bfloat16)[None],
        grad_up.astype(jnp.bfloat16)[None],
        grad_down.astype(jnp.bfloat16)[None],
    )


def solution(mesh):
    n_dp = mesh.shape["dp"]
    n_tensor = mesh.shape["tensor"]
    fine = Mesh(
        np.asarray(mesh.devices).reshape(n_dp, n_tensor // 2, 2), ("dp", "zh", "core")
    )
    tp = ("zh", "core")
    in_specs = (
        P("dp", None),
        P("dp", None),
        P("dp", None),
        P("dp", None),
        P("dp"),
        P(),
        P("dp", tp, None),
        P("dp", tp, None),
        P("dp", tp, None),
    )
    out_specs = (
        P("dp", tp),
        P("dp", tp, None),
        P("dp", tp, None),
        P("dp", tp, None),
    )
    return jax.shard_map(body, mesh=fine, in_specs=in_specs, out_specs=out_specs, check_vma=False)
```

```python
import functools

import jax
import jax.numpy as jnp
import numpy as np
from jax import lax
from jax.experimental import pallas as pl
from jax.experimental.pallas import tpu as pltpu
from jax.sharding import Mesh
from jax.sharding import PartitionSpec as P


MESH = pl.DeviceIdType.MESH


def _exchange_kernel(n, axis, x_ref, y_ref, send_sem, recv_sem, own_sem):
    me = lax.axis_index(axis)

    def copy_to(peer):
        return pltpu.make_async_remote_copy(
            src_ref=x_ref.at[peer],
            dst_ref=y_ref.at[me],
            send_sem=send_sem.at[peer],
            recv_sem=recv_sem.at[me],
            device_id={axis: peer},
            device_id_type=MESH,
        )

    def copy_from(source):
        return pltpu.make_async_remote_copy(
            src_ref=x_ref.at[source],
            dst_ref=y_ref.at[source],
            send_sem=send_sem.at[source],
            recv_sem=recv_sem.at[source],
            device_id={axis: source},
            device_id_type=MESH,
        )

    barrier = pltpu.get_barrier_semaphore()

    def greet(i, carry):
        pl.semaphore_signal(barrier, inc=1, device_id={axis: lax.rem(me + i, n)}, device_id_type=MESH)
        return carry

    lax.fori_loop(1, n, greet, 0)
    pl.semaphore_wait(barrier, n - 1)
    own = pltpu.make_async_copy(x_ref.at[me], y_ref.at[me], own_sem)
    own.start()

    def send(i, carry):
        copy_to(lax.rem(me + i, n)).start()
        return carry

    lax.fori_loop(1, n, send, 0)

    def finish(i, carry):
        copy_to(lax.rem(me + i, n)).wait_send()
        copy_from(lax.rem(me + n - i, n)).wait_recv()
        return carry

    lax.fori_loop(1, n, finish, 0)
    own.wait()


def _exchange(x, collective_id, axis="dp"):
    n = x.shape[0]
    return pl.pallas_call(
        functools.partial(_exchange_kernel, n, axis),
        out_shape=jax.ShapeDtypeStruct(x.shape, x.dtype),
        in_specs=[pl.BlockSpec(memory_space=pl.ANY)],
        out_specs=pl.BlockSpec(memory_space=pl.ANY),
        scratch_shapes=[
            pltpu.SemaphoreType.DMA((n,)),
            pltpu.SemaphoreType.DMA((n,)),
            pltpu.SemaphoreType.DMA(()),
        ],
        compiler_params=pltpu.CompilerParams(collective_id=collective_id, has_side_effects=True),
    )(x)


def _ring4_kernel(axis, x_ref, y_ref, relay_up, relay_down, send_sem, recv_sem, own_sem):
    me = lax.axis_index(axis)
    up, down, across = lax.rem(me + 1, 4), lax.rem(me + 3, 4), lax.rem(me + 2, 4)
    rows = x_ref.shape[1] // 2

    def remote(src, dst, slot, peer):
        return pltpu.make_async_remote_copy(
            src_ref=src,
            dst_ref=dst,
            send_sem=send_sem.at[slot],
            recv_sem=recv_sem.at[slot],
            device_id={axis: peer},
            device_id_type=MESH,
        )

    barrier = pltpu.get_barrier_semaphore()
    for peer in (up, down):
        pl.semaphore_signal(barrier, inc=1, device_id={axis: peer}, device_id_type=MESH)
    pl.semaphore_wait(barrier, 2)

    own = pltpu.make_async_copy(x_ref.at[me], y_ref.at[me], own_sem)
    own.start()
    to_up = remote(x_ref.at[up], y_ref.at[me], 0, up)
    to_down = remote(x_ref.at[down], y_ref.at[me], 1, down)
    lift = remote(x_ref.at[across, pl.ds(0, rows)], relay_up, 2, up)
    drop = remote(x_ref.at[across, pl.ds(rows, rows)], relay_down, 3, down)
    for copy in (to_up, to_down, lift, drop):
        copy.start()
    lift.wait_recv()
    pass_up = remote(relay_up, y_ref.at[down, pl.ds(0, rows)], 4, up)
    pass_up.start()
    drop.wait_recv()
    pass_down = remote(relay_down, y_ref.at[up, pl.ds(rows, rows)], 5, down)
    pass_down.start()
    for copy in (to_up, to_down, lift, drop, pass_up, pass_down):
        copy.wait_send()
    to_up.wait_recv()
    to_down.wait_recv()
    pass_up.wait_recv()
    pass_down.wait_recv()
    own.wait()


def _ring4_exchange(x, collective_id, axis):
    rows = x.shape[1] // 2
    return pl.pallas_call(
        functools.partial(_ring4_kernel, axis),
        out_shape=jax.ShapeDtypeStruct(x.shape, x.dtype),
        in_specs=[pl.BlockSpec(memory_space=pl.ANY)],
        out_specs=pl.BlockSpec(memory_space=pl.ANY),
        scratch_shapes=[
            pltpu.VMEM((rows,) + x.shape[2:], x.dtype),
            pltpu.VMEM((rows,) + x.shape[2:], x.dtype),
            pltpu.SemaphoreType.DMA((6,)),
            pltpu.SemaphoreType.DMA((6,)),
            pltpu.SemaphoreType.DMA(()),
        ],
        compiler_params=pltpu.CompilerParams(collective_id=collective_id, has_side_effects=True),
    )(x)


def _both_kernel(n, a_ref, b_ref, ya_ref, yb_ref, yp_ref, a_send, a_recv, a_own, relay_up, relay_down, b_send, b_recv, b_own, p_sem):
    me = lax.axis_index("dp")
    at = lax.axis_index("zh")
    up, down, across = lax.rem(at + 1, 4), lax.rem(at + 3, 4), lax.rem(at + 2, 4)
    rows = b_ref.shape[1] // 2

    def dp_copy(src, dst, slot_send, slot_recv, peer):
        return pltpu.make_async_remote_copy(
            src_ref=src,
            dst_ref=dst,
            send_sem=a_send.at[slot_send],
            recv_sem=a_recv.at[slot_recv],
            device_id={"dp": peer},
            device_id_type=MESH,
        )

    def zh_copy(src, dst, slot, peer):
        return pltpu.make_async_remote_copy(
            src_ref=src,
            dst_ref=dst,
            send_sem=b_send.at[slot],
            recv_sem=b_recv.at[slot],
            device_id={"zh": peer},
            device_id_type=MESH,
        )

    barrier = pltpu.get_barrier_semaphore()

    def greet(i, carry):
        pl.semaphore_signal(barrier, inc=1, device_id={"dp": lax.rem(me + i, n)}, device_id_type=MESH)
        return carry

    lax.fori_loop(1, n, greet, 0)
    for peer in (up, down):
        pl.semaphore_signal(barrier, inc=1, device_id={"zh": peer}, device_id_type=MESH)
    partner = 1 - lax.axis_index("core")
    pl.semaphore_signal(barrier, inc=1, device_id={"core": partner}, device_id_type=MESH)
    pl.semaphore_wait(barrier, n + 2)

    own_a = pltpu.make_async_copy(a_ref.at[me], ya_ref.at[me], a_own)
    own_a.start()
    own_b = pltpu.make_async_copy(b_ref.at[at], yb_ref.at[at], b_own)
    own_b.start()
    def send(i, carry):
        peer = lax.rem(me + i, n)
        dp_copy(a_ref.at[peer], ya_ref.at[me], peer, me, peer).start()
        return carry

    lax.fori_loop(1, n, send, 0)

    to_up = zh_copy(b_ref.at[up], yb_ref.at[at], 0, up)
    to_down = zh_copy(b_ref.at[down], yb_ref.at[at], 1, down)
    lift = zh_copy(b_ref.at[across, pl.ds(0, rows)], relay_up, 2, up)
    drop = zh_copy(b_ref.at[across, pl.ds(rows, rows)], relay_down, 3, down)
    for copy in (to_up, to_down, lift, drop):
        copy.start()
    lift.wait_recv()
    pass_up = zh_copy(relay_up, yb_ref.at[down, pl.ds(0, rows)], 4, up)
    pass_up.start()
    drop.wait_recv()
    pass_down = zh_copy(relay_down, yb_ref.at[up, pl.ds(rows, rows)], 5, down)
    pass_down.start()

    def finish(i, carry):
        peer = lax.rem(me + i, n)
        source = lax.rem(me + n - i, n)
        dp_copy(a_ref.at[peer], ya_ref.at[me], peer, me, peer).wait_send()
        dp_copy(a_ref.at[source], ya_ref.at[source], source, source, source).wait_recv()
        return carry

    lax.fori_loop(1, n, finish, 0)
    own_a.wait()
    to_partner = pltpu.make_async_remote_copy(
        src_ref=ya_ref,
        dst_ref=yp_ref,
        send_sem=p_sem.at[0],
        recv_sem=p_sem.at[1],
        device_id={"core": partner},
        device_id_type=MESH,
    )
    to_partner.start()
    for copy in (to_up, to_down, lift, drop, pass_up, pass_down):
        copy.wait_send()
    for copy in (to_up, to_down, pass_up, pass_down):
        copy.wait_recv()
    own_b.wait()
    to_partner.wait()


def _exchange_both(a, b, collective_id):
    n = a.shape[0]
    rows = b.shape[1] // 2
    return pl.pallas_call(
        functools.partial(_both_kernel, n),
        out_shape=(
            jax.ShapeDtypeStruct(a.shape, a.dtype),
            jax.ShapeDtypeStruct(b.shape, b.dtype),
            jax.ShapeDtypeStruct(a.shape, a.dtype),
        ),
        in_specs=[pl.BlockSpec(memory_space=pl.ANY)] * 2,
        out_specs=(pl.BlockSpec(memory_space=pl.ANY),) * 3,
        scratch_shapes=[
            pltpu.SemaphoreType.DMA((n,)),
            pltpu.SemaphoreType.DMA((n,)),
            pltpu.SemaphoreType.DMA(()),
            pltpu.VMEM((rows,) + b.shape[2:], b.dtype),
            pltpu.VMEM((rows,) + b.shape[2:], b.dtype),
            pltpu.SemaphoreType.DMA((6,)),
            pltpu.SemaphoreType.DMA((6,)),
            pltpu.SemaphoreType.DMA(()),
            pltpu.SemaphoreType.DMA((2,)),
        ],
        compiler_params=pltpu.CompilerParams(collective_id=collective_id, has_side_effects=True),
    )(a, b)


def _swap_pair(x):
    return lax.ppermute(x, "core", [(0, 1), (1, 0)])


def body(
    tokens,
    cotangent,
    expert_ids,
    route_weight,
    forget_mask,
    lengths,
    gate_weight,
    up_weight,
    down_weight,
):
    tok_rows = tokens.shape[0]
    features = tokens.shape[1]
    half = features // 2
    top_count = expert_ids.shape[1]
    owners = lax.axis_size("dp")
    groups = lax.axis_size("zh")
    block = features // (2 * groups)
    capacity = 5 * tok_rows * top_count // (4 * owners)
    core = lax.axis_index("core")
    is_first = core == 0

    seq_count = lengths.shape[0]
    seq_len = tok_rows * owners // seq_count
    token_index = lax.axis_index("dp") * tok_rows + jnp.arange(tok_rows, dtype=jnp.int32)
    seq_id = token_index // seq_len
    seq_pos = token_index - seq_id * seq_len
    in_seq = seq_id[:, None] == jnp.arange(seq_count, dtype=jnp.int32)[None, :]
    limits = jnp.sum(jnp.where(in_seq, lengths[None, :], 0), axis=1)
    is_valid = (seq_pos < limits).astype(jnp.int32)
    forget = is_valid * forget_mask
    retain = is_valid - forget

    shares = route_weight / jnp.sum(route_weight, axis=1, keepdims=True)
    share_flat = shares.reshape(-1)
    assigned = tok_rows * top_count
    flat_ids = expert_ids.reshape(-1)
    one_hot = (flat_ids[:, None] == jnp.arange(owners, dtype=jnp.int32)[None, :]).astype(jnp.int32)
    before = jnp.cumsum(one_hot, axis=0) - one_hot
    slot_id = jnp.sum(before * one_hot, axis=1)
    target = flat_ids * capacity + slot_id
    slots_all = owners * capacity
    hit = target[None, :] == jnp.arange(slots_all, dtype=jnp.int32)[:, None]
    hit_tok = jnp.any(hit.reshape(slots_all, tok_rows, top_count), axis=2)

    slot_share = jnp.sum(jnp.where(hit, share_flat[None, :], 0.0), axis=1)
    share_hi = lax.reduce_precision(slot_share, exponent_bits=8, mantissa_bits=7)
    rest = slot_share - share_hi
    share_mid = lax.reduce_precision(rest, exponent_bits=8, mantissa_bits=7)
    share_lo = rest - share_mid
    slot_forget = jnp.sum(jnp.where(hit_tok, forget[None, :], 0), axis=1).astype(jnp.float32)
    slot_retain = jnp.sum(jnp.where(hit_tok, retain[None, :], 0), axis=1).astype(jnp.float32)
    per_slot = jnp.stack([share_hi, share_mid, share_lo, slot_forget, slot_retain], axis=1)
    per_slot = per_slot.reshape(owners, capacity * 5)
    local_counts = jnp.stack([jnp.sum(forget), jnp.sum(retain)]).astype(jnp.float32)
    meta = jnp.concatenate(
        [
            per_slot,
            jnp.broadcast_to(local_counts[None, :], (owners, 2)),
            jnp.zeros((owners, features - capacity * 5 - 2), jnp.float32),
        ],
        axis=1,
    ).astype(jnp.bfloat16)
    my_tokens = lax.dynamic_slice_in_dim(tokens, core * half, half, axis=1)
    my_cotan = lax.dynamic_slice_in_dim(cotangent, core * half, half, axis=1)
    lanes = 128
    pick = hit_tok.astype(tokens.dtype)
    send_tok = jnp.dot(pick, my_tokens, preferred_element_type=jnp.float32).astype(tokens.dtype)
    send_cot = jnp.dot(pick, my_cotan, preferred_element_type=jnp.float32).astype(tokens.dtype)
    got = _exchange(send_tok.reshape(owners, capacity * half // lanes, lanes), 0).reshape(slots_all, half)
    other = _swap_pair(got)
    rows_in = jnp.concatenate(
        [jnp.where(is_first, got, other), jnp.where(is_first, other, got)], axis=1
    )

    contract_last = (((1,), (1,)), ((), ()))
    contract_first = (((0,), (0,)), ((), ()))
    gate_pre = lax.dot_general(
        gate_weight[0], rows_in, contract_last, preferred_element_type=jnp.float32
    )
    up_pre = lax.dot_general(
        up_weight[0], rows_in, contract_last, preferred_element_type=jnp.float32
    )
    sigmoid_gate = jax.nn.sigmoid(gate_pre)
    hidden = (gate_pre * sigmoid_gate * up_pre).astype(jnp.bfloat16)
    down_groups = down_weight[0].reshape(down_weight.shape[1], groups, 2, block)
    keep_w = jnp.where(is_first, down_groups[:, :, 0, :], down_groups[:, :, 1, :])
    give_w = jnp.where(is_first, down_groups[:, :, 1, :], down_groups[:, :, 0, :])
    keep = jnp.einsum("hr,hzb->zrb", hidden, keep_w, preferred_element_type=jnp.float32).astype(jnp.bfloat16)
    give = jnp.einsum("hr,hzb->zrb", hidden, give_w, preferred_element_type=jnp.float32).astype(jnp.bfloat16)
    pair_sum = (keep.astype(jnp.float32) + _swap_pair(give).astype(jnp.float32)).astype(jnp.bfloat16)
    send = jnp.concatenate(
        [send_cot.reshape(owners, capacity * half // lanes, lanes), meta.reshape(owners, features // lanes, lanes)],
        axis=1,
    )
    recv, by_group, recv_other = _exchange_both(send, pair_sum, 3)
    got_cot = recv[:, : capacity * half // lanes, :].reshape(slots_all, half)
    got_meta = recv[:, capacity * half // lanes :, :].reshape(owners, features).astype(jnp.float32)
    other_cot = recv_other[:, : capacity * half // lanes, :].reshape(slots_all, half)
    cot_in = jnp.concatenate(
        [jnp.where(is_first, got_cot, other_cot), jnp.where(is_first, other_cot, got_cot)], axis=1
    )
    n_forget = jnp.sum(got_meta[:, capacity * 5])
    n_retain = jnp.sum(got_meta[:, capacity * 5 + 1])
    slot_meta = got_meta[:, : capacity * 5].reshape(slots_all, 5)
    got_share = (slot_meta[:, 0] + slot_meta[:, 1]) + slot_meta[:, 2]
    coefficient = float(top_count * tok_rows) * (
        slot_meta[:, 4] / n_retain - slot_meta[:, 3] / n_forget
    )
    routed = ((coefficient * got_share)[:, None] * cot_in.astype(jnp.float32)).astype(jnp.bfloat16)
    slice_sum = jnp.sum(by_group.astype(jnp.float32), axis=0).astype(jnp.bfloat16)
    returned = lax.all_to_all(
        slice_sum.reshape(owners, capacity, block), "dp", split_axis=0, concat_axis=0, tiled=True
    )
    picked = jnp.dot(
        hit.T.astype(returned.dtype),
        returned.reshape(slots_all, block),
        preferred_element_type=jnp.float32,
    ) * share_flat[:, None]
    mixed_out = jnp.sum(picked.reshape(tok_rows, top_count, block), axis=1).astype(jnp.bfloat16)

    grad_down = jnp.dot(hidden, routed, preferred_element_type=jnp.float32)
    dhidden = lax.dot_general(
        down_weight[0], routed, contract_last, preferred_element_type=jnp.float32
    )
    dgate = (dhidden * up_pre * sigmoid_gate * (1.0 + gate_pre * (1.0 - sigmoid_gate))).astype(
        jnp.bfloat16
    )
    dup = (dhidden * gate_pre * sigmoid_gate).astype(jnp.bfloat16)
    grad_gate = jnp.dot(dgate, rows_in, preferred_element_type=jnp.float32)
    grad_up = jnp.dot(dup, rows_in, preferred_element_type=jnp.float32)
    return (
        mixed_out,
        grad_gate.astype(jnp.bfloat16)[None],
        grad_up.astype(jnp.bfloat16)[None],
        grad_down.astype(jnp.bfloat16)[None],
    )


def solution(mesh):
    n_dp = mesh.shape["dp"]
    n_tensor = mesh.shape["tensor"]
    fine = Mesh(
        np.asarray(mesh.devices).reshape(n_dp, n_tensor // 2, 2), ("dp", "zh", "core")
    )
    tp = ("zh", "core")
    in_specs = (
        P("dp", None),
        P("dp", None),
        P("dp", None),
        P("dp", None),
        P("dp"),
        P(),
        P("dp", tp, None),
        P("dp", tp, None),
        P("dp", tp, None),
    )
    out_specs = (
        P("dp", tp),
        P("dp", tp, None),
        P("dp", tp, None),
        P("dp", tp, None),
    )
    return jax.shard_map(body, mesh=fine, in_specs=in_specs, out_specs=out_specs, check_vma=False)
```

```python
import functools

import jax
import jax.numpy as jnp
import numpy as np
from jax import lax
from jax.experimental import pallas as pl
from jax.experimental.pallas import tpu as pltpu
from jax.sharding import Mesh
from jax.sharding import PartitionSpec as P


MESH = pl.DeviceIdType.MESH


def _exchange_kernel(n, axis, x_ref, y_ref, send_sem, recv_sem, own_sem):
    me = lax.axis_index(axis)

    def copy_to(peer):
        return pltpu.make_async_remote_copy(
            src_ref=x_ref.at[peer],
            dst_ref=y_ref.at[me],
            send_sem=send_sem.at[peer],
            recv_sem=recv_sem.at[me],
            device_id={axis: peer},
            device_id_type=MESH,
        )

    def copy_from(source):
        return pltpu.make_async_remote_copy(
            src_ref=x_ref.at[source],
            dst_ref=y_ref.at[source],
            send_sem=send_sem.at[source],
            recv_sem=recv_sem.at[source],
            device_id={axis: source},
            device_id_type=MESH,
        )

    barrier = pltpu.get_barrier_semaphore()

    def greet(i, carry):
        pl.semaphore_signal(barrier, inc=1, device_id={axis: lax.rem(me + i, n)}, device_id_type=MESH)
        return carry

    lax.fori_loop(1, n, greet, 0)
    pl.semaphore_wait(barrier, n - 1)
    own = pltpu.make_async_copy(x_ref.at[me], y_ref.at[me], own_sem)
    own.start()

    def send(i, carry):
        copy_to(lax.rem(me + i, n)).start()
        return carry

    lax.fori_loop(1, n, send, 0)

    def finish(i, carry):
        copy_to(lax.rem(me + i, n)).wait_send()
        copy_from(lax.rem(me + n - i, n)).wait_recv()
        return carry

    lax.fori_loop(1, n, finish, 0)
    own.wait()


def _exchange(x, collective_id, axis="dp"):
    n = x.shape[0]
    return pl.pallas_call(
        functools.partial(_exchange_kernel, n, axis),
        out_shape=jax.ShapeDtypeStruct(x.shape, x.dtype),
        in_specs=[pl.BlockSpec(memory_space=pl.ANY)],
        out_specs=pl.BlockSpec(memory_space=pl.ANY),
        scratch_shapes=[
            pltpu.SemaphoreType.DMA((n,)),
            pltpu.SemaphoreType.DMA((n,)),
            pltpu.SemaphoreType.DMA(()),
        ],
        compiler_params=pltpu.CompilerParams(collective_id=collective_id, has_side_effects=True),
    )(x)


def _ring4_kernel(axis, x_ref, y_ref, relay_up, relay_down, send_sem, recv_sem, own_sem):
    me = lax.axis_index(axis)
    up, down, across = lax.rem(me + 1, 4), lax.rem(me + 3, 4), lax.rem(me + 2, 4)
    rows = x_ref.shape[1] // 2

    def remote(src, dst, slot, peer):
        return pltpu.make_async_remote_copy(
            src_ref=src,
            dst_ref=dst,
            send_sem=send_sem.at[slot],
            recv_sem=recv_sem.at[slot],
            device_id={axis: peer},
            device_id_type=MESH,
        )

    barrier = pltpu.get_barrier_semaphore()
    for peer in (up, down):
        pl.semaphore_signal(barrier, inc=1, device_id={axis: peer}, device_id_type=MESH)
    pl.semaphore_wait(barrier, 2)

    own = pltpu.make_async_copy(x_ref.at[me], y_ref.at[me], own_sem)
    own.start()
    to_up = remote(x_ref.at[up], y_ref.at[me], 0, up)
    to_down = remote(x_ref.at[down], y_ref.at[me], 1, down)
    lift = remote(x_ref.at[across, pl.ds(0, rows)], relay_up, 2, up)
    drop = remote(x_ref.at[across, pl.ds(rows, rows)], relay_down, 3, down)
    for copy in (to_up, to_down, lift, drop):
        copy.start()
    lift.wait_recv()
    pass_up = remote(relay_up, y_ref.at[down, pl.ds(0, rows)], 4, up)
    pass_up.start()
    drop.wait_recv()
    pass_down = remote(relay_down, y_ref.at[up, pl.ds(rows, rows)], 5, down)
    pass_down.start()
    for copy in (to_up, to_down, lift, drop, pass_up, pass_down):
        copy.wait_send()
    to_up.wait_recv()
    to_down.wait_recv()
    pass_up.wait_recv()
    pass_down.wait_recv()
    own.wait()


def _ring4_exchange(x, collective_id, axis):
    rows = x.shape[1] // 2
    return pl.pallas_call(
        functools.partial(_ring4_kernel, axis),
        out_shape=jax.ShapeDtypeStruct(x.shape, x.dtype),
        in_specs=[pl.BlockSpec(memory_space=pl.ANY)],
        out_specs=pl.BlockSpec(memory_space=pl.ANY),
        scratch_shapes=[
            pltpu.VMEM((rows,) + x.shape[2:], x.dtype),
            pltpu.VMEM((rows,) + x.shape[2:], x.dtype),
            pltpu.SemaphoreType.DMA((6,)),
            pltpu.SemaphoreType.DMA((6,)),
            pltpu.SemaphoreType.DMA(()),
        ],
        compiler_params=pltpu.CompilerParams(collective_id=collective_id, has_side_effects=True),
    )(x)


def _both_kernel(n, a_ref, b_ref, ya_ref, yb_ref, yp_ref, a_send, a_recv, a_own, relay_up, relay_down, b_send, b_recv, b_own, p_sem):
    me = lax.axis_index("dp")
    at = lax.axis_index("zh")
    up, down, across = lax.rem(at + 1, 4), lax.rem(at + 3, 4), lax.rem(at + 2, 4)
    rows = b_ref.shape[1] // 2

    def dp_copy(src, dst, slot_send, slot_recv, peer):
        return pltpu.make_async_remote_copy(
            src_ref=src,
            dst_ref=dst,
            send_sem=a_send.at[slot_send],
            recv_sem=a_recv.at[slot_recv],
            device_id={"dp": peer},
            device_id_type=MESH,
        )

    def zh_copy(src, dst, slot, peer):
        return pltpu.make_async_remote_copy(
            src_ref=src,
            dst_ref=dst,
            send_sem=b_send.at[slot],
            recv_sem=b_recv.at[slot],
            device_id={"zh": peer},
            device_id_type=MESH,
        )

    barrier = pltpu.get_barrier_semaphore()

    def greet(i, carry):
        pl.semaphore_signal(barrier, inc=1, device_id={"dp": lax.rem(me + i, n)}, device_id_type=MESH)
        return carry

    lax.fori_loop(1, n, greet, 0)
    for peer in (up, down):
        pl.semaphore_signal(barrier, inc=1, device_id={"zh": peer}, device_id_type=MESH)
    partner = 1 - lax.axis_index("core")
    pl.semaphore_signal(barrier, inc=1, device_id={"core": partner}, device_id_type=MESH)
    pl.semaphore_wait(barrier, n + 2)

    own_a = pltpu.make_async_copy(a_ref.at[me], ya_ref.at[me], a_own)
    own_a.start()
    own_b = pltpu.make_async_copy(b_ref.at[at], yb_ref.at[at], b_own)
    own_b.start()
    to_up = zh_copy(b_ref.at[up], yb_ref.at[at], 0, up)
    to_down = zh_copy(b_ref.at[down], yb_ref.at[at], 1, down)
    lift = zh_copy(b_ref.at[across, pl.ds(0, rows)], relay_up, 2, up)
    drop = zh_copy(b_ref.at[across, pl.ds(rows, rows)], relay_down, 3, down)
    for copy in (to_up, to_down, lift, drop):
        copy.start()

    def send(i, carry):
        peer = lax.rem(me + i, n)
        dp_copy(a_ref.at[peer], ya_ref.at[me], peer, me, peer).start()
        return carry

    lax.fori_loop(1, n, send, 0)
    lift.wait_recv()
    pass_up = zh_copy(relay_up, yb_ref.at[down, pl.ds(0, rows)], 4, up)
    pass_up.start()
    drop.wait_recv()
    pass_down = zh_copy(relay_down, yb_ref.at[up, pl.ds(rows, rows)], 5, down)
    pass_down.start()

    def finish(i, carry):
        peer = lax.rem(me + i, n)
        source = lax.rem(me + n - i, n)
        dp_copy(a_ref.at[peer], ya_ref.at[me], peer, me, peer).wait_send()
        dp_copy(a_ref.at[source], ya_ref.at[source], source, source, source).wait_recv()
        return carry

    lax.fori_loop(1, n, finish, 0)
    own_a.wait()
    body_rows = a_ref.shape[1] - 16
    to_partner = pltpu.make_async_remote_copy(
        src_ref=ya_ref.at[:, pl.ds(0, body_rows)],
        dst_ref=yp_ref.at[:, pl.ds(0, body_rows)],
        send_sem=p_sem.at[0],
        recv_sem=p_sem.at[1],
        device_id={"core": partner},
        device_id_type=MESH,
    )
    to_partner.start()
    for copy in (to_up, to_down, lift, drop, pass_up, pass_down):
        copy.wait_send()
    for copy in (to_up, to_down, pass_up, pass_down):
        copy.wait_recv()
    own_b.wait()
    to_partner.wait()


def _exchange_both(a, b, collective_id):
    n = a.shape[0]
    rows = b.shape[1] // 2
    return pl.pallas_call(
        functools.partial(_both_kernel, n),
        out_shape=(
            jax.ShapeDtypeStruct(a.shape, a.dtype),
            jax.ShapeDtypeStruct(b.shape, b.dtype),
            jax.ShapeDtypeStruct(a.shape, a.dtype),
        ),
        in_specs=[pl.BlockSpec(memory_space=pl.ANY)] * 2,
        out_specs=(pl.BlockSpec(memory_space=pl.ANY),) * 3,
        scratch_shapes=[
            pltpu.SemaphoreType.DMA((n,)),
            pltpu.SemaphoreType.DMA((n,)),
            pltpu.SemaphoreType.DMA(()),
            pltpu.VMEM((rows,) + b.shape[2:], b.dtype),
            pltpu.VMEM((rows,) + b.shape[2:], b.dtype),
            pltpu.SemaphoreType.DMA((6,)),
            pltpu.SemaphoreType.DMA((6,)),
            pltpu.SemaphoreType.DMA(()),
            pltpu.SemaphoreType.DMA((2,)),
        ],
        compiler_params=pltpu.CompilerParams(collective_id=collective_id, has_side_effects=True),
    )(a, b)


def _swap_pair(x):
    return lax.ppermute(x, "core", [(0, 1), (1, 0)])


def body(
    tokens,
    cotangent,
    expert_ids,
    route_weight,
    forget_mask,
    lengths,
    gate_weight,
    up_weight,
    down_weight,
):
    tok_rows = tokens.shape[0]
    features = tokens.shape[1]
    half = features // 2
    top_count = expert_ids.shape[1]
    owners = lax.axis_size("dp")
    groups = lax.axis_size("zh")
    block = features // (2 * groups)
    capacity = 5 * tok_rows * top_count // (4 * owners)
    core = lax.axis_index("core")
    is_first = core == 0

    seq_count = lengths.shape[0]
    seq_len = tok_rows * owners // seq_count
    token_index = lax.axis_index("dp") * tok_rows + jnp.arange(tok_rows, dtype=jnp.int32)
    seq_id = token_index // seq_len
    seq_pos = token_index - seq_id * seq_len
    in_seq = seq_id[:, None] == jnp.arange(seq_count, dtype=jnp.int32)[None, :]
    limits = jnp.sum(jnp.where(in_seq, lengths[None, :], 0), axis=1)
    is_valid = (seq_pos < limits).astype(jnp.int32)
    forget = is_valid * forget_mask
    retain = is_valid - forget

    shares = route_weight / jnp.sum(route_weight, axis=1, keepdims=True)
    share_flat = shares.reshape(-1)
    assigned = tok_rows * top_count
    flat_ids = expert_ids.reshape(-1)
    one_hot = (flat_ids[:, None] == jnp.arange(owners, dtype=jnp.int32)[None, :]).astype(jnp.int32)
    before = jnp.cumsum(one_hot, axis=0) - one_hot
    slot_id = jnp.sum(before * one_hot, axis=1)
    target = flat_ids * capacity + slot_id
    slots_all = owners * capacity
    hit = target[None, :] == jnp.arange(slots_all, dtype=jnp.int32)[:, None]
    hit_tok = jnp.any(hit.reshape(slots_all, tok_rows, top_count), axis=2)

    slot_share = jnp.sum(jnp.where(hit, share_flat[None, :], 0.0), axis=1)
    share_hi = lax.reduce_precision(slot_share, exponent_bits=8, mantissa_bits=7)
    rest = slot_share - share_hi
    share_mid = lax.reduce_precision(rest, exponent_bits=8, mantissa_bits=7)
    share_lo = rest - share_mid
    slot_forget = jnp.sum(jnp.where(hit_tok, forget[None, :], 0), axis=1).astype(jnp.float32)
    slot_retain = jnp.sum(jnp.where(hit_tok, retain[None, :], 0), axis=1).astype(jnp.float32)
    per_slot = jnp.stack([share_hi, share_mid, share_lo, slot_forget, slot_retain], axis=1)
    per_slot = per_slot.reshape(owners, capacity * 5)
    local_counts = jnp.stack([jnp.sum(forget), jnp.sum(retain)]).astype(jnp.float32)
    meta = jnp.concatenate(
        [
            per_slot,
            jnp.broadcast_to(local_counts[None, :], (owners, 2)),
            jnp.zeros((owners, features - capacity * 5 - 2), jnp.float32),
        ],
        axis=1,
    ).astype(jnp.bfloat16)
    my_tokens = lax.dynamic_slice_in_dim(tokens, core * half, half, axis=1)
    my_cotan = lax.dynamic_slice_in_dim(cotangent, core * half, half, axis=1)
    lanes = 128
    pick = hit_tok.astype(tokens.dtype)
    send_tok = jnp.dot(pick, my_tokens, preferred_element_type=jnp.float32).astype(tokens.dtype)
    send_cot = jnp.dot(pick, my_cotan, preferred_element_type=jnp.float32).astype(tokens.dtype)
    got = _exchange(send_tok.reshape(owners, capacity * half // lanes, lanes), 0).reshape(slots_all, half)
    other = _swap_pair(got)
    rows_in = jnp.concatenate(
        [jnp.where(is_first, got, other), jnp.where(is_first, other, got)], axis=1
    )

    contract_last = (((1,), (1,)), ((), ()))
    contract_first = (((0,), (0,)), ((), ()))
    gate_pre = lax.dot_general(
        gate_weight[0], rows_in, contract_last, preferred_element_type=jnp.float32
    )
    up_pre = lax.dot_general(
        up_weight[0], rows_in, contract_last, preferred_element_type=jnp.float32
    )
    sigmoid_gate = jax.nn.sigmoid(gate_pre)
    hidden = (gate_pre * sigmoid_gate * up_pre).astype(jnp.bfloat16)
    down_groups = down_weight[0].reshape(down_weight.shape[1], groups, 2, block)
    keep_w = jnp.where(is_first, down_groups[:, :, 0, :], down_groups[:, :, 1, :])
    give_w = jnp.where(is_first, down_groups[:, :, 1, :], down_groups[:, :, 0, :])
    keep = jnp.einsum("hr,hzb->zrb", hidden, keep_w, preferred_element_type=jnp.float32).astype(jnp.bfloat16)
    give = jnp.einsum("hr,hzb->zrb", hidden, give_w, preferred_element_type=jnp.float32).astype(jnp.bfloat16)
    pair_sum = (keep.astype(jnp.float32) + _swap_pair(give).astype(jnp.float32)).astype(jnp.bfloat16)
    send = jnp.concatenate(
        [send_cot.reshape(owners, capacity * half // lanes, lanes), meta.reshape(owners, features // lanes, lanes)],
        axis=1,
    )
    recv, by_group, recv_other = _exchange_both(send, pair_sum, 3)
    got_cot = recv[:, : capacity * half // lanes, :].reshape(slots_all, half)
    got_meta = recv[:, capacity * half // lanes :, :].reshape(owners, features).astype(jnp.float32)
    other_cot = recv_other[:, : capacity * half // lanes, :].reshape(slots_all, half)
    cot_in = jnp.concatenate(
        [jnp.where(is_first, got_cot, other_cot), jnp.where(is_first, other_cot, got_cot)], axis=1
    )
    n_forget = jnp.sum(got_meta[:, capacity * 5])
    n_retain = jnp.sum(got_meta[:, capacity * 5 + 1])
    slot_meta = got_meta[:, : capacity * 5].reshape(slots_all, 5)
    got_share = (slot_meta[:, 0] + slot_meta[:, 1]) + slot_meta[:, 2]
    coefficient = float(top_count * tok_rows) * (
        slot_meta[:, 4] / n_retain - slot_meta[:, 3] / n_forget
    )
    routed = ((coefficient * got_share)[:, None] * cot_in.astype(jnp.float32)).astype(jnp.bfloat16)
    slice_sum = jnp.sum(by_group.astype(jnp.float32), axis=0).astype(jnp.bfloat16)
    returned = lax.all_to_all(
        slice_sum.reshape(owners, capacity, block), "dp", split_axis=0, concat_axis=0, tiled=True
    )
    picked = jnp.dot(
        hit.T.astype(returned.dtype),
        returned.reshape(slots_all, block),
        preferred_element_type=jnp.float32,
    ) * share_flat[:, None]
    mixed_out = jnp.sum(picked.reshape(tok_rows, top_count, block), axis=1).astype(jnp.bfloat16)

    grad_down = jnp.dot(hidden, routed, preferred_element_type=jnp.float32)
    dhidden = lax.dot_general(
        down_weight[0], routed, contract_last, preferred_element_type=jnp.float32
    )
    dgate = (dhidden * up_pre * sigmoid_gate * (1.0 + gate_pre * (1.0 - sigmoid_gate))).astype(
        jnp.bfloat16
    )
    dup = (dhidden * gate_pre * sigmoid_gate).astype(jnp.bfloat16)
    grad_gate = jnp.dot(dgate, rows_in, preferred_element_type=jnp.float32)
    grad_up = jnp.dot(dup, rows_in, preferred_element_type=jnp.float32)
    return (
        mixed_out,
        grad_gate.astype(jnp.bfloat16)[None],
        grad_up.astype(jnp.bfloat16)[None],
        grad_down.astype(jnp.bfloat16)[None],
    )


def solution(mesh):
    n_dp = mesh.shape["dp"]
    n_tensor = mesh.shape["tensor"]
    fine = Mesh(
        np.asarray(mesh.devices).reshape(n_dp, n_tensor // 2, 2), ("dp", "zh", "core")
    )
    tp = ("zh", "core")
    in_specs = (
        P("dp", None),
        P("dp", None),
        P("dp", None),
        P("dp", None),
        P("dp"),
        P(),
        P("dp", tp, None),
        P("dp", tp, None),
        P("dp", tp, None),
    )
    out_specs = (
        P("dp", tp),
        P("dp", tp, None),
        P("dp", tp, None),
        P("dp", tp, None),
    )
    return jax.shard_map(body, mesh=fine, in_specs=in_specs, out_specs=out_specs, check_vma=False)
```
